32 devices in a mesh: dp: 2 (over core), fsdp: 16 (over z, y, x).
Axes of the slice: x: 2, y: 2, z: 4, core: 2. Of those that a mesh axis runs over, the one named last changes fastest.
Arguments:
- hidden_in: bfloat16 [32768, 768], P(('dp', 'fsdp')), may hold values from -6 to 6
- lengths: int32 [32, 4], P(('dp', 'fsdp')), may hold values from 0 to 1024, as said below
- out_grad: bfloat16 [32768, 768], P(('dp', 'fsdp')), may hold values from -6 to 6
- query_matrix: bfloat16 [768, 768], P('fsdp'), may hold values from -0.21875 to 0.21875
- query_offset: bfloat16 [768], P('fsdp'), may hold values from -1.75 to 1.75
- key_matrix: bfloat16 [768, 768], P('fsdp'), may hold values from -0.21875 to 0.21875
- key_offset: bfloat16 [768], P('fsdp'), may hold values from -1.75 to 1.75
- value_matrix: bfloat16 [768, 768], P('fsdp'), may hold values from -0.21875 to 0.21875
- value_offset: bfloat16 [768], P('fsdp'), may hold values from -1.25 to 1.25
- output_matrix: bfloat16 [768, 768], P('fsdp'), may hold values from -1.75 to 1.75
- output_offset: bfloat16 [768], P('fsdp'), may hold values from -1.25 to 1.25
- first_gain: bfloat16 [768], P('fsdp'), may hold values from 0.25 to 1.75
- first_offset: bfloat16 [768], P('fsdp'), may hold values from -1.25 to 1.25
- up_matrix: bfloat16 [768, 3072], P('fsdp'), may hold values from -0.21875 to 0.21875
- up_offset: bfloat16 [3072], P('fsdp'), may hold values from -1.75 to 1.75
- down_matrix: bfloat16 [3072, 768], P('fsdp'), may hold values from -0.109375 to 0.109375
- down_offset: bfloat16 [768], P('fsdp'), may hold values from -1.25 to 1.25
- second_gain: bfloat16 [768], P('fsdp'), may hold values from 0.25 to 1.75
- second_offset: bfloat16 [768], P('fsdp'), may hold values from -1.25 to 1.25
Outputs:
- hidden_out: bfloat16 [32768, 768], P(('dp', 'fsdp'))
- input_grad: bfloat16 [32768, 768], P(('dp', 'fsdp'))
- query_matrix_grad: float32 [768, 768], P('fsdp')
- query_offset_grad: float32 [768], P('fsdp')
- key_matrix_grad: float32 [768, 768], P('fsdp')
- key_offset_grad: float32 [768], P('fsdp')
- value_matrix_grad: float32 [768, 768], P('fsdp')
- value_offset_grad: float32 [768], P('fsdp')
- output_matrix_grad: float32 [768, 768], P('fsdp')
- output_offset_grad: float32 [768], P('fsdp')
- first_gain_grad: float32 [768], P('fsdp')
- first_offset_grad: float32 [768], P('fsdp')
- up_matrix_grad: float32 [768, 3072], P('fsdp')
- up_offset_grad: float32 [3072], P('fsdp')
- down_matrix_grad: float32 [3072, 768], P('fsdp')
- down_offset_grad: float32 [768], P('fsdp')
- second_gain_grad: float32 [768], P('fsdp')
- second_offset_grad: float32 [768], P('fsdp')
The draws below stay inside these ranges and needn't reach their ends.
Inputs may be any that keep to these rules, and one draw needn't show every extreme that they name: Row r holds the lengths of device r's 4 sequence slots; a row sums to at most 1024 and a zero marks an empty slot. In every draw one device holds a single sequence of 1024 tokens.
All inputs are finite; a program needn't handle non-finite values.
Results may differ from the reference program's by a relative error of at most 0.018.
Values may be sent and summed in bfloat16 or wider, within the bound.
No kernel may reach another device: no remote copies, remote signals or barrier semaphores. Data moves between devices by JAX's collectives and lax.ppermute only.
A program may use at most 256 MiB of HBM per device.

```python
import jax
import jax.numpy as jnp
from jax import lax

HEADS = 12
HEAD_DIM = 64
D = 768
FF = 3072
TOK_DEV = 1024
SEQ_DEV = 4
NDEV = 32
SLOTS = 32768


def draw_lengths(key, part):
    first, second, third, fourth = jax.random.split(key, 4)
    left = jax.random.randint(first, (NDEV,), 0, 13)
    right = jax.random.randint(second, (NDEV,), 0, 13)
    least_tokens = TOK_DEV // 3
    totals = least_tokens + left * right * (TOK_DEV - least_tokens) // 144
    chosen = jax.random.randint(third, (), 0, NDEV)
    devices = jnp.arange(NDEV)
    totals = jnp.where(devices == chosen, TOK_DEV, totals).astype(jnp.int32)
    cuts = jax.random.randint(fourth, (NDEV, SEQ_DEV - 1), 0, totals[:, None] + 1)
    cuts = jnp.sort(cuts, axis=1).astype(jnp.int32)
    zeros = jnp.zeros((NDEV, 1), jnp.int32)
    bounds = jnp.concatenate([zeros, cuts, totals[:, None]], axis=1)
    pieces = bounds[:, 1:] - bounds[:, :-1]
    single = jnp.concatenate([jnp.full((NDEV, 1), TOK_DEV, jnp.int32), jnp.zeros((NDEV, SEQ_DEV - 1), jnp.int32)], axis=1)
    return jnp.where((devices == chosen)[:, None], single, pieces).astype(jnp.int32)


def block_levels(own_key, shape, shards, smallest, high):
    def one(dim, blocks):
        heights = jax.random.uniform(jax.random.fold_in(jax.random.fold_in(own_key, 6), dim), (blocks,), jnp.float32, smallest / len(shards), high / len(shards))
        return jnp.repeat(jnp.exp(heights), shape[dim] // blocks).reshape((-1,) + (1,) * (len(shape) - dim - 1))

    level = one(*shards[0])
    for cut in shards[1:]:
        level = level * one(*cut)
    return level


def centred(stream_key, shape, scale, most, cuts=(), kind=jnp.bfloat16):
    values = scale * jax.random.normal(stream_key, shape, jnp.float32)
    if cuts:
        values = values * block_levels(stream_key, shape, cuts, -0.22, 0.18)
    return jnp.clip(values, -most, most).astype(kind)


def setup_inputs(seed: int = 0) -> dict:
    splits = jax.random.split(jax.random.key(seed), 20)
    hidden_in = centred(splits[0], (SLOTS, D), 1.0, 6.0, ((0, 32),))
    lengths = draw_lengths(jax.random.fold_in(splits[19], 71), 0)
    out_grad = centred(splits[2], (SLOTS, D), 1.0, 6.0, ((0, 32),))
    query_matrix = centred(splits[3], (D, D), D ** -0.5, 0.21875, ((0, 16),))
    query_offset = centred(splits[4], (D,), 0.3, 1.75, ((0, 16),))
    key_matrix = centred(splits[5], (D, D), D ** -0.5, 0.21875, ((0, 16),))
    key_offset = centred(splits[6], (D,), 0.3, 1.75, ((0, 16),))
    value_matrix = centred(splits[7], (D, D), D ** -0.5, 0.21875, ((0, 16),))
    value_offset = centred(splits[8], (D,), 0.2, 1.25, ((0, 16),))
    output_matrix = centred(splits[9], (D, D), (D // 64) ** -0.5, 1.75, ((0, 16),))
    output_offset = centred(splits[10], (D,), 0.2, 1.25, ((0, 16),))
    first_gain = jnp.clip(1.0 + 0.15 * jax.random.normal(splits[11], (D,), jnp.float32), 0.25, 1.75).astype(jnp.bfloat16)
    first_offset = centred(splits[12], (D,), 0.2, 1.25, ((0, 16),))
    up_matrix = centred(splits[13], (D, FF), D ** -0.5, 0.21875, ((0, 16),))
    up_offset = centred(splits[14], (FF,), 0.3, 1.75, ((0, 16),))
    down_matrix = centred(splits[15], (FF, D), FF ** -0.5, 0.109375, ((0, 16),))
    down_offset = centred(splits[16], (D,), 0.2, 1.25, ((0, 16),))
    second_gain = jnp.clip(1.0 + 0.15 * jax.random.normal(splits[17], (D,), jnp.float32), 0.25, 1.75).astype(jnp.bfloat16)
    second_offset = centred(splits[18], (D,), 0.2, 1.25, ((0, 16),))
    return {"hidden_in": hidden_in, "lengths": lengths, "out_grad": out_grad, "query_matrix": query_matrix, "query_offset": query_offset, "key_matrix": key_matrix, "key_offset": key_offset, "value_matrix": value_matrix, "value_offset": value_offset, "output_matrix": output_matrix, "output_offset": output_offset, "first_gain": first_gain, "first_offset": first_offset, "up_matrix": up_matrix, "up_offset": up_offset, "down_matrix": down_matrix, "down_offset": down_offset, "second_gain": second_gain, "second_offset": second_offset}


EPSILON = 1e-12
NEGATIVE = -1e+30
HIGHEST = lax.Precision.HIGHEST

@jax.custom_vjp
def low(v):
    return lax.optimization_barrier(v.astype(jnp.bfloat16)).astype(jnp.float32)

@jax.custom_vjp
def low_back(v):
    return v

def low_keep(v):
    return (low(v), None)

def low_pass(kept, grad):
    return (grad,)

def back_keep(v):
    return (v, None)

def back_low(kept, grad):
    return (low(grad),)
low.defvjp(low_keep, low_pass)
low_back.defvjp(back_keep, back_low)

def layout(lengths, count):
    ends = jnp.cumsum(lengths).astype(jnp.int32)
    starts = (ends - lengths).astype(jnp.int32)
    slots = jnp.arange(count, dtype=jnp.int32)
    segment = lax.optimization_barrier(jnp.sum((slots[:, None] >= ends[None, :]).astype(jnp.int32), axis=1)).astype(jnp.int32)
    owner = segment[:, None] == jnp.arange(lengths.shape[0], dtype=jnp.int32)[None, :]
    begin = lax.optimization_barrier(jnp.sum(jnp.where(owner, starts[None, :], 0), axis=1)).astype(jnp.int32)
    position = (slots - begin).astype(jnp.float32)
    valid = (segment < lengths.shape[0]).astype(jnp.float32)
    return (segment, position, valid)

def rotary(position, width, head_dim):
    column = jnp.arange(width, dtype=jnp.int32)
    pair = (column % head_dim // 2).astype(jnp.float32)
    inverse = jnp.power(10000.0, -2.0 * pair / head_dim)
    angle = position[:, None] * inverse[None, :]
    even = (column % 2 == 0)[None, :]
    return (jnp.cos(angle), jnp.sin(angle), even)

def partner(value, even):
    return jnp.where(even, -jnp.roll(value, -1, axis=1), jnp.roll(value, 1, axis=1))

def rope(value, cosines, sines, even):
    return value * cosines + partner(value, even) * sines

def layer_norm(value, gain, offset):
    center = value - lax.optimization_barrier(jnp.mean(value, axis=-1, keepdims=True))
    spread = lax.optimization_barrier(jnp.mean(center * center, axis=-1, keepdims=True))
    return center * lax.rsqrt(spread + EPSILON) * gain + offset

def layer_forward(params, rows, segment, cosines, sines, even, valid):
    query_matrix, query_offset, key_matrix, key_offset, value_matrix, value_offset, output_matrix, output_offset, first_gain, first_offset, up_matrix, up_offset, down_matrix, down_offset, second_gain, second_offset = params
    count = rows.shape[0]
    query_pre = jnp.dot(rows, query_matrix, precision=HIGHEST) + query_offset
    key_pre = jnp.dot(rows, key_matrix, precision=HIGHEST) + key_offset
    value_pre = jnp.dot(rows, value_matrix, precision=HIGHEST) + value_offset
    queries = low(rope(low_back(query_pre), cosines, sines, even)).reshape(count, HEADS, HEAD_DIM)
    keys = low(rope(low_back(key_pre), cosines, sines, even)).reshape(count, HEADS, HEAD_DIM)
    values = low(low_back(value_pre)).reshape(count, HEADS, HEAD_DIM)
    raw = jnp.einsum('qhd,khd->hqk', queries, keys, precision=HIGHEST)
    same = (segment[:, None] == segment[None, :])[None, :, :]
    scores = low_back(jnp.where(same, raw * HEAD_DIM ** (-0.5), NEGATIVE))
    probs = low(jax.nn.softmax(scores, axis=-1))
    mixed = jnp.einsum('hqk,khd->qhd', probs, values, precision=HIGHEST).reshape(count, D)
    mixed = low(low_back(mixed))
    branch = low_back(jnp.dot(mixed, output_matrix, precision=HIGHEST) + output_offset)
    normed = layer_norm(rows + branch, first_gain, first_offset)
    normed_low = low(normed)
    upward = low_back(jnp.dot(normed_low, up_matrix, precision=HIGHEST) + up_offset)
    activated = low(jax.nn.gelu(upward, approximate=False))
    second_sum = normed + low_back(jnp.dot(activated, down_matrix, precision=HIGHEST) + down_offset)
    return valid[:, None] * layer_norm(second_sum, second_gain, second_offset)

def reference(hidden_in, lengths, out_grad, query_matrix, query_offset, key_matrix, key_offset, value_matrix, value_offset, output_matrix, output_offset, first_gain, first_offset, up_matrix, up_offset, down_matrix, down_offset, second_gain, second_offset):
    params = tuple((item.astype(jnp.float32) for item in (query_matrix, query_offset, key_matrix, key_offset, value_matrix, value_offset, output_matrix, output_offset, first_gain, first_offset, up_matrix, up_offset, down_matrix, down_offset, second_gain, second_offset)))
    rows_all = hidden_in.astype(jnp.float32).reshape(NDEV, TOK_DEV, D)
    grads_all = out_grad.astype(jnp.float32).reshape(NDEV, TOK_DEV, D)

    def one_device(totals, pieces):
        rows, grads, device_lengths = pieces
        segment, position, valid = layout(device_lengths, TOK_DEV)
        cosines, sines, even = rotary(position, D, HEAD_DIM)

        def forward(params_in, rows_in):
            return layer_forward(params_in, rows_in, segment, cosines, sines, even, valid)
        result, backward = jax.vjp(forward, params, rows)
        param_grads, row_grads = backward(grads)
        totals = jax.tree.map(lambda left, right: left + right, totals, param_grads)
        return (totals, (result.astype(jnp.bfloat16), row_grads.astype(jnp.bfloat16)))
    zeros = tuple((jnp.zeros_like(item) for item in params))
    totals, (results, row_grads) = lax.scan(one_device, zeros, (rows_all, grads_all, lengths))
    return (results.reshape(SLOTS, D), row_grads.reshape(SLOTS, D), totals[0], totals[1], totals[2], totals[3], totals[4], totals[5], totals[6], totals[7], totals[8], totals[9], totals[10], totals[11], totals[12], totals[13], totals[14], totals[15])
```

```python
from functools import partial
import math

import jax
import jax.numpy as jnp
from jax import lax
from jax.experimental import pallas as pl
from jax.experimental.pallas import tpu as pltpu
from jax.sharding import PartitionSpec as P

HEAD_DIM = 64


EPSILON = 1e-12
NEGATIVE = -1e30


def sides(count):
    side = math.isqrt(count // 4)
    if count % 4 == 0 and 4 * side * side == count:
        return (4, side, side)
    return (count, 1, 1)


def hop(value, leg, step, shape):
    deep, tall, wide = shape
    count = deep * tall * wide
    pairs = []
    for core in range(2):
        for here in range(count):
            z, y, x = here // (tall * wide), here // wide % tall, here % wide
            if leg == 0:
                z = (z + step) % deep
            elif (leg == 1) == (core == 0):
                y = (y + step) % tall
            else:
                x = (x + step) % wide
            there = (z * tall + y) * wide + x
            pairs.append((core * count + there, core * count + here))
    return lax.ppermute(value, ("dp", "fsdp"), pairs)


def swapped(value):
    return lax.ppermute(value, "dp", [(0, 1), (1, 0)])


def gathered(unit, shape):
    blocks = unit[None]
    for leg, size in enumerate(shape):
        blocks = jnp.concatenate([blocks] + [hop(blocks, leg, s, shape) for s in range(1, size)], 0)
    return blocks


def scattered(blocks, shape):
    for leg in (2, 1, 0):
        size = shape[leg]
        pieces = blocks.reshape(size, -1, *blocks.shape[1:])
        total = pieces[0].astype(jnp.float32)
        for s in range(1, size):
            total = total + hop(pieces[s], leg, size - s, shape).astype(jnp.float32)
        blocks = total.astype(jnp.bfloat16)
    return blocks[0]


def order(core, shape):
    deep, tall, wide = shape
    here = lax.axis_index("fsdp")
    z, y, x = here // (tall * wide), here // wide % tall, here % wide
    slot = jnp.arange(deep * tall * wide, dtype=jnp.int32)
    first, second = slot // deep % tall, slot // (deep * tall)
    z = (z + slot % deep) % deep
    y = (y + jnp.where(core == 0, first, second)) % tall
    x = (x + jnp.where(core == 0, second, first)) % wide
    return (z * tall + y) * wide + x


def inverse(table):
    slots = jnp.arange(table.shape[0], dtype=jnp.int32)
    return jnp.sum(jnp.where(table[None, :] == slots[:, None], slots[None, :], 0), axis=1)


def copy_block(table_ref, source_ref, target_ref):
    target_ref[...] = source_ref[...]


def picked(blocks, table):
    block = (1, *blocks.shape[1:])
    return pl.pallas_call(
        copy_block,
        out_shape=jax.ShapeDtypeStruct(blocks.shape, blocks.dtype),
        grid_spec=pltpu.PrefetchScalarGridSpec(
            num_scalar_prefetch=1,
            grid=(blocks.shape[0],),
            in_specs=[pl.BlockSpec(block, lambda i, t: (t[i], 0, 0))],
            out_specs=pl.BlockSpec(block, lambda i, t: (i, 0, 0)),
        ),
    )(table, blocks)


def half_of(array, side):
    width = array.shape[1] // 2
    return lax.dynamic_slice_in_dim(array, side * width, width, 1)


def both_halves(mine, core):
    theirs = swapped(mine)
    first = jnp.where(core == 0, mine, theirs)
    second = jnp.where(core == 0, theirs, mine)
    return jnp.stack([first, second], axis=-2)


def collected(unit, shape, core, table, other_table):
    mine = gathered(unit, shape)
    theirs = swapped(mine)
    mine = picked(mine, inverse(table))
    theirs = picked(theirs, inverse(other_table))
    first = jnp.where(core == 0, mine, theirs)
    second = jnp.where(core == 0, theirs, mine)
    whole = jnp.stack([first, second], axis=-2)
    return whole.reshape(-1, *whole.shape[2:])


def distributed(grad, shape, core, table):
    mine = lax.dynamic_index_in_dim(grad, core, 1, keepdims=False)
    theirs = lax.dynamic_index_in_dim(grad, 1 - core, 1, keepdims=False)
    arrived = swapped(theirs.astype(jnp.bfloat16))
    total = (mine.astype(jnp.float32) + arrived.astype(jnp.float32)).astype(jnp.bfloat16)
    blocks = total.reshape(table.shape[0], -1, total.shape[1])
    own = scattered(picked(blocks, table), shape)
    return both_halves(own, core).astype(jnp.float32)


def layout(lengths, count):
    ends = jnp.sum(
        jnp.where(jnp.arange(lengths.shape[0])[:, None] >= jnp.arange(lengths.shape[0])[None, :], lengths[None, :], 0), axis=1
    )
    starts = ends - lengths
    slots = jnp.arange(count, dtype=jnp.int32)
    segment = jnp.sum((slots[:, None] >= ends[None, :]).astype(jnp.int32), axis=1)
    owner = segment[:, None] == jnp.arange(lengths.shape[0], dtype=jnp.int32)[None, :]
    begin = jnp.sum(jnp.where(owner, starts[None, :], 0), axis=1)
    position = (slots - begin).astype(jnp.float32)
    valid = (segment < lengths.shape[0]).astype(jnp.float32)
    return (segment, position, valid)


def rotary(position, width, head_dim):
    column = jnp.arange(width, dtype=jnp.int32)
    pair = (jnp.arange(head_dim, dtype=jnp.int32) // 2).astype(jnp.float32)
    inverse = jnp.power(10000.0, -2.0 * pair / head_dim)
    angle = position[:, None] * inverse[None, :]
    even = (column % 2 == 0)[None, :]
    cosines, sines = lax.optimization_barrier((jnp.cos(angle), jnp.sin(angle)))
    return (jnp.tile(cosines, (1, width // head_dim)), jnp.tile(sines, (1, width // head_dim)), even)


def partner(value, even):
    return jnp.where(even, -jnp.roll(value, -1, axis=1), jnp.roll(value, 1, axis=1))


def rope(value, cosines, sines, even):
    return value * cosines + partner(value, even) * sines


def rope_back(grad, cosines, sines, even):
    return grad * cosines - partner(grad * sines, even)


def layer_norm(value, gain, offset):
    center = value - jnp.mean(value, axis=-1, keepdims=True)
    spread = jnp.mean(center * center, axis=-1, keepdims=True)
    return center * lax.rsqrt(spread + EPSILON) * gain + offset


def project(rows, matrix, offset):
    return jnp.dot(rows, matrix, preferred_element_type=jnp.float32) + offset.astype(jnp.float32)


def contract_rows(left, right):
    return lax.dot_general(
        left, right, (((0,), (0,)), ((), ())), preferred_element_type=jnp.float32
    )


def times_transposed(left, matrix):
    return lax.dot_general(
        left, matrix, (((1,), (1,)), ((), ())), preferred_element_type=jnp.float32
    )


def column_sums(grad_low):
    return jnp.sum(grad_low.astype(jnp.float32), axis=0)


def block_scores(query_block, key_heads, query_segment, segment):
    block = query_block.shape[0]
    heads = key_heads.shape[1]
    query_heads = query_block.reshape(block, heads, HEAD_DIM)
    raw = jnp.einsum("qhd,khd->hqk", query_heads, key_heads, preferred_element_type=jnp.float32)
    same = (query_segment[:, None] == segment[None, :])[None, :, :]
    return (jnp.where(same, raw * HEAD_DIM ** (-0.5), NEGATIVE), query_heads)


def attend(queries, keys, values, segment):
    count, width = queries.shape
    heads = width // HEAD_DIM
    block = min(512, count)
    blocks = count // block
    key_heads = keys.reshape(count, heads, HEAD_DIM)
    value_heads = values.reshape(count, heads, HEAD_DIM)

    def one_block(pieces):
        query_block, query_segment = pieces
        scores, _ = block_scores(query_block, key_heads, query_segment, segment)
        peak = jnp.max(scores, axis=2, keepdims=True)
        expo = jnp.exp(scores - peak)
        total = jnp.sum(expo, axis=2, keepdims=True)
        probs = (expo / total).astype(jnp.bfloat16)
        mixed = jnp.einsum("hqk,khd->qhd", probs, value_heads, preferred_element_type=jnp.float32)
        return (mixed.reshape(block, width), (peak + jnp.log(total))[:, :, 0])

    mixed, logsum = lax.map(
        one_block, (queries.reshape(blocks, block, width), segment.reshape(blocks, block))
    )
    return (mixed.reshape(count, width), logsum)


def attend_back(queries, keys, values, segment, logsum, grad_mixed):
    count, width = queries.shape
    heads = width // HEAD_DIM
    block = min(512, count)
    blocks = count // block
    scale = HEAD_DIM ** (-0.5)
    key_heads = keys.reshape(count, heads, HEAD_DIM)
    value_heads = values.reshape(count, heads, HEAD_DIM)

    def one_block(carry, pieces):
        key_grad, value_grad = carry
        query_block, query_segment, block_logsum, grad_block = pieces
        scores, query_heads = block_scores(query_block, key_heads, query_segment, segment)
        probs = jnp.exp(scores - block_logsum[:, :, None])
        grad_heads = grad_block.reshape(block, heads, HEAD_DIM)
        value_grad = value_grad + jnp.einsum(
            "hqk,qhd->khd",
            probs.astype(jnp.bfloat16),
            grad_heads,
            preferred_element_type=jnp.float32,
        )
        grad_probs = jnp.einsum(
            "qhd,khd->hqk", grad_heads, value_heads, preferred_element_type=jnp.float32
        )
        inner = jnp.sum(probs * grad_probs, axis=2, keepdims=True)
        grad_scores = (probs * (grad_probs - inner)).astype(jnp.bfloat16)
        query_grad = (
            jnp.einsum("hqk,khd->qhd", grad_scores, key_heads, preferred_element_type=jnp.float32)
            * scale
        )
        key_grad = (
            key_grad
            + jnp.einsum(
                "hqk,qhd->khd", grad_scores, query_heads, preferred_element_type=jnp.float32
            )
            * scale
        )
        return ((key_grad, value_grad), query_grad.reshape(block, width))

    empty = jnp.zeros((count, heads, HEAD_DIM), jnp.float32)
    (key_grad, value_grad), query_grad = lax.scan(
        one_block,
        (empty, empty),
        (
            queries.reshape(blocks, block, width),
            segment.reshape(blocks, block),
            logsum,
            grad_mixed.reshape(blocks, block, width),
        ),
    )
    return (
        query_grad.reshape(count, width),
        key_grad.reshape(count, width),
        value_grad.reshape(count, width),
    )


def shards(
    hidden_in,
    lengths,
    out_grad,
    query_matrix,
    query_offset,
    key_matrix,
    key_offset,
    value_matrix,
    value_offset,
    output_matrix,
    output_offset,
    first_gain,
    first_offset,
    up_matrix,
    up_offset,
    down_matrix,
    down_offset,
    second_gain,
    second_offset,
):
    count, width = hidden_in.shape
    segment, position, valid = layout(lengths[0], count)
    cosines, sines, even = rotary(position, width, HEAD_DIM)
    rows_float = hidden_in.astype(jnp.float32)
    core = lax.axis_index("dp")
    shape = sides(lax.axis_size("fsdp"))
    table, other_table = order(core, shape), order(1 - core, shape)
    rows = query_matrix.shape[0]
    vectors = (
        query_offset, key_offset, value_offset, output_offset, first_gain, first_offset,
        down_offset, second_gain, second_offset,
    )
    columns = [v[:, None] for v in vectors] + [up_offset.reshape(-1, rows).T]
    small = jnp.concatenate(columns, axis=1)
    small = jnp.pad(small, ((0, 0), (0, 128 - small.shape[1])))
    attn_unit = jnp.concatenate(
        [half_of(m, core) for m in (query_matrix, key_matrix, value_matrix, output_matrix)] + [small], axis=1
    )
    half = width // 2
    attn = collected(attn_unit, shape, core, table, other_table)
    query_whole, key_whole, value_whole, output_whole = (
        attn[:, :, k * half : (k + 1) * half].reshape(width, width) for k in range(4)
    )
    small = attn[:, 0, 4 * half :]
    up_whole = collected(half_of(up_matrix, core), shape, core, table, other_table).reshape(width, -1)
    down_whole = collected(half_of(down_matrix, core), shape, core, table, other_table).reshape(-1, width)
    parts = up_offset.shape[0] // rows
    up_bias = small[:, 9 : 9 + parts].reshape(-1, rows, parts).swapaxes(1, 2).reshape(-1)
    attn_full = (
        query_whole, small[:, 0], key_whole, small[:, 1], value_whole, small[:, 2], output_whole, small[:, 3],
        small[:, 4], small[:, 5],
    )
    ffn_full = (up_whole, up_bias, down_whole, small[:, 6], small[:, 7], small[:, 8])
    attn_back, ffn_back = attn_full, ffn_full
    query_pre = project(hidden_in, attn_full[0], attn_full[1])
    key_pre = project(hidden_in, attn_full[2], attn_full[3])
    value_pre = project(hidden_in, attn_full[4], attn_full[5])
    queries = rope(query_pre, cosines, sines, even).astype(jnp.bfloat16)
    keys = rope(key_pre, cosines, sines, even).astype(jnp.bfloat16)
    values = value_pre.astype(jnp.bfloat16)
    mixed, logsum = attend(queries, keys, values, segment)
    mixed_low = mixed.astype(jnp.bfloat16)
    first_sum = rows_float + project(mixed_low, attn_full[6], attn_full[7])
    normed_one = layer_norm(
        first_sum, attn_full[8].astype(jnp.float32), attn_full[9].astype(jnp.float32)
    )
    normed_low = normed_one.astype(jnp.bfloat16)
    upward = project(normed_low, ffn_full[0], ffn_full[1])
    activated = jax.nn.gelu(upward, approximate=False).astype(jnp.bfloat16)
    second_sum = normed_one + project(activated, ffn_full[2], ffn_full[3])
    result = valid[:, None] * layer_norm(
        second_sum, ffn_full[4].astype(jnp.float32), ffn_full[5].astype(jnp.float32)
    )
    hidden_out = result.astype(jnp.bfloat16)
    grad_result = out_grad.astype(jnp.float32) * valid[:, None]
    _, norm_two_back = jax.vjp(
        layer_norm, second_sum, ffn_back[4].astype(jnp.float32), ffn_back[5].astype(jnp.float32)
    )
    grad_second, second_gain_grad, second_offset_grad = norm_two_back(grad_result)
    grad_branch_two = grad_second.astype(jnp.bfloat16)
    down_matrix_grad = contract_rows(activated, grad_branch_two)
    down_offset_grad = column_sums(grad_branch_two)
    grad_activated = times_transposed(grad_branch_two, ffn_back[2])
    _, gelu_back = jax.vjp(partial(jax.nn.gelu, approximate=False), upward)
    grad_upward = gelu_back(grad_activated)[0].astype(jnp.bfloat16)
    up_matrix_grad = contract_rows(normed_low, grad_upward)
    up_offset_grad = column_sums(grad_upward)
    grad_normed = grad_second + times_transposed(grad_upward, ffn_back[0])
    up_done = distributed(up_matrix_grad.reshape(width, 2, -1), shape, core, table)
    down_done = distributed(down_matrix_grad.reshape(-1, 2, half), shape, core, table)
    _, norm_one_back = jax.vjp(
        layer_norm, first_sum, attn_back[8].astype(jnp.float32), attn_back[9].astype(jnp.float32)
    )
    grad_first, first_gain_grad, first_offset_grad = norm_one_back(grad_normed)
    grad_branch_one = grad_first.astype(jnp.bfloat16)
    output_matrix_grad = contract_rows(mixed_low, grad_branch_one)
    output_offset_grad = column_sums(grad_branch_one)
    grad_mixed = times_transposed(grad_branch_one, attn_back[6]).astype(jnp.bfloat16)
    query_rotated, key_rotated, value_summed = attend_back(
        queries, keys, values, segment, logsum, grad_mixed
    )
    grad_queries = rope_back(query_rotated, cosines, sines, even).astype(jnp.bfloat16)
    grad_keys = rope_back(key_rotated, cosines, sines, even).astype(jnp.bfloat16)
    grad_values = value_summed.astype(jnp.bfloat16)
    query_matrix_grad = contract_rows(hidden_in, grad_queries)
    key_matrix_grad = contract_rows(hidden_in, grad_keys)
    value_matrix_grad = contract_rows(hidden_in, grad_values)
    query_offset_grad = column_sums(grad_queries)
    key_offset_grad = column_sums(grad_keys)
    value_offset_grad = column_sums(grad_values)
    input_grad = (
        grad_first
        + times_transposed(grad_queries, attn_back[0])
        + times_transposed(grad_keys, attn_back[2])
        + times_transposed(grad_values, attn_back[4])
    ).astype(jnp.bfloat16)
    sums = (
        query_offset_grad, key_offset_grad, value_offset_grad, output_offset_grad, first_gain_grad, first_offset_grad,
        down_offset_grad, second_gain_grad, second_offset_grad,
    )
    columns = [v[:, None] for v in sums]
    columns.append(up_offset_grad.reshape(-1, parts, rows).swapaxes(1, 2).reshape(width, parts))
    small_grad = jnp.concatenate(columns, axis=1)
    taken = small_grad.shape[1]
    small_grad = jnp.pad(small_grad, ((0, 0), (0, -taken % 2))).reshape(width, 2, -1)
    each = small_grad.shape[2]
    small_grad = jnp.pad(small_grad, ((0, 0), (0, 0), (0, 128 - each)))
    attn_grad = jnp.concatenate(
        [
            g.astype(jnp.bfloat16).reshape(width, 2, half)
            for g in (query_matrix_grad, key_matrix_grad, value_matrix_grad, output_matrix_grad)
        ]
        + [small_grad.astype(jnp.bfloat16)],
        axis=2,
    )
    attn_done = distributed(attn_grad, shape, core, table)
    matrices = [attn_done[:, :, k * half : (k + 1) * half].reshape(rows, width) for k in range(4)]
    small_done = attn_done[:, :, 4 * half : 4 * half + each].reshape(rows, 2 * each)
    return (
        hidden_out,
        input_grad,
        matrices[0],
        small_done[:, 0],
        matrices[1],
        small_done[:, 1],
        matrices[2],
        small_done[:, 2],
        matrices[3],
        small_done[:, 3],
        small_done[:, 4],
        small_done[:, 5],
        up_done.reshape(rows, -1),
        small_done[:, 9 : 9 + parts].T.reshape(-1),
        down_done.reshape(-1, width),
        small_done[:, 6],
        small_done[:, 7],
        small_done[:, 8],
    )


def solution(mesh):
    placed = (
        P(("dp", "fsdp"), None),
        P(("dp", "fsdp"), None),
        P(("dp", "fsdp"), None),
        P("fsdp", None),
        P("fsdp"),
        P("fsdp", None),
        P("fsdp"),
        P("fsdp", None),
        P("fsdp"),
        P("fsdp", None),
        P("fsdp"),
        P("fsdp"),
        P("fsdp"),
        P("fsdp", None),
        P("fsdp"),
        P("fsdp", None),
        P("fsdp"),
        P("fsdp"),
        P("fsdp"),
    )
    return jax.shard_map(
        shards,
        mesh=mesh,
        in_specs=placed,
        out_specs=(
            P(("dp", "fsdp"), None),
            P(("dp", "fsdp"), None),
            P("fsdp", None),
            P("fsdp"),
            P("fsdp", None),
            P("fsdp"),
            P("fsdp", None),
            P("fsdp"),
            P("fsdp", None),
            P("fsdp"),
            P("fsdp"),
            P("fsdp"),
            P("fsdp", None),
            P("fsdp"),
            P("fsdp", None),
            P("fsdp"),
            P("fsdp"),
            P("fsdp"),
        ),
        check_vma=False,
    )
```

```python
import math
from functools import partial
import jax, jax.numpy as jnp
from jax import lax
from jax.experimental import pallas as pl
from jax.experimental.pallas import tpu as pltpu
from jax.sharding import PartitionSpec as P

HEAD_DIM = 64
EPSILON = 1e-12
FAR = -1e30
LOG2E = 1.4426950408889634
BLOCK = 256
SAFE = 105.0
F32 = jnp.float32
BF16 = jnp.bfloat16
VMEM_LIMIT = 58 * 2**20


def dot(a, b):
    return jnp.dot(a, b, preferred_element_type=F32)


def dot_right(a, b):
    return lax.dot_general(a, b, (((1,), (1,)), ((), ())), preferred_element_type=F32)


def dot_rows(a, b):
    return lax.dot_general(a, b, (((0,), (0,)), ((), ())), preferred_element_type=F32)


def turned(value, cosines, sines, even_lane):
    partner = jnp.where(even_lane, -pltpu.roll(value, 127, 1), pltpu.roll(value, 1, 1))
    return value * cosines + partner * sines


def lse_lane(head):
    return (HEAD_DIM if head % 2 == 0 else 0) + 8 + 3 * head


def delta_lane(head, heads):
    return lse_lane(head) + 3 * heads


def lanes_of(rows):
    return lax.broadcasted_iota(jnp.int32, (rows, 128), 1)


def load_rows(table_ref, source_ref, target_ref, sem):
    rows = source_ref.shape[1]
    copies = [
        pltpu.make_async_copy(
            source_ref.at[i, :, pl.ds(0, target_ref.shape[1])],
            target_ref.at[pl.ds(pl.multiple_of(table_ref[i] * rows, math.gcd(rows, 256)), rows)],
            sem.at[i],
        )
        for i in range(source_ref.shape[0])
    ]
    for c in copies:
        c.start()
    return copies


def project_kernel(table_ref, x_ref, w_ref, bias_ref, cos_ref, sin_ref, extq_ref, extk_ref, q_ref, k_ref, v_ref, norm_ref, w_s, sem):
    step = pl.program_id(0)

    @pl.when(step == 0)
    def _():
        for c in load_rows(table_ref, w_ref, w_s, sem):
            c.wait()
        norm_ref[...] = jnp.zeros_like(norm_ref)

    heads = q_ref.shape[0]
    width = heads * HEAD_DIM
    lane = lanes_of(BLOCK)
    first_half = lane < HEAD_DIM
    even_lane = lax.rem(lane, 2) == 0
    y = dot(x_ref[...], w_s[...]) + bias_ref[...]
    cosines, sines = cos_ref[...], sin_ref[...]
    extq, extk = extq_ref[...].astype(F32), extk_ref[...].astype(F32)
    row = lax.broadcasted_iota(jnp.int32, (128, BLOCK), 0)
    squares = []
    for p in range(width // 128):
        at = slice(p * 128, p * 128 + 128)
        q = turned(y[:, at], cosines, sines, even_lane) * (HEAD_DIM**-0.5 * LOG2E)
        k = turned(y[:, width + p * 128 : width + p * 128 + 128], cosines, sines, even_lane)
        v = y[:, 2 * width + p * 128 : 2 * width + p * 128 + 128].T
        squares.append(((q * q).astype(BF16), (k * k).astype(BF16)))
        for h in (2 * p, 2 * p + 1):
            own = first_half if h % 2 == 0 else jnp.logical_not(first_half)
            start = lse_lane(h)
            ones = (lane >= start) & (lane < start + 3)
            q_ref[h] = jnp.where(own, q, extq).astype(BF16)
            k_ref[h] = jnp.where(own, k, jnp.where(ones, 1.0, extk)).astype(BF16)
            start = delta_lane(h, heads)
            ones = (row >= start) & (row < start + 3)
            own = row < HEAD_DIM if h % 2 == 0 else row >= HEAD_DIM
            v_ref[h] = jnp.where(own, v, jnp.where(ones, 1.0, 0.0)).astype(BF16)
    column = lax.broadcasted_iota(jnp.int32, (width, 128), 0) // HEAD_DIM
    picks = jnp.where(column == lax.broadcasted_iota(jnp.int32, (width, 128), 1), 1.0, 0.0).astype(BF16)
    sums = [dot(jnp.concatenate([a[n] for a in squares], axis=1), picks) for n in range(2)]
    most = [jnp.max(t, axis=0, keepdims=True) for t in sums]
    norm_ref[...] = jnp.maximum(norm_ref[...], jnp.concatenate(most, axis=1))


def project(x, weights, table, bias, tables):
    count, width = x.shape
    blocks, rows, _ = weights.shape
    total = bias.shape[1]
    heads = total // (3 * HEAD_DIM)
    cosines, sines, extq, extk = tables
    row = lambda a: pl.BlockSpec((BLOCK, a.shape[1]), lambda i, t: (i, 0))
    head = pl.BlockSpec((heads, BLOCK, 128), lambda i, t: (0, i, 0))
    shape = jax.ShapeDtypeStruct((heads, count, 128), BF16)
    return pl.pallas_call(
        project_kernel,
        out_shape=(shape, shape, jax.ShapeDtypeStruct((heads, 128, count), BF16), jax.ShapeDtypeStruct((8, 256), F32)),
        grid_spec=pltpu.PrefetchScalarGridSpec(
            num_scalar_prefetch=1,
            grid=(count // BLOCK,),
            in_specs=[
                row(x),
                pl.BlockSpec(memory_space=pl.ANY),
                pl.BlockSpec((1, total), lambda i, t: (0, 0)),
                row(cosines), row(sines), row(extq), row(extk),
            ],
            out_specs=[head, head, pl.BlockSpec((heads, 128, BLOCK), lambda i, t: (0, 0, i)), pl.BlockSpec((8, 256), lambda i, t: (0, 0))],
            scratch_shapes=[pltpu.VMEM((blocks * rows, total), BF16), pltpu.SemaphoreType.DMA((blocks,))],
        ),
        compiler_params=pltpu.CompilerParams(vmem_limit_bytes=VMEM_LIMIT),
        cost_estimate=pl.CostEstimate(flops=2 * count * width * total, bytes_accessed=8 * 2**20, transcendentals=0),
        name="project",
    )(table, x, weights, bias, cosines, sines, extq, extk)


def three_parts(value):
    high = value.astype(BF16).astype(F32)
    rest = value - high
    middle = rest.astype(BF16).astype(F32)
    return high, middle, rest - middle


def attend_kernel(plan_ref, q_ref, k_ref, v_ref, norm_ref, extq_ref, mixed_ref, lse_ref):
    step = pl.program_id(0)
    heads, count, _ = k_ref.shape
    blocks = count // BLOCK
    first, need = plan_ref[2 * step], plan_ref[2 * step + 1]
    safe = jnp.max(norm_ref[:, :128]) * jnp.max(norm_ref[:, 128:]) < SAFE * SAFE
    lane = lanes_of(BLOCK)
    start_lane, any_lane = lane < 0, lane < 0
    for h in range(heads):
        start_lane = start_lane | (lane == lse_lane(h))
        any_lane = any_lane | ((lane >= lse_lane(h)) & (lane < lse_lane(h) + 3))
    pad = extq_ref[:, HEAD_DIM + 4 : HEAD_DIM + 5].astype(F32) > 0.5

    def rows_of(c, plain):
        keys = pl.ds(pl.multiple_of(jnp.minimum(first, blocks - c) * BLOCK, BLOCK), c * BLOCK)
        scores = [dot_right(k_ref[h, keys, :], q_ref[h]) for h in range(heads)]
        outs = []
        packs = [jnp.zeros((24, BLOCK), F32)] * 2
        row = lax.broadcasted_iota(jnp.int32, (24, BLOCK), 0)
        for h in range(heads):
            s = scores[h]
            if not plain:
                peak = jnp.max(s, axis=0, keepdims=True)
                s = s - peak
            o = dot(v_ref[h, :, keys], jnp.exp2(s).astype(BF16))
            ones = delta_lane(h, heads)
            total = o[ones : ones + 1, :]
            outs.append((o[:HEAD_DIM] if h % 2 == 0 else o[HEAD_DIM:]) / total)
            lse = -jnp.log2(total)
            if not plain:
                lse = lse - peak
            for j, part in enumerate(three_parts(lse)):
                packs[h % 2] = jnp.where(row == 3 * h + j, part, packs[h % 2])
        mixed_ref[...] = jnp.concatenate(outs, axis=0).T.astype(BF16)
        gap = lambda n: jnp.zeros((n, BLOCK), F32)
        packed = jnp.concatenate([gap(8), packs[1], gap(40), packs[0], gap(32)], axis=0).T
        lse_ref[...] = jnp.where(pad & any_lane, jnp.where(start_lane, FAR, 0.0), packed).astype(BF16)

    @pl.when(need == 0)
    def _():
        mixed_ref[...] = jnp.zeros_like(mixed_ref)
        lse_ref[...] = jnp.where(start_lane, FAR, 0.0).astype(BF16)

    for c in range(1, blocks + 1):
        pl.when(safe & (need == c))(partial(rows_of, c, True))
    pl.when(jnp.logical_not(safe) & (need > 0))(partial(rows_of, blocks, False))


def attend(plan, q, k, v, norms, extq):
    heads, count, _ = q.shape
    whole = lambda a: pl.BlockSpec(a.shape, lambda i, p: (0,) * a.ndim)
    return pl.pallas_call(
        attend_kernel,
        out_shape=(jax.ShapeDtypeStruct((count, heads * HEAD_DIM), BF16), jax.ShapeDtypeStruct((count, 128), BF16)),
        grid_spec=pltpu.PrefetchScalarGridSpec(
            num_scalar_prefetch=1,
            grid=(count // BLOCK,),
            in_specs=[
                pl.BlockSpec((heads, BLOCK, 128), lambda i, p: (0, i, 0)), whole(k), whole(v), whole(norms),
                pl.BlockSpec((BLOCK, 128), lambda i, p: (i, 0)),
            ],
            out_specs=[pl.BlockSpec((BLOCK, heads * HEAD_DIM), lambda i, p: (i, 0)), pl.BlockSpec((BLOCK, 128), lambda i, p: (i, 0))],
        ),
        compiler_params=pltpu.CompilerParams(vmem_limit_bytes=VMEM_LIMIT),
        cost_estimate=pl.CostEstimate(flops=4 * heads * count * count * 256, bytes_accessed=6 * 2**20, transcendentals=heads * count * count),
        name="attend",
    )(plan, q, k, v, norms, extq)


def attend_back_kernel(plan_ref, q_ref, k_ref, v_ref, lse_ref, mixed_ref, grad_ref, cos_ref, sin_ref, cos_all, sin_all,
                       d_ref, dk_s, dv_s):
    step = pl.program_id(0)
    heads, count, _ = k_ref.shape
    width = heads * HEAD_DIM
    blocks = count // BLOCK
    first, need = plan_ref[2 * step], plan_ref[2 * step + 1]
    lane = lanes_of(BLOCK)
    first_half = lane < HEAD_DIM
    even_lane = lax.rem(lane, 2) == 0
    scale = HEAD_DIM**-0.5

    @pl.when(step == 0)
    def _():
        dk_s[...] = jnp.zeros_like(dk_s)
        dv_s[...] = jnp.zeros_like(dv_s)

    def rows_of(c):
        keys = pl.ds(pl.multiple_of(jnp.minimum(first, blocks - c) * BLOCK, BLOCK), c * BLOCK)
        grad = grad_ref[...].astype(F32)
        product = grad * mixed_ref[...].astype(F32)
        high = product.astype(BF16)
        low = (product - high.astype(F32)).astype(BF16)
        column = lax.broadcasted_iota(jnp.int32, (width, 128), 0) // HEAD_DIM
        slot = lax.broadcasted_iota(jnp.int32, (width, 128), 1)
        slot = slot - jnp.where(lax.rem(column, 2) == 0, delta_lane(0, heads), delta_lane(0, heads) - HEAD_DIM)
        picks = jnp.where((slot >= 3 * column) & (slot < 3 * column + 3), 1.0, 0.0).astype(BF16)
        delta = three_parts(-(dot(high, picks) + dot(low, picks)))
        inner = jnp.where(first_half, lane, lane - HEAD_DIM)
        part = lax.rem(inner + 1, 3)
        delta = jnp.where(part == 0, delta[0], jnp.where(part == 1, delta[1], delta[2]))
        extra = jnp.where(inner < 8 + 3 * heads, lse_ref[...].astype(F32), delta)
        dqs = []
        for p in range(width // 128):
            at = slice(p * 128, p * 128 + 128)
            pair = grad[:, at]
            pair_t = pair.T.astype(BF16)
            qs = [q_ref[2 * p].astype(F32), q_ref[2 * p + 1].astype(F32)]
            q_t = jnp.where(first_half, qs[0], qs[1]).T.astype(BF16)
            both = []
            for n in range(2):
                h = 2 * p + n
                own = first_half if n == 0 else jnp.logical_not(first_half)
                side = slice(n * HEAD_DIM, n * HEAD_DIM + HEAD_DIM)
                g = jnp.where(own, pair, extra).astype(BF16)
                q = jnp.where(own | (inner < 8), qs[n], extra).astype(BF16)
                k = k_ref[h, keys, :]
                probs = jnp.exp2(dot_right(q, k))
                shifted = dot(g, v_ref[h, :, keys])
                grads = (probs * shifted).astype(BF16)
                dv_s[h, :, keys] += dot(pair_t[side], probs.astype(BF16))
                dk_s[h, :, keys] += dot(q_t[side], grads)
                both.append(dot(grads, k))
            dq = jnp.where(first_half, both[0], both[1]) * scale
            d_ref[pl.ds(pl.multiple_of(step * BLOCK, BLOCK), BLOCK), at] = turned(dq, cos_ref[...], -sin_ref[...], even_lane).astype(BF16)

    @pl.when(need == 0)
    def _():
        d_ref[pl.ds(pl.multiple_of(step * BLOCK, BLOCK), BLOCK), :width] = jnp.zeros((BLOCK, width), BF16)

    for c in range(1, blocks + 1):
        pl.when(need == c)(partial(rows_of, c))

    @pl.when(step == blocks - 1)
    def _():
        for p in range(width // 128):
            for r in range(blocks):
                at = slice(r * BLOCK, r * BLOCK + BLOCK)
                dv = jnp.concatenate([dv_s[2 * p, :, at], dv_s[2 * p + 1, :, at]], axis=0).T
                dk = jnp.concatenate([dk_s[2 * p, :, at], dk_s[2 * p + 1, :, at]], axis=0).T * (1.0 / LOG2E)
                d_ref[at, 2 * width + p * 128 : 2 * width + p * 128 + 128] = dv.astype(BF16)
                d_ref[at, width + p * 128 : width + p * 128 + 128] = turned(dk, cos_all[at, :], -sin_all[at, :], even_lane).astype(BF16)


def attend_back(plan, q, k, v, lse, mixed, grad, tables):
    heads, count, _ = q.shape
    width = heads * HEAD_DIM
    cosines, sines = tables[:2]
    whole = lambda a: pl.BlockSpec(a.shape, lambda i, p: (0,) * a.ndim)
    row = lambda a: pl.BlockSpec((BLOCK, a.shape[1]), lambda i, p: (i, 0))
    shape = jax.ShapeDtypeStruct((count, 3 * width), BF16)
    return pl.pallas_call(
        attend_back_kernel,
        out_shape=shape,
        grid_spec=pltpu.PrefetchScalarGridSpec(
            num_scalar_prefetch=1,
            grid=(count // BLOCK,),
            in_specs=[
                pl.BlockSpec((heads, BLOCK, 128), lambda i, p: (0, i, 0)), whole(k), whole(v), row(lse), row(mixed), row(grad),
                row(cosines), row(sines), whole(cosines), whole(sines),
            ],
            out_specs=pl.BlockSpec((count, 3 * width), lambda i, p: (0, 0)),
            scratch_shapes=[pltpu.VMEM((heads, HEAD_DIM, count), F32)] * 2,
        ),
        compiler_params=pltpu.CompilerParams(vmem_limit_bytes=VMEM_LIMIT),
        cost_estimate=pl.CostEstimate(flops=10 * heads * count * count * 256, bytes_accessed=8 * 2**20, transcendentals=heads * count * count),
        name="attend_back",
    )(plan, q, k, v, lse, mixed, grad, cosines, sines, cosines, sines)


def described(lengths, count):
    total = lengths.shape[0]
    index = jnp.arange(total)
    ends = jnp.sum(jnp.where(index[:, None] >= index[None, :], lengths[None, :], 0), axis=1)
    starts = ends - lengths
    slots = jnp.arange(count, dtype=jnp.int32)
    segment = jnp.sum((slots[:, None] >= ends[None, :]).astype(jnp.int32), axis=1)
    owner = segment[:, None] == jnp.arange(total, dtype=jnp.int32)[None, :]
    begin = jnp.sum(jnp.where(owner, starts[None, :], 0), axis=1)
    position = (slots - begin).astype(F32)
    lane = jnp.arange(128, dtype=jnp.int32)
    inverse = jnp.power(10000.0, -2.0 * (lane % HEAD_DIM // 2).astype(F32) / HEAD_DIM)
    angle = position[:, None] * inverse[None, :]
    cosines, sines = jnp.cos(angle), jnp.sin(angle)
    code = (lane % HEAD_DIM)[None, :]
    extq = jnp.where(code == segment[:, None], 1.0, 0.0).astype(BF16)
    extk = jnp.where((code < total) & (code != segment[:, None]), FAR, 0.0).astype(BF16)
    filled = jnp.sum(lengths)
    opens = jnp.arange(count // BLOCK, dtype=jnp.int32) * BLOCK
    closes = jnp.minimum(opens + BLOCK, filled)
    low = jnp.max(jnp.where(ends[None, :] <= opens[:, None], ends[None, :], 0), axis=1)
    high = jnp.min(jnp.where(ends[None, :] >= closes[:, None], ends[None, :], filled), axis=1)
    first = low // BLOCK
    need = jnp.where(opens < filled, (high + BLOCK - 1) // BLOCK - first, 0)
    plan = jnp.stack([first, need], axis=1).reshape(-1)
    valid = (segment < total).astype(F32)
    return (cosines, sines, extq, extk), plan, valid


def normed_of(value):
    center = value - jnp.mean(value, axis=1, keepdims=True)
    scale = lax.rsqrt(jnp.mean(center * center, axis=1, keepdims=True) + EPSILON)
    return center * scale, scale


def norm_back(grad, gain, normed, scale):
    scaled = grad * gain
    return (scaled - jnp.mean(scaled, axis=1, keepdims=True) - normed * jnp.mean(scaled * normed, axis=1, keepdims=True)) * scale


def gelu_and_slope(value):
    bell = jnp.exp2(value * value * (-0.5 * LOG2E))
    t = 1.0 / (1.0 + (0.3275911 * 0.5**0.5) * jnp.abs(value))
    tail = t * (0.5 * 0.254829592 + t * (0.5 * -0.284496736 + t * (0.5 * 1.421413741 + t * (0.5 * -1.453152027 + t * (0.5 * 1.061405429)))))
    tail = tail * bell
    below = jnp.where(value < 0.0, tail, 1.0 - tail)
    return value * below, below + value * bell * (2.0 * math.pi) ** -0.5


CHUNK = 512


def place_halves(place_ref, table_ref, other_ref, mine_ref, theirs_ref, target_ref, sem):
    blocks, rows, width = mine_ref.shape
    copies = []
    for n, (order, source) in enumerate(((table_ref, mine_ref), (other_ref, theirs_ref))):
        side = place_ref[0] if n == 0 else 1 - place_ref[0]
        for i in range(blocks):
            at = pl.ds(pl.multiple_of(order[i] * rows, math.gcd(rows, 256)), rows)
            columns = pl.ds(pl.multiple_of(side * width, 128), width)
            copies.append(pltpu.make_async_copy(source.at[i], target_ref.at[at, columns], sem.at[n * blocks + i]))
    return copies


def middle_kernel(place_ref, table_ref, other_ref, x_ref, mine_ref, theirs_ref, og_ref, valid_ref,
                  wo_mine, wo_theirs, wu_mine, wu_theirs, wd_mine, wd_theirs, vec_ref, bu_ref,
                  out_ref, low_ref, act_ref, gtwo_ref, gup_ref, gone_ref, gm_mine_ref, gm_theirs_ref, sums_ref, upsum_ref,
                  wo, wu, wd, mixed_s, slope_s, gm_s, so, su, sd):
    step = pl.program_id(0)
    core = place_ref[0]
    half = mine_ref.shape[1]
    width = 2 * half
    hidden = bu_ref.shape[1]
    args = (place_ref, table_ref, other_ref)
    o_copies = place_halves(*args, wo_mine, wo_theirs, wo, so)
    u_copies = place_halves(*args, wu_mine, wu_theirs, wu, su)
    d_copies = place_halves(*args, wd_mine, wd_theirs, wd, sd)

    @pl.when(step == 0)
    def _():
        for c in o_copies + u_copies + d_copies:
            c.start()
        sums_ref[...] = jnp.zeros_like(sums_ref)
        upsum_ref[...] = jnp.zeros_like(upsum_ref)
        for c in o_copies:
            c.wait()

    vec = lambda i: vec_ref[i : i + 1, :]
    mine = pl.ds(pl.multiple_of(core * half, 128), half)
    theirs = pl.ds(pl.multiple_of((1 - core) * half, 128), half)
    mixed_s[:, mine] = mine_ref[...]
    mixed_s[:, theirs] = theirs_ref[...]
    first_sum = x_ref[...].astype(F32) + (dot(mixed_s[...], wo[...]) + vec(0))
    normal_one, scale_one = normed_of(first_sum)
    normed = normal_one * vec(1) + vec(2)
    low = normed.astype(BF16)
    low_ref[...] = low

    @pl.when(step == 0)
    def _():
        for c in u_copies + d_copies:
            c.wait()

    second_sum = normed + vec(3)
    for c in range(hidden // CHUNK):
        at = slice(c * CHUNK, c * CHUNK + CHUNK)
        upward = dot(low, wu[:, at]) + bu_ref[:, at]
        activated, slope = gelu_and_slope(upward)
        activated = activated.astype(BF16)
        act_ref[:, at] = activated
        slope_s[:, at] = slope.astype(BF16)
        second_sum = second_sum + dot(activated, wd[at, :])
    normal_two, scale_two = normed_of(second_sum)
    valid = valid_ref[:, :1]
    out_ref[...] = (valid * (normal_two * vec(4) + vec(5))).astype(BF16)
    grad = og_ref[...].astype(F32) * valid
    grad_second = norm_back(grad, vec(4), normal_two, scale_two)
    grad_two = grad_second.astype(BF16)
    gtwo_ref[...] = grad_two
    total = lambda v: jnp.sum(v, axis=0, keepdims=True)
    sums = [None] * 8
    sums[4], sums[5], sums[3] = total(grad * normal_two), total(grad), total(grad_two.astype(F32))
    grad_normed = grad_second
    for c in range(hidden // CHUNK):
        at = slice(c * CHUNK, c * CHUNK + CHUNK)
        grad_up = (dot_right(grad_two, wd[at, :]) * slope_s[:, at].astype(F32)).astype(BF16)
        gup_ref[:, at] = grad_up
        upsum_ref[:, at] += total(grad_up.astype(F32))
        grad_normed = grad_normed + dot_right(grad_up, wu[:, at])
    sums[1], sums[2] = total(grad_normed * normal_one), total(grad_normed)
    grad_first = norm_back(grad_normed, vec(1), normal_one, scale_one)
    grad_one = grad_first.astype(BF16)
    gone_ref[...] = grad_one
    sums[0] = total(grad_one.astype(F32))
    for i in range(6):
        sums_ref[i : i + 1, :] += sums[i]
    gm_s[...] = dot_right(grad_one, wo[...]).astype(BF16)
    gm_mine_ref[...] = gm_s[:, mine]
    gm_theirs_ref[...] = gm_s[:, theirs]


def middle(place, table, other, x, mine, theirs, out_grad, valid, weights, vectors, up_bias):
    count, width = x.shape
    half = width // 2
    hidden = up_bias.shape[1]
    blocks = weights[0].shape[0]
    row = lambda a: pl.BlockSpec((BLOCK, a.shape[1]), lambda i, *_: (i, 0))
    rows_of = lambda n: pl.BlockSpec((BLOCK, n), lambda i, *_: (i, 0))
    whole = lambda a: pl.BlockSpec(a.shape, lambda i, *_: (0, 0))
    anywhere = pl.BlockSpec(memory_space=pl.ANY)
    shape = lambda n: jax.ShapeDtypeStruct((count, n), BF16)
    sums, upsum = jax.ShapeDtypeStruct((8, width), F32), jax.ShapeDtypeStruct((1, hidden), F32)
    return pl.pallas_call(
        middle_kernel,
        out_shape=(shape(width), shape(width), shape(hidden), shape(width), shape(hidden), shape(width), shape(half), shape(half), sums, upsum),
        grid_spec=pltpu.PrefetchScalarGridSpec(
            num_scalar_prefetch=3,
            grid=(count // BLOCK,),
            in_specs=[row(x), row(mine), row(theirs), row(out_grad), row(valid)] + [anywhere] * 6 + [whole(vectors), whole(up_bias)],
            out_specs=[rows_of(width), rows_of(width), rows_of(hidden), rows_of(width), rows_of(hidden), rows_of(width), rows_of(half), rows_of(half), whole(sums), whole(upsum)],
            scratch_shapes=[
                pltpu.VMEM((width, width), BF16), pltpu.VMEM((width, hidden), BF16), pltpu.VMEM((hidden, width), BF16),
                pltpu.VMEM((BLOCK, width), BF16), pltpu.VMEM((BLOCK, hidden), BF16), pltpu.VMEM((BLOCK, width), BF16),
            ] + [pltpu.SemaphoreType.DMA((2 * blocks,))] * 3,
        ),
        compiler_params=pltpu.CompilerParams(vmem_limit_bytes=VMEM_LIMIT),
        cost_estimate=pl.CostEstimate(flops=2 * count * width * (2 * width + 4 * hidden), bytes_accessed=32 * 2**20, transcendentals=2 * count * hidden),
        name="middle",
    )(place, table, other, x, mine, theirs, out_grad, valid, *weights, vectors, up_bias)


def outer_kernel(split, place_ref, table_ref, other_ref, left_ref, right_ref, mine_ref, theirs_ref, total_s, sem):
    step = pl.program_id(0)
    product = dot_rows(left_ref[...], right_ref[...]).astype(BF16)
    rows, columns = product.shape
    if split:
        total_s[:, pl.ds(pl.multiple_of(step * columns, 128), columns)] = product
    else:
        total_s[pl.ds(pl.multiple_of(step * rows, 256), rows), :] = product

    @pl.when(step == pl.num_programs(0) - 1)
    def _():
        blocks, rows, width = mine_ref.shape
        copies = []
        for n, (order, target) in enumerate(((other_ref, theirs_ref), (table_ref, mine_ref))):
            side = 1 - place_ref[0] if n == 0 else place_ref[0]
            for i in range(blocks):
                at = pl.ds(pl.multiple_of(order[i] * rows, math.gcd(rows, 256)), rows)
                copies.append(pltpu.make_async_copy(total_s.at[at, pl.ds(pl.multiple_of(side * width, 128), width)], target.at[i], sem.at[n * blocks + i]))
        for c in copies:
            c.start()
        for c in copies:
            c.wait()


def outer(place, table, other, left, right, split):
    count, rows = left.shape
    columns = right.shape[1]
    blocks = table.shape[0]
    shape = jax.ShapeDtypeStruct((blocks, rows // blocks, columns // 2), BF16)
    anywhere = pl.BlockSpec(memory_space=pl.ANY)
    if split:
        steps = columns // 512 if columns % 512 == 0 else columns // 384
        specs = [pl.BlockSpec((count, rows), lambda i, *_: (0, 0)), pl.BlockSpec((count, columns // steps), lambda i, *_: (0, i))]
    else:
        steps = rows // 512
        specs = [pl.BlockSpec((count, rows // steps), lambda i, *_: (0, i)), pl.BlockSpec((count, columns), lambda i, *_: (0, 0))]
    return pl.pallas_call(
        partial(outer_kernel, split),
        out_shape=(shape, shape),
        grid_spec=pltpu.PrefetchScalarGridSpec(
            num_scalar_prefetch=3,
            grid=(steps,),
            in_specs=specs,
            out_specs=[anywhere, anywhere],
            scratch_shapes=[pltpu.VMEM((rows, columns), BF16), pltpu.SemaphoreType.DMA((2 * blocks,))],
        ),
        compiler_params=pltpu.CompilerParams(vmem_limit_bytes=VMEM_LIMIT),
        cost_estimate=pl.CostEstimate(flops=2 * count * rows * columns, bytes_accessed=2 * (count * (rows + columns) + rows * columns), transcendentals=0),
        name="outer",
    )(place, table, other, left, right)


def qkv_grad_kernel(table_ref, own_ref, other_ref, down_ref, dother_ref, small_ref, out_ref, sums_ref, total_s, sem):
    step = pl.program_id(0)
    product = (dot_rows(own_ref[...], down_ref[...]) + dot_rows(other_ref[...], dother_ref[...])).astype(BF16)
    ones = jnp.ones((8, own_ref.shape[0]), BF16)
    sums_ref[...] = dot(ones, down_ref[...]) + dot(ones, dother_ref[...])
    columns = product.shape[1]
    total_s[:, pl.ds(pl.multiple_of(step * columns, 128), columns)] = product

    @pl.when(step == pl.num_programs(0) - 1)
    def _():
        blocks, rows, width = out_ref.shape
        copies = []
        for i in range(blocks):
            at = pl.ds(pl.multiple_of(table_ref[i] * rows, math.gcd(rows, 256)), rows)
            copies.append(pltpu.make_async_copy(total_s.at[at], out_ref.at[i], sem.at[i]))
        for c in copies:
            c.start()
        for c in copies:
            c.wait()


def qkv_grad(table, own, other, grad_own, grad_other):
    count, rows = own.shape
    columns = grad_own.shape[1]
    blocks = table.shape[0]
    whole = pl.BlockSpec((count, rows), lambda i, *_: (0, 0))
    tile = pl.BlockSpec((count, 384), lambda i, *_: (0, i))

    def kernel(table_ref, a, b, c, d, out_ref, sums_ref, total_s, sem):
        qkv_grad_kernel(table_ref, a, b, c, d, None, out_ref, sums_ref, total_s, sem)

    return pl.pallas_call(
        kernel,
        out_shape=(jax.ShapeDtypeStruct((blocks, rows // blocks, columns), BF16), jax.ShapeDtypeStruct((8, columns), F32)),
        grid_spec=pltpu.PrefetchScalarGridSpec(
            num_scalar_prefetch=1,
            grid=(columns // 384,),
            in_specs=[whole, whole, tile, tile],
            out_specs=[pl.BlockSpec(memory_space=pl.ANY), pl.BlockSpec((8, 384), lambda i, *_: (0, i))],
            scratch_shapes=[pltpu.VMEM((rows, columns), BF16), pltpu.SemaphoreType.DMA((blocks,))],
        ),
        compiler_params=pltpu.CompilerParams(vmem_limit_bytes=VMEM_LIMIT),
        cost_estimate=pl.CostEstimate(flops=4 * count * rows * columns, bytes_accessed=2 * (2 * count * (rows + columns) + rows * columns), transcendentals=0),
        name="qkv_grad",
    )(table, own, other, grad_own, grad_other)


def input_kernel(added, table_ref, grad_ref, w_ref, *refs):
    out_ref, w_s, sem = refs[-3:]

    @pl.when(pl.program_id(0) == 0)
    def _():
        for c in load_rows(table_ref, w_ref, w_s, sem):
            c.wait()

    total = dot_right(grad_ref[...], w_s[...])
    for ref in refs[:added]:
        total = total + ref[...].astype(F32)
    out_ref[...] = total.astype(BF16)


def input_part(table, grad, weights, width, *added):
    count, columns = grad.shape
    blocks, rows, _ = weights.shape
    row = lambda n: pl.BlockSpec((BLOCK, n), lambda i, *_: (i, 0))
    return pl.pallas_call(
        partial(input_kernel, len(added)),
        out_shape=jax.ShapeDtypeStruct((count, width), BF16),
        grid_spec=pltpu.PrefetchScalarGridSpec(
            num_scalar_prefetch=1,
            grid=(count // BLOCK,),
            in_specs=[row(columns), pl.BlockSpec(memory_space=pl.ANY)] + [row(width)] * len(added),
            out_specs=row(width),
            scratch_shapes=[pltpu.VMEM((blocks * rows, columns), BF16), pltpu.SemaphoreType.DMA((blocks,))],
        ),
        compiler_params=pltpu.CompilerParams(vmem_limit_bytes=VMEM_LIMIT),
        cost_estimate=pl.CostEstimate(flops=2 * count * width * columns, bytes_accessed=2 * count * (columns + width * (1 + len(added))), transcendentals=0),
        name="input_part",
    )(table, grad, weights, *added)


def copy_block(table_ref, source_ref, target_ref):
    target_ref[...] = source_ref[...]


def picked(blocks, table):
    block = (1, *blocks.shape[1:])
    return pl.pallas_call(
        copy_block,
        out_shape=jax.ShapeDtypeStruct(blocks.shape, blocks.dtype),
        grid_spec=pltpu.PrefetchScalarGridSpec(
            num_scalar_prefetch=1,
            grid=(blocks.shape[0],),
            in_specs=[pl.BlockSpec(block, lambda i, t: (t[i], 0, 0))],
            out_specs=pl.BlockSpec(block, lambda i, t: (i, 0, 0)),
        ),
        name="picked",
    )(table, blocks)


def sides(count):
    side = math.isqrt(count // 4)
    if count % 4 == 0 and 4 * side * side == count:
        return (4, side, side)
    return (count, 1, 1)


def hop(value, leg, step, shape):
    deep, tall, wide = shape
    count = deep * tall * wide
    pairs = []
    for core in range(2):
        for here in range(count):
            z, y, x = here // (tall * wide), here // wide % tall, here % wide
            if leg == 0:
                z = (z + step) % deep
            elif (leg == 1) == (core == 0):
                y = (y + step) % tall
            else:
                x = (x + step) % wide
            there = (z * tall + y) * wide + x
            pairs.append((core * count + there, core * count + here))
    return lax.ppermute(value, ("dp", "fsdp"), pairs)


def swapped(value):
    return lax.ppermute(value, "dp", [(0, 1), (1, 0)])


def gathered(unit, shape):
    blocks = unit[None]
    for leg, size in enumerate(shape):
        blocks = jnp.concatenate([blocks] + [hop(blocks, leg, s, shape) for s in range(1, size)], 0)
    return blocks


def scattered(blocks, shape):
    for leg in (2, 1, 0):
        size = shape[leg]
        pieces = blocks.reshape(size, -1, *blocks.shape[1:])
        total = pieces[0].astype(F32)
        for s in range(1, size):
            total = total + hop(pieces[s], leg, size - s, shape).astype(F32)
        blocks = total.astype(BF16)
    return blocks[0]


def order(core, shape):
    deep, tall, wide = shape
    here = lax.axis_index("fsdp")
    z, y, x = here // (tall * wide), here // wide % tall, here % wide
    slot = jnp.arange(deep * tall * wide, dtype=jnp.int32)
    first, second = slot // deep % tall, slot // (deep * tall)
    z = (z + slot % deep) % deep
    y = (y + jnp.where(core == 0, first, second)) % tall
    x = (x + jnp.where(core == 0, second, first)) % wide
    return (z * tall + y) * wide + x


def inverse(table):
    slots = jnp.arange(table.shape[0], dtype=jnp.int32)
    return jnp.sum(jnp.where(table[None, :] == slots[:, None], slots[None, :], 0), axis=1)


def half_of(array, side):
    width = array.shape[1] // 2
    return lax.dynamic_slice_in_dim(array, side * width, width, 1)


def joined(mine, theirs, core):
    first = jnp.where(core == 0, mine, theirs)
    second = jnp.where(core == 0, theirs, mine)
    return first, second


def reordered(small, table):
    slots = jnp.arange(table.shape[0], dtype=jnp.int32)
    chosen = (table[:, None] == slots[None, :]).astype(F32)
    flat = small.reshape(table.shape[0], -1)
    return jnp.dot(chosen, flat, precision=lax.Precision.HIGHEST).reshape(small.shape)


def shards(
    hidden_in,
    lengths,
    out_grad,
    query_matrix,
    query_offset,
    key_matrix,
    key_offset,
    value_matrix,
    value_offset,
    output_matrix,
    output_offset,
    first_gain,
    first_offset,
    up_matrix,
    up_offset,
    down_matrix,
    down_offset,
    second_gain,
    second_offset,
):
    count, width = hidden_in.shape
    half = width // 2
    rows = query_matrix.shape[0]
    parts = up_offset.shape[0] // rows
    core = lax.axis_index("dp")
    shape = sides(lax.axis_size("fsdp"))
    positions = math.prod(shape)
    table, other_table = order(core, shape), order(1 - core, shape)
    direct = rows % 16 == 0
    place = jnp.reshape(core, (1,)).astype(jnp.int32)
    zero = jnp.zeros((1,), jnp.int32)
    own_order, their_order = (table, other_table) if direct else (zero, zero)

    def usable(blocks, places):
        return blocks if direct else picked(blocks, inverse(places)).reshape(1, -1, blocks.shape[2])

    def in_blocks(array, places):
        return array if direct else picked(array.reshape(positions, -1, array.shape[2]), places)

    other_in = swapped(hidden_in)
    other_lengths = swapped(lengths)
    tables, plan, valid = described(lengths[0], count)
    other_tables, other_plan, _ = described(other_lengths[0], count)

    vectors = (
        query_offset, key_offset, value_offset, output_offset, first_gain, first_offset,
        down_offset, second_gain, second_offset,
    )
    columns = [v[:, None] for v in vectors] + [up_offset.reshape(-1, rows).T]
    small = jnp.concatenate(columns, axis=1)
    small = jnp.pad(small, ((0, 0), (0, 128 - small.shape[1])))
    unit = jnp.concatenate([half_of(m, core) for m in (query_matrix, key_matrix, value_matrix)] + [small], axis=1)
    attn = gathered(unit, shape)
    small = reordered(attn[:, :, 3 * half :].astype(F32), inverse(table))
    attn = usable(attn, table)
    output_mine = gathered(half_of(output_matrix, core), shape)
    up_mine = gathered(half_of(up_matrix, core), shape)
    down_mine = gathered(half_of(down_matrix, core), shape)
    halves = []
    for mine in (output_mine, up_mine, down_mine):
        halves += [usable(mine, table), usable(swapped(mine), other_table)]

    whole = small.reshape(width, 128)
    up_bias = small[:, :, 9 : 9 + parts].swapaxes(1, 2).reshape(1, -1)
    bias = lax.dynamic_slice_in_dim(whole[:, :3], core * half, half, 0).T.reshape(1, -1)
    vector_rows = jnp.pad(whole[:, 3:9].T, ((0, 2), (0, 0)))

    other_q, other_k, other_v, other_norms = project(other_in, attn, own_order, bias, other_tables)
    q, k, v, norms = project(hidden_in, attn, own_order, bias, tables)
    other_mixed, other_lse = attend(other_plan, other_q, other_k, other_v, other_norms, other_tables[2])
    mixed, lse = attend(plan, q, k, v, norms, tables[2])
    mixed_theirs = swapped(other_mixed)

    (
        hidden_out, normed_low, activated, grad_two, grad_up, grad_one, grad_mine, grad_theirs, sums, up_sum,
    ) = middle(
        place, own_order, their_order, hidden_in, mixed, mixed_theirs, out_grad,
        jnp.broadcast_to(valid[:, None], (count, 128)), halves, vector_rows, up_bias,
    )
    other_grad = swapped(grad_theirs)
    places = (place, own_order, their_order)

    def reduced(pair):
        mine, theirs = in_blocks(pair[0], table), in_blocks(pair[1], other_table)
        total = (mine.astype(F32) + swapped(theirs).astype(F32)).astype(BF16)
        return scattered(total, shape)

    down_done = reduced(outer(*places, activated, grad_two, 0))
    up_done = reduced(outer(*places, normed_low, grad_up, 1))
    first_mixed, second_mixed = joined(mixed, mixed_theirs, core)
    output_pair = outer(*places, jnp.concatenate([first_mixed, second_mixed], axis=1), grad_one, 1)

    slot_sums = [sums[i].reshape(positions, rows, 1) for i in range(6)]
    slot_sums.append(up_sum.reshape(positions, parts, rows).swapaxes(1, 2))
    slot_sums = jnp.concatenate(slot_sums, axis=2)
    slot_sums = jnp.pad(slot_sums, ((0, 0), (0, 0), (0, 128 - 6 - parts)))
    output_pair = tuple(
        jnp.concatenate([in_blocks(p, t), reordered(slot_sums, t).astype(BF16)], axis=2)
        for p, t in zip(output_pair, (table, other_table))
    )
    output_total = (output_pair[0].astype(F32) + swapped(output_pair[1]).astype(F32)).astype(BF16)
    output_done = scattered(output_total, shape)

    other_d = attend_back(other_plan, other_q, other_k, other_v, other_lse, other_mixed, other_grad, other_tables)
    own_d = attend_back(plan, q, k, v, lse, mixed, grad_mine, tables)
    matrices, qkv_sums = qkv_grad(own_order, hidden_in, other_in, own_d, other_d)
    own_sums = jnp.zeros((3, width), F32)
    own_sums = lax.dynamic_update_slice_in_dim(own_sums, qkv_sums[0].reshape(3, half), core * half, 1)
    own_sums = jnp.pad(own_sums.reshape(3, positions, rows).transpose(1, 2, 0), ((0, 0), (0, 0), (0, 125)))
    matrices = jnp.concatenate([in_blocks(matrices, table), reordered(own_sums, table).astype(BF16)], axis=2)
    matrices_done = scattered(matrices, shape)
    sent_grad = input_part(own_order, other_d, attn, width)
    input_grad = input_part(own_order, own_d, attn, width, swapped(sent_grad), grad_one)

    up_first, up_second = joined(up_done, swapped(up_done), core)
    down_first, down_second = joined(down_done, swapped(down_done), core)
    output_first, output_second = joined(output_done, swapped(output_done), core)
    first, second = joined(matrices_done, swapped(matrices_done), core)
    wide = lambda a, b: jnp.concatenate([a, b], axis=1).astype(F32)
    pick = lambda n: wide(first[:, n * half : (n + 1) * half], second[:, n * half : (n + 1) * half])
    offsets = (first[:, 3 * half :].astype(F32) + second[:, 3 * half :].astype(F32))[:, :3]
    others = output_first[:, half:].astype(F32)
    return (
        hidden_out,
        input_grad,
        pick(0),
        offsets[:, 0],
        pick(1),
        offsets[:, 1],
        pick(2),
        offsets[:, 2],
        wide(output_first[:, :half], output_second[:, :half]),
        others[:, 0],
        others[:, 1],
        others[:, 2],
        wide(up_first, up_second),
        others[:, 6 : 6 + parts].T.reshape(-1),
        wide(down_first, down_second),
        others[:, 3],
        others[:, 4],
        others[:, 5],
    )


def solution(mesh):
    placed = (
        P(("dp", "fsdp"), None),
        P(("dp", "fsdp"), None),
        P(("dp", "fsdp"), None),
        P("fsdp", None),
        P("fsdp"),
        P("fsdp", None),
        P("fsdp"),
        P("fsdp", None),
        P("fsdp"),
        P("fsdp", None),
        P("fsdp"),
        P("fsdp"),
        P("fsdp"),
        P("fsdp", None),
        P("fsdp"),
        P("fsdp", None),
        P("fsdp"),
        P("fsdp"),
        P("fsdp"),
    )
    return jax.shard_map(
        shards,
        mesh=mesh,
        in_specs=placed,
        out_specs=(
            P(("dp", "fsdp"), None),
            P(("dp", "fsdp"), None),
            P("fsdp", None),
            P("fsdp"),
            P("fsdp", None),
            P("fsdp"),
            P("fsdp", None),
            P("fsdp"),
            P("fsdp", None),
            P("fsdp"),
            P("fsdp"),
            P("fsdp"),
            P("fsdp", None),
            P("fsdp"),
            P("fsdp", None),
            P("fsdp"),
            P("fsdp"),
            P("fsdp"),
        ),
        check_vma=False,
    )
```

```python
import math
from functools import partial
import jax, jax.numpy as jnp
from jax import lax
from jax.experimental import pallas as pl
from jax.experimental.pallas import tpu as pltpu
from jax.sharding import PartitionSpec as P

HEAD_DIM = 64
EPSILON = 1e-12
FAR = -1e30
LOG2E = 1.4426950408889634
BLOCK = 256
SAFE = 105.0
F32 = jnp.float32
BF16 = jnp.bfloat16
VMEM_LIMIT = 58 * 2**20


def dot(a, b):
    return jnp.dot(a, b, preferred_element_type=F32)


def dot_right(a, b):
    return lax.dot_general(a, b, (((1,), (1,)), ((), ())), preferred_element_type=F32)


def dot_rows(a, b):
    return lax.dot_general(a, b, (((0,), (0,)), ((), ())), preferred_element_type=F32)


def turned(value, cosines, sines, even_lane):
    partner = jnp.where(even_lane, -pltpu.roll(value, 127, 1), pltpu.roll(value, 1, 1))
    return value * cosines + partner * sines


def lse_lane(head):
    return (HEAD_DIM if head % 2 == 0 else 0) + 8 + 3 * head


def delta_lane(head, heads):
    return lse_lane(head) + 3 * heads


def lanes_of(rows):
    return lax.broadcasted_iota(jnp.int32, (rows, 128), 1)


def load_rows(table_ref, source_refs, target_ref, sem):
    copies = []
    for source in source_refs:
        rows = source.shape[1]
        for i in range(source.shape[0]):
            n = len(copies)
            at = pl.ds(pl.multiple_of(table_ref[n] * rows, math.gcd(rows, 256)), rows)
            copies.append(pltpu.make_async_copy(source.at[i, :, pl.ds(0, target_ref.shape[1])], target_ref.at[at], sem.at[n]))
    for c in copies:
        c.start()
    return copies


def project_kernel(table_ref, x_ref, bias_ref, cos_ref, sin_ref, extq_ref, extk_ref, *refs):
    *w_refs, q_ref, k_ref, v_ref, norm_ref, w_s, sem = refs
    step = pl.program_id(0)

    @pl.when(step == 0)
    def _():
        for c in load_rows(table_ref, w_refs, w_s, sem):
            c.wait()
        norm_ref[...] = jnp.zeros_like(norm_ref)

    heads = q_ref.shape[0]
    width = heads * HEAD_DIM
    lane = lanes_of(BLOCK)
    first_half = lane < HEAD_DIM
    even_lane = lax.rem(lane, 2) == 0
    y = dot(x_ref[...], w_s[...]) + bias_ref[...]
    cosines, sines = cos_ref[...], sin_ref[...]
    extq, extk = extq_ref[...].astype(F32), extk_ref[...].astype(F32)
    row = lax.broadcasted_iota(jnp.int32, (128, BLOCK), 0)
    squares = []
    for p in range(width // 128):
        at = slice(p * 128, p * 128 + 128)
        q = turned(y[:, at], cosines, sines, even_lane) * (HEAD_DIM**-0.5 * LOG2E)
        k = turned(y[:, width + p * 128 : width + p * 128 + 128], cosines, sines, even_lane)
        v = y[:, 2 * width + p * 128 : 2 * width + p * 128 + 128].T
        squares.append(((q * q).astype(BF16), (k * k).astype(BF16)))
        for h in (2 * p, 2 * p + 1):
            own = first_half if h % 2 == 0 else jnp.logical_not(first_half)
            start = lse_lane(h)
            ones = (lane >= start) & (lane < start + 3)
            q_ref[h] = jnp.where(own, q, extq).astype(BF16)
            k_ref[h] = jnp.where(own, k, jnp.where(ones, 1.0, extk)).astype(BF16)
            start = delta_lane(h, heads)
            ones = (row >= start) & (row < start + 3)
            own = row < HEAD_DIM if h % 2 == 0 else row >= HEAD_DIM
            v_ref[h] = jnp.where(own, v, jnp.where(ones, 1.0, 0.0)).astype(BF16)
    column = lax.broadcasted_iota(jnp.int32, (width, 128), 0) // HEAD_DIM
    picks = jnp.where(column == lax.broadcasted_iota(jnp.int32, (width, 128), 1), 1.0, 0.0).astype(BF16)
    sums = [dot(jnp.concatenate([a[n] for a in squares], axis=1), picks) for n in range(2)]
    most = [jnp.max(t, axis=0, keepdims=True) for t in sums]
    norm_ref[...] = jnp.maximum(norm_ref[...], jnp.concatenate(most, axis=1))


def project(x, weights, table, bias, tables):
    count, width = x.shape
    blocks = table.shape[0]
    total = bias.shape[1]
    heads = total // (3 * HEAD_DIM)
    cosines, sines, extq, extk = tables
    row = lambda a: pl.BlockSpec((BLOCK, a.shape[1]), lambda i, t: (i, 0))
    head = pl.BlockSpec((heads, BLOCK, 128), lambda i, t: (0, i, 0))
    shape = jax.ShapeDtypeStruct((heads, count, 128), BF16)
    return pl.pallas_call(
        project_kernel,
        out_shape=(shape, shape, jax.ShapeDtypeStruct((heads, 128, count), BF16), jax.ShapeDtypeStruct((8, 256), F32)),
        grid_spec=pltpu.PrefetchScalarGridSpec(
            num_scalar_prefetch=1,
            grid=(count // BLOCK,),
            in_specs=[
                row(x), pl.BlockSpec((1, total), lambda i, t: (0, 0)), row(cosines), row(sines), row(extq), row(extk),
            ]
            + [pl.BlockSpec(memory_space=pl.ANY)] * len(weights),
            out_specs=[head, head, pl.BlockSpec((heads, 128, BLOCK), lambda i, t: (0, 0, i)), pl.BlockSpec((8, 256), lambda i, t: (0, 0))],
            scratch_shapes=[pltpu.VMEM((width, total), BF16), pltpu.SemaphoreType.DMA((blocks,))],
        ),
        compiler_params=pltpu.CompilerParams(vmem_limit_bytes=VMEM_LIMIT),
        cost_estimate=pl.CostEstimate(flops=2 * count * width * total, bytes_accessed=8 * 2**20, transcendentals=0),
        name="project",
    )(table, x, bias, cosines, sines, extq, extk, *weights)


def three_parts(value):
    high = value.astype(BF16).astype(F32)
    rest = value - high
    middle = rest.astype(BF16).astype(F32)
    return high, middle, rest - middle


def attend_kernel(plan_ref, q_ref, k_ref, v_ref, norm_ref, extq_ref, mixed_ref, lse_ref):
    step = pl.program_id(0)
    heads, count, _ = k_ref.shape
    blocks = count // BLOCK
    first, need = plan_ref[2 * step], plan_ref[2 * step + 1]
    safe = jnp.max(norm_ref[:, :128]) * jnp.max(norm_ref[:, 128:]) < SAFE * SAFE
    lane = lanes_of(BLOCK)
    start_lane, any_lane = lane < 0, lane < 0
    for h in range(heads):
        start_lane = start_lane | (lane == lse_lane(h))
        any_lane = any_lane | ((lane >= lse_lane(h)) & (lane < lse_lane(h) + 3))
    pad = extq_ref[:, HEAD_DIM + 4 : HEAD_DIM + 5].astype(F32) > 0.5

    def rows_of(c, plain):
        keys = pl.ds(pl.multiple_of(jnp.minimum(first, blocks - c) * BLOCK, BLOCK), c * BLOCK)
        scores = [dot_right(k_ref[h, keys, :], q_ref[h]) for h in range(heads)]
        outs = []
        packs = [jnp.zeros((24, BLOCK), F32)] * 2
        row = lax.broadcasted_iota(jnp.int32, (24, BLOCK), 0)
        for h in range(heads):
            s = scores[h]
            if not plain:
                peak = jnp.max(s, axis=0, keepdims=True)
                s = s - peak
            o = dot(v_ref[h, :, keys], jnp.exp2(s).astype(BF16))
            ones = delta_lane(h, heads)
            total = o[ones : ones + 1, :]
            outs.append((o[:HEAD_DIM] if h % 2 == 0 else o[HEAD_DIM:]) / total)
            lse = -jnp.log2(total)
            if not plain:
                lse = lse - peak
            for j, part in enumerate(three_parts(lse)):
                packs[h % 2] = jnp.where(row == 3 * h + j, part, packs[h % 2])
        mixed_ref[...] = jnp.concatenate(outs, axis=0).T.astype(BF16)
        gap = lambda n: jnp.zeros((n, BLOCK), F32)
        packed = jnp.concatenate([gap(8), packs[1], gap(40), packs[0], gap(32)], axis=0).T
        lse_ref[...] = jnp.where(pad & any_lane, jnp.where(start_lane, FAR, 0.0), packed).astype(BF16)

    @pl.when(need == 0)
    def _():
        mixed_ref[...] = jnp.zeros_like(mixed_ref)
        lse_ref[...] = jnp.where(start_lane, FAR, 0.0).astype(BF16)

    for c in range(1, blocks + 1):
        pl.when(safe & (need == c))(partial(rows_of, c, True))
    pl.when(jnp.logical_not(safe) & (need > 0))(partial(rows_of, blocks, False))


def attend(plan, q, k, v, norms, extq):
    heads, count, _ = q.shape
    whole = lambda a: pl.BlockSpec(a.shape, lambda i, p: (0,) * a.ndim)
    return pl.pallas_call(
        attend_kernel,
        out_shape=(jax.ShapeDtypeStruct((count, heads * HEAD_DIM), BF16), jax.ShapeDtypeStruct((count, 128), BF16)),
        grid_spec=pltpu.PrefetchScalarGridSpec(
            num_scalar_prefetch=1,
            grid=(count // BLOCK,),
            in_specs=[
                pl.BlockSpec((heads, BLOCK, 128), lambda i, p: (0, i, 0)), whole(k), whole(v), whole(norms),
                pl.BlockSpec((BLOCK, 128), lambda i, p: (i, 0)),
            ],
            out_specs=[pl.BlockSpec((BLOCK, heads * HEAD_DIM), lambda i, p: (i, 0)), pl.BlockSpec((BLOCK, 128), lambda i, p: (i, 0))],
        ),
        compiler_params=pltpu.CompilerParams(vmem_limit_bytes=VMEM_LIMIT),
        cost_estimate=pl.CostEstimate(flops=4 * heads * count * count * 256, bytes_accessed=6 * 2**20, transcendentals=heads * count * count),
        name="attend",
    )(plan, q, k, v, norms, extq)


def attend_back_kernel(plan_ref, q_ref, k_ref, v_ref, lse_ref, mixed_ref, grad_ref, cos_ref, sin_ref, cos_all, sin_all,
                       d_ref, dk_s, dv_s):
    step = pl.program_id(0)
    heads, count, _ = k_ref.shape
    width = heads * HEAD_DIM
    blocks = count // BLOCK
    first, need = plan_ref[2 * step], plan_ref[2 * step + 1]
    lane = lanes_of(BLOCK)
    first_half = lane < HEAD_DIM
    even_lane = lax.rem(lane, 2) == 0
    scale = HEAD_DIM**-0.5

    @pl.when(step == 0)
    def _():
        dk_s[...] = jnp.zeros_like(dk_s)
        dv_s[...] = jnp.zeros_like(dv_s)

    def rows_of(c):
        keys = pl.ds(pl.multiple_of(jnp.minimum(first, blocks - c) * BLOCK, BLOCK), c * BLOCK)
        grad = grad_ref[...].astype(F32)
        product = grad * mixed_ref[...].astype(F32)
        high = product.astype(BF16)
        low = (product - high.astype(F32)).astype(BF16)
        column = lax.broadcasted_iota(jnp.int32, (width, 128), 0) // HEAD_DIM
        slot = lax.broadcasted_iota(jnp.int32, (width, 128), 1)
        slot = slot - jnp.where(lax.rem(column, 2) == 0, delta_lane(0, heads), delta_lane(0, heads) - HEAD_DIM)
        picks = jnp.where((slot >= 3 * column) & (slot < 3 * column + 3), 1.0, 0.0).astype(BF16)
        delta = three_parts(-(dot(high, picks) + dot(low, picks)))
        inner = jnp.where(first_half, lane, lane - HEAD_DIM)
        part = lax.rem(inner + 1, 3)
        delta = jnp.where(part == 0, delta[0], jnp.where(part == 1, delta[1], delta[2]))
        extra = jnp.where(inner < 8 + 3 * heads, lse_ref[...].astype(F32), delta)
        dqs = []
        for p in range(width // 128):
            at = slice(p * 128, p * 128 + 128)
            pair = grad[:, at]
            pair_t = pair.T.astype(BF16)
            qs = [q_ref[2 * p].astype(F32), q_ref[2 * p + 1].astype(F32)]
            q_t = jnp.where(first_half, qs[0], qs[1]).T.astype(BF16)
            both = []
            for n in range(2):
                h = 2 * p + n
                own = first_half if n == 0 else jnp.logical_not(first_half)
                side = slice(n * HEAD_DIM, n * HEAD_DIM + HEAD_DIM)
                g = jnp.where(own, pair, extra).astype(BF16)
                q = jnp.where(own | (inner < 8), qs[n], extra).astype(BF16)
                k = k_ref[h, keys, :]
                probs = jnp.exp2(dot_right(q, k))
                shifted = dot(g, v_ref[h, :, keys])
                grads = (probs * shifted).astype(BF16)
                dv_s[h, :, keys] += dot(pair_t[side], probs.astype(BF16))
                dk_s[h, :, keys] += dot(q_t[side], grads)
                both.append(dot(grads, k))
            dq = jnp.where(first_half, both[0], both[1]) * scale
            d_ref[pl.ds(pl.multiple_of(step * BLOCK, BLOCK), BLOCK), at] = turned(dq, cos_ref[...], -sin_ref[...], even_lane).astype(BF16)

    @pl.when(need == 0)
    def _():
        d_ref[pl.ds(pl.multiple_of(step * BLOCK, BLOCK), BLOCK), :width] = jnp.zeros((BLOCK, width), BF16)

    for c in range(1, blocks + 1):
        pl.when(need == c)(partial(rows_of, c))

    @pl.when(step == blocks - 1)
    def _():
        for p in range(width // 128):
            for r in range(blocks):
                at = slice(r * BLOCK, r * BLOCK + BLOCK)
                dv = jnp.concatenate([dv_s[2 * p, :, at], dv_s[2 * p + 1, :, at]], axis=0).T
                dk = jnp.concatenate([dk_s[2 * p, :, at], dk_s[2 * p + 1, :, at]], axis=0).T * (1.0 / LOG2E)
                d_ref[at, 2 * width + p * 128 : 2 * width + p * 128 + 128] = dv.astype(BF16)
                d_ref[at, width + p * 128 : width + p * 128 + 128] = turned(dk, cos_all[at, :], -sin_all[at, :], even_lane).astype(BF16)


def attend_back(plan, q, k, v, lse, mixed, grad, tables):
    heads, count, _ = q.shape
    width = heads * HEAD_DIM
    cosines, sines = tables[:2]
    whole = lambda a: pl.BlockSpec(a.shape, lambda i, p: (0,) * a.ndim)
    row = lambda a: pl.BlockSpec((BLOCK, a.shape[1]), lambda i, p: (i, 0))
    shape = jax.ShapeDtypeStruct((count, 3 * width), BF16)
    return pl.pallas_call(
        attend_back_kernel,
        out_shape=shape,
        grid_spec=pltpu.PrefetchScalarGridSpec(
            num_scalar_prefetch=1,
            grid=(count // BLOCK,),
            in_specs=[
                pl.BlockSpec((heads, BLOCK, 128), lambda i, p: (0, i, 0)), whole(k), whole(v), row(lse), row(mixed), row(grad),
                row(cosines), row(sines), whole(cosines), whole(sines),
            ],
            out_specs=pl.BlockSpec((count, 3 * width), lambda i, p: (0, 0)),
            scratch_shapes=[pltpu.VMEM((heads, HEAD_DIM, count), F32)] * 2,
        ),
        compiler_params=pltpu.CompilerParams(vmem_limit_bytes=VMEM_LIMIT),
        cost_estimate=pl.CostEstimate(flops=10 * heads * count * count * 256, bytes_accessed=8 * 2**20, transcendentals=heads * count * count),
        name="attend_back",
    )(plan, q, k, v, lse, mixed, grad, cosines, sines, cosines, sines)


def described(lengths, count):
    total = lengths.shape[0]
    index = jnp.arange(total)
    ends = jnp.sum(jnp.where(index[:, None] >= index[None, :], lengths[None, :], 0), axis=1)
    starts = ends - lengths
    slots = jnp.arange(count, dtype=jnp.int32)
    segment = jnp.sum((slots[:, None] >= ends[None, :]).astype(jnp.int32), axis=1)
    owner = segment[:, None] == jnp.arange(total, dtype=jnp.int32)[None, :]
    begin = jnp.sum(jnp.where(owner, starts[None, :], 0), axis=1)
    position = (slots - begin).astype(F32)
    lane = jnp.arange(128, dtype=jnp.int32)
    inverse = jnp.power(10000.0, -2.0 * (lane % HEAD_DIM // 2).astype(F32) / HEAD_DIM)
    angle = position[:, None] * inverse[None, :]
    cosines, sines = jnp.cos(angle), jnp.sin(angle)
    code = (lane % HEAD_DIM)[None, :]
    extq = jnp.where(code == segment[:, None], 1.0, 0.0).astype(BF16)
    extk = jnp.where((code < total) & (code != segment[:, None]), FAR, 0.0).astype(BF16)
    filled = jnp.sum(lengths)
    opens = jnp.arange(count // BLOCK, dtype=jnp.int32) * BLOCK
    closes = jnp.minimum(opens + BLOCK, filled)
    low = jnp.max(jnp.where(ends[None, :] <= opens[:, None], ends[None, :], 0), axis=1)
    high = jnp.min(jnp.where(ends[None, :] >= closes[:, None], ends[None, :], filled), axis=1)
    first = low // BLOCK
    need = jnp.where(opens < filled, (high + BLOCK - 1) // BLOCK - first, 0)
    plan = jnp.stack([first, need], axis=1).reshape(-1)
    valid = (segment < total).astype(F32)
    return (cosines, sines, extq, extk), plan, valid


def normed_of(value):
    center = value - jnp.mean(value, axis=1, keepdims=True)
    scale = lax.rsqrt(jnp.mean(center * center, axis=1, keepdims=True) + EPSILON)
    return center * scale, scale


def norm_back(grad, gain, normed, scale):
    scaled = grad * gain
    return (scaled - jnp.mean(scaled, axis=1, keepdims=True) - normed * jnp.mean(scaled * normed, axis=1, keepdims=True)) * scale


def gelu_and_slope(value):
    bell = jnp.exp2(value * value * (-0.5 * LOG2E))
    t = 1.0 / (1.0 + (0.3275911 * 0.5**0.5) * jnp.abs(value))
    tail = t * (0.5 * 0.254829592 + t * (0.5 * -0.284496736 + t * (0.5 * 1.421413741 + t * (0.5 * -1.453152027 + t * (0.5 * 1.061405429)))))
    tail = tail * bell
    below = jnp.where(value < 0.0, tail, 1.0 - tail)
    return value * below, below + value * bell * (2.0 * math.pi) ** -0.5


CHUNK = 1024
MIDDLE = 512


def place_halves(place_ref, orders, sources, first, rows, target_ref, sem):
    copies = []
    for n, (order, refs) in enumerate(zip(orders, sources)):
        side = place_ref[0] if n == 0 else 1 - place_ref[0]
        blocks = 0
        for ref in refs:
            width = ref.shape[2]
            for i in range(ref.shape[0]):
                at = pl.ds(pl.multiple_of(order[blocks] * rows, math.gcd(rows, 256)), rows)
                columns = pl.ds(pl.multiple_of(side * width, 128), width)
                copies.append(pltpu.make_async_copy(ref.at[i, pl.ds(first, rows)], target_ref.at[at, columns], sem.at[len(copies)]))
                blocks += 1
    return copies


def middle_kernel(counts, place_ref, table_ref, other_ref, x_ref, mine_ref, theirs_ref, og_ref, valid_ref, vec_ref, bu_ref, *refs):
    weight_refs, refs = refs[: sum(counts)], refs[sum(counts) :]
    (
        out_ref, low_ref, act_ref, gtwo_ref, gup_ref, gone_ref, gm_mine_ref, gm_theirs_ref, mixed_ref, sums_ref, upsum_ref,
        wo, wu, wd, mixed_s, slope_s, gm_s, so, su, sd,
    ) = refs
    step = pl.program_id(0)
    sequences = 4
    core = place_ref[0]
    half = mine_ref.shape[1]
    width = 2 * half
    hidden = bu_ref.shape[1]
    lists = [weight_refs[sum(counts[:n]) : sum(counts[: n + 1])] for n in range(4)]
    orders = (table_ref, other_ref)
    blocks = table_ref.shape[0]
    down_rows, rows = hidden // blocks, width // blocks
    o_copies = place_halves(place_ref, orders, lists[2:], down_rows, rows, wo, so)
    u_copies = place_halves(place_ref, orders, lists[:2], 0, rows, wu, su)
    d_copies = place_halves(place_ref, orders, lists[2:], 0, down_rows, wd, sd)

    @pl.when(step == 0)
    def _():
        for c in o_copies + u_copies + d_copies:
            c.start()
        sums_ref[...] = jnp.zeros_like(sums_ref)
        upsum_ref[...] = jnp.zeros_like(upsum_ref)
        for c in o_copies:
            c.wait()

    vec = lambda i: vec_ref[i : i + 1, :]
    total = lambda v: jnp.sum(v, axis=0, keepdims=True)
    mine = pl.ds(pl.multiple_of(core * half, 128), half)
    theirs = pl.ds(pl.multiple_of((1 - core) * half, 128), half)
    mixed_s[:, mine] = mine_ref[...]
    mixed_s[:, theirs] = theirs_ref[...]
    mixed_ref[...] = mixed_s[...]
    groups = [slice(g * BLOCK, g * BLOCK + BLOCK) for g in range(x_ref.shape[0] // BLOCK)]
    chunks = [slice(c * CHUNK, c * CHUNK + CHUNK) for c in range(hidden // CHUNK)]
    firsts = [x_ref[g, :].astype(F32) + (dot(mixed_s[g, :], wo[...]) + vec(0)) for g in groups]
    ones = [normed_of(f) for f in firsts]
    normeds = [n * vec(1) + vec(2) for n, _ in ones]
    lows = [n.astype(BF16) for n in normeds]
    for g, low in zip(groups, lows):
        low_ref[g, :] = low

    @pl.when(step == 0)
    def _():
        for c in u_copies + d_copies:
            c.wait()

    seconds = [n + vec(3) for n in normeds]
    aheads = [dot(low, wu[:, chunks[0]]) for low in lows]
    for c, at in enumerate(chunks):
        for n, g in enumerate(groups):
            upward = aheads[n] + bu_ref[:, at]
            if c + 1 < len(chunks):
                aheads[n] = dot(lows[n], wu[:, chunks[c + 1]])
            activated, slope = gelu_and_slope(upward)
            activated = activated.astype(BF16)
            act_ref[g, at] = activated
            slope_s[g, at] = slope.astype(BF16)
            seconds[n] = seconds[n] + dot(activated, wd[at, :])
    sums = [0.0] * 6
    twos, grads = [], []
    for n, g in enumerate(groups):
        normal, scale = normed_of(seconds[n])
        valid = 1.0 - valid_ref[g, sequences : sequences + 1].astype(F32)
        out_ref[g, :] = (valid * (normal * vec(4) + vec(5))).astype(BF16)
        grad = og_ref[g, :].astype(F32) * valid
        grad_second = norm_back(grad, vec(4), normal, scale)
        grad_two = grad_second.astype(BF16)
        gtwo_ref[g, :] = grad_two
        sums[4] += total(grad * normal)
        sums[5] += total(grad)
        sums[3] += total(grad_two.astype(F32))
        twos.append(grad_two)
        grads.append(grad_second)
    aheads = [dot_right(two, wd[chunks[0], :]) for two in twos]
    for c, at in enumerate(chunks):
        for n, g in enumerate(groups):
            now = aheads[n]
            if c + 1 < len(chunks):
                aheads[n] = dot_right(twos[n], wd[chunks[c + 1], :])
            grad_up = (now * slope_s[g, at].astype(F32)).astype(BF16)
            gup_ref[g, at] = grad_up
            upsum_ref[:, at] += total(grad_up.astype(F32))
            grads[n] = grads[n] + dot_right(grad_up, wu[:, at])
    for n, g in enumerate(groups):
        normal, scale = ones[n]
        sums[1] += total(grads[n] * normal)
        sums[2] += total(grads[n])
        grad_one = norm_back(grads[n], vec(1), normal, scale).astype(BF16)
        gone_ref[g, :] = grad_one
        sums[0] += total(grad_one.astype(F32))
        gm_s[g, :] = dot_right(grad_one, wo[...]).astype(BF16)
    for i in range(6):
        sums_ref[i : i + 1, :] += sums[i]
    gm_mine_ref[...] = gm_s[:, mine]
    gm_theirs_ref[...] = gm_s[:, theirs]


def middle(place, table, other, x, mine, theirs, out_grad, valid, weights, vectors, up_bias):
    count, width = x.shape
    half = width // 2
    hidden = up_bias.shape[1]
    blocks = table.shape[0]
    row = lambda a: pl.BlockSpec((MIDDLE, a.shape[1]), lambda i, *_: (i, 0))
    rows_of = lambda n: pl.BlockSpec((MIDDLE, n), lambda i, *_: (i, 0))
    whole = lambda a: pl.BlockSpec(a.shape, lambda i, *_: (0, 0))
    anywhere = pl.BlockSpec(memory_space=pl.ANY)
    shape = lambda n: jax.ShapeDtypeStruct((count, n), BF16)
    sums, upsum = jax.ShapeDtypeStruct((8, width), F32), jax.ShapeDtypeStruct((1, hidden), F32)
    return pl.pallas_call(
        partial(middle_kernel, tuple(map(len, weights))),
        out_shape=(shape(width), shape(width), shape(hidden), shape(width), shape(hidden), shape(width), shape(half), shape(half), shape(width), sums, upsum),
        grid_spec=pltpu.PrefetchScalarGridSpec(
            num_scalar_prefetch=3,
            grid=(count // MIDDLE,),
            in_specs=[row(x), row(mine), row(theirs), row(out_grad), row(valid), whole(vectors), whole(up_bias)] + [anywhere] * sum(map(len, weights)),
            out_specs=[rows_of(width), rows_of(width), rows_of(hidden), rows_of(width), rows_of(hidden), rows_of(width), rows_of(half), rows_of(half), rows_of(width), whole(sums), whole(upsum)],
            scratch_shapes=[
                pltpu.VMEM((width, width), BF16), pltpu.VMEM((width, hidden), BF16), pltpu.VMEM((hidden, width), BF16),
                pltpu.VMEM((MIDDLE, width), BF16), pltpu.VMEM((MIDDLE, hidden), BF16), pltpu.VMEM((MIDDLE, width), BF16),
            ] + [pltpu.SemaphoreType.DMA((2 * blocks,))] * 3,
        ),
        compiler_params=pltpu.CompilerParams(vmem_limit_bytes=VMEM_LIMIT),
        cost_estimate=pl.CostEstimate(flops=2 * count * width * (2 * width + 4 * hidden), bytes_accessed=32 * 2**20, transcendentals=2 * count * hidden),
        name="middle",
    )(place, table, other, x, mine, theirs, out_grad, valid, vectors, up_bias, *(w for group in weights for w in group))


def outer_kernel(split, place_ref, table_ref, other_ref, left_ref, right_ref, mine_ref, theirs_ref, total_s, sem):
    step = pl.program_id(0)
    product = dot_rows(left_ref[...], right_ref[...]).astype(BF16)
    rows, columns = product.shape
    if split:
        total_s[:, pl.ds(pl.multiple_of(step * columns, 128), columns)] = product
    else:
        total_s[pl.ds(pl.multiple_of(step * rows, 256), rows), :] = product

    @pl.when(step == pl.num_programs(0) - 1)
    def _():
        blocks, rows, width = mine_ref.shape
        copies = []
        for n, (order, target) in enumerate(((other_ref, theirs_ref), (table_ref, mine_ref))):
            side = 1 - place_ref[0] if n == 0 else place_ref[0]
            for i in range(blocks):
                at = pl.ds(pl.multiple_of(order[i] * rows, math.gcd(rows, 256)), rows)
                copies.append(pltpu.make_async_copy(total_s.at[at, pl.ds(pl.multiple_of(side * width, 128), width)], target.at[i], sem.at[n * blocks + i]))
        for c in copies:
            c.start()
        for c in copies:
            c.wait()


def outer(place, table, other, left, right, split):
    count, rows = left.shape
    columns = right.shape[1]
    blocks = table.shape[0]
    shape = jax.ShapeDtypeStruct((blocks, rows // blocks, columns // 2), BF16)
    anywhere = pl.BlockSpec(memory_space=pl.ANY)
    if split:
        steps = columns // 512 if columns % 512 == 0 else columns // 384
        specs = [pl.BlockSpec((count, rows), lambda i, *_: (0, 0)), pl.BlockSpec((count, columns // steps), lambda i, *_: (0, i))]
    else:
        steps = rows // 512
        specs = [pl.BlockSpec((count, rows // steps), lambda i, *_: (0, i)), pl.BlockSpec((count, columns), lambda i, *_: (0, 0))]
    return pl.pallas_call(
        partial(outer_kernel, split),
        out_shape=(shape, shape),
        grid_spec=pltpu.PrefetchScalarGridSpec(
            num_scalar_prefetch=3,
            grid=(steps,),
            in_specs=specs,
            out_specs=[anywhere, anywhere],
            scratch_shapes=[pltpu.VMEM((rows, columns), BF16), pltpu.SemaphoreType.DMA((2 * blocks,))],
        ),
        compiler_params=pltpu.CompilerParams(vmem_limit_bytes=VMEM_LIMIT),
        cost_estimate=pl.CostEstimate(flops=2 * count * rows * columns, bytes_accessed=2 * (count * (rows + columns) + rows * columns), transcendentals=0),
        name="outer",
    )(place, table, other, left, right)


def qkv_grad_kernel(table_ref, own_ref, other_ref, down_ref, dother_ref, small_ref, out_ref, sums_ref, total_s, sem):
    step = pl.program_id(0)
    product = (dot_rows(own_ref[...], down_ref[...]) + dot_rows(other_ref[...], dother_ref[...])).astype(BF16)
    ones = jnp.ones((8, own_ref.shape[0]), BF16)
    sums_ref[...] = dot(ones, down_ref[...]) + dot(ones, dother_ref[...])
    columns = product.shape[1]
    total_s[:, pl.ds(pl.multiple_of(step * columns, 128), columns)] = product

    @pl.when(step == pl.num_programs(0) - 1)
    def _():
        blocks, rows, width = out_ref.shape
        copies = []
        for i in range(blocks):
            at = pl.ds(pl.multiple_of(table_ref[i] * rows, math.gcd(rows, 256)), rows)
            copies.append(pltpu.make_async_copy(total_s.at[at], out_ref.at[i], sem.at[i]))
        for c in copies:
            c.start()
        for c in copies:
            c.wait()


def qkv_grad(table, own, other, grad_own, grad_other):
    count, rows = own.shape
    columns = grad_own.shape[1]
    blocks = table.shape[0]
    whole = pl.BlockSpec((count, rows), lambda i, *_: (0, 0))
    tile = pl.BlockSpec((count, 384), lambda i, *_: (0, i))

    def kernel(table_ref, a, b, c, d, out_ref, sums_ref, total_s, sem):
        qkv_grad_kernel(table_ref, a, b, c, d, None, out_ref, sums_ref, total_s, sem)

    return pl.pallas_call(
        kernel,
        out_shape=(jax.ShapeDtypeStruct((blocks, rows // blocks, columns), BF16), jax.ShapeDtypeStruct((8, columns), F32)),
        grid_spec=pltpu.PrefetchScalarGridSpec(
            num_scalar_prefetch=1,
            grid=(columns // 384,),
            in_specs=[whole, whole, tile, tile],
            out_specs=[pl.BlockSpec(memory_space=pl.ANY), pl.BlockSpec((8, 384), lambda i, *_: (0, i))],
            scratch_shapes=[pltpu.VMEM((rows, columns), BF16), pltpu.SemaphoreType.DMA((blocks,))],
        ),
        compiler_params=pltpu.CompilerParams(vmem_limit_bytes=VMEM_LIMIT),
        cost_estimate=pl.CostEstimate(flops=4 * count * rows * columns, bytes_accessed=2 * (2 * count * (rows + columns) + rows * columns), transcendentals=0),
        name="qkv_grad",
    )(table, own, other, grad_own, grad_other)


def input_kernel(added, table_ref, grad_ref, *refs):
    added_refs, w_refs, (out_ref, w_s, sem) = refs[:added], refs[added:-3], refs[-3:]

    @pl.when(pl.program_id(0) == 0)
    def _():
        for c in load_rows(table_ref, w_refs, w_s, sem):
            c.wait()

    total = dot_right(grad_ref[...], w_s[...])
    for ref in added_refs:
        total = total + ref[...].astype(F32)
    out_ref[...] = total.astype(BF16)


def input_part(table, grad, weights, width, *added):
    count, columns = grad.shape
    blocks = table.shape[0]
    row = lambda n: pl.BlockSpec((BLOCK, n), lambda i, *_: (i, 0))
    return pl.pallas_call(
        partial(input_kernel, len(added)),
        out_shape=jax.ShapeDtypeStruct((count, width), BF16),
        grid_spec=pltpu.PrefetchScalarGridSpec(
            num_scalar_prefetch=1,
            grid=(count // BLOCK,),
            in_specs=[row(columns)] + [row(width)] * len(added) + [pl.BlockSpec(memory_space=pl.ANY)] * len(weights),
            out_specs=row(width),
            scratch_shapes=[pltpu.VMEM((width, columns), BF16), pltpu.SemaphoreType.DMA((blocks,))],
        ),
        compiler_params=pltpu.CompilerParams(vmem_limit_bytes=VMEM_LIMIT),
        cost_estimate=pl.CostEstimate(flops=2 * count * width * columns, bytes_accessed=2 * count * (columns + width * (1 + len(added))), transcendentals=0),
        name="input_part",
    )(table, grad, *added, *weights)


def copy_block(table_ref, source_ref, target_ref):
    target_ref[...] = source_ref[...]


def picked(blocks, table):
    block = (1, *blocks.shape[1:])
    return pl.pallas_call(
        copy_block,
        out_shape=jax.ShapeDtypeStruct(blocks.shape, blocks.dtype),
        grid_spec=pltpu.PrefetchScalarGridSpec(
            num_scalar_prefetch=1,
            grid=(blocks.shape[0],),
            in_specs=[pl.BlockSpec(block, lambda i, t: (t[i], 0, 0))],
            out_specs=pl.BlockSpec(block, lambda i, t: (i, 0, 0)),
        ),
        name="picked",
    )(table, blocks)


def sides(count):
    side = math.isqrt(count // 4)
    if count % 4 == 0 and 4 * side * side == count:
        return (4, side, side)
    return (count, 1, 1)


def hop(value, leg, step, shape):
    deep, tall, wide = shape
    count = deep * tall * wide
    pairs = []
    for core in range(2):
        for here in range(count):
            z, y, x = here // (tall * wide), here // wide % tall, here % wide
            if leg == 0:
                z = (z + step) % deep
            elif (leg == 1) == (core == 0):
                y = (y + step) % tall
            else:
                x = (x + step) % wide
            there = (z * tall + y) * wide + x
            pairs.append((core * count + there, core * count + here))
    return lax.ppermute(value, ("dp", "fsdp"), pairs)


def swapped(value):
    return lax.ppermute(value, "dp", [(0, 1), (1, 0)])


def received(blocks, leg, shape):
    return [hop(blocks, leg, s, shape) for s in range(1, shape[leg])]


def sent(total, leg, shape):
    pieces = total.reshape(shape[leg], -1, *total.shape[1:])
    return [pieces[0]] + [hop(pieces[s], leg, shape[leg] - s, shape) for s in range(1, shape[leg])]


def summed(values):
    return sum(v.astype(F32) for v in values).astype(BF16)


def tied(value, *others):
    return lax.optimization_barrier((value, *others))[0]


def tied_list(values, *others):
    return list(lax.optimization_barrier((tuple(values), *others))[0])


def order(core, shape):
    deep, tall, wide = shape
    here = lax.axis_index("fsdp")
    z, y, x = here // (tall * wide), here // wide % tall, here % wide
    slot = jnp.arange(deep * tall * wide, dtype=jnp.int32)
    first, second = slot // deep % tall, slot // (deep * tall)
    z = (z + slot % deep) % deep
    y = (y + jnp.where(core == 0, first, second)) % tall
    x = (x + jnp.where(core == 0, second, first)) % wide
    return (z * tall + y) * wide + x


def inverse(table):
    slots = jnp.arange(table.shape[0], dtype=jnp.int32)
    return jnp.sum(jnp.where(table[None, :] == slots[:, None], slots[None, :], 0), axis=1)


def half_of(array, side):
    width = array.shape[1] // 2
    return lax.dynamic_slice_in_dim(array, side * width, width, 1)


def joined(mine, theirs, core):
    first = jnp.where(core == 0, mine, theirs)
    second = jnp.where(core == 0, theirs, mine)
    return first, second


def reordered(small, table):
    slots = jnp.arange(table.shape[0], dtype=jnp.int32)
    chosen = (table[:, None] == slots[None, :]).astype(F32)
    flat = small.reshape(table.shape[0], -1)
    return jnp.dot(chosen, flat, precision=lax.Precision.HIGHEST).reshape(small.shape)


def shards(
    hidden_in,
    lengths,
    out_grad,
    query_matrix,
    query_offset,
    key_matrix,
    key_offset,
    value_matrix,
    value_offset,
    output_matrix,
    output_offset,
    first_gain,
    first_offset,
    up_matrix,
    up_offset,
    down_matrix,
    down_offset,
    second_gain,
    second_offset,
):
    count, width = hidden_in.shape
    half = width // 2
    rows = query_matrix.shape[0]
    parts = up_offset.shape[0] // rows
    core = lax.axis_index("dp")
    shape = sides(lax.axis_size("fsdp"))
    positions = math.prod(shape)
    table, other_table = order(core, shape), order(1 - core, shape)
    direct = rows % 16 == 0
    place = jnp.reshape(core, (1,)).astype(jnp.int32)
    zero = jnp.zeros((1,), jnp.int32)
    own_order, their_order = (table, other_table) if direct else (zero, zero)
    down_rows = down_matrix.shape[0]
    join = lambda arrays: jnp.concatenate(arrays, axis=0)

    def usable(pieces, places, cuts):
        if direct:
            return pieces
        blocks, parts, first = join(pieces), [], 0
        for cut in cuts:
            parts.append(picked(blocks[:, first : first + cut], inverse(places)).reshape(1, -1, blocks.shape[2]))
            first += cut
        return [jnp.concatenate(parts, axis=1)]

    def in_blocks(array, places):
        return array if direct else picked(array.reshape(positions, -1, array.shape[2]), places)

    vectors = (
        query_offset, key_offset, value_offset, output_offset, first_gain, first_offset,
        down_offset, second_gain, second_offset,
    )
    left = jnp.pad(jnp.stack(vectors), ((0, rows - len(vectors)), (0, 64 - rows)))
    right = jnp.pad(up_offset.reshape(parts, rows), ((0, rows - parts), (0, 64 - rows)))
    halves = [half_of(m, core) for m in (query_matrix, key_matrix, value_matrix)]
    unit = jnp.concatenate(halves + [left, right], axis=1)[None]
    attn_far = received(unit, 0, shape)
    other_lengths = swapped(lengths)
    other_in = swapped(hidden_in)
    tables, plan, valid = described(lengths[0], count)
    attn_four = join([unit] + attn_far)
    attn_far = received(attn_four, 1, shape)
    up_unit = tied(half_of(up_matrix, core)[None], attn_four)
    up_far = received(up_unit, 0, shape)
    other_tables, other_plan, _ = described(tied(other_lengths, attn_four)[0], count)
    attn_eight = join([attn_four] + attn_far)
    attn_far = received(attn_eight, 2, shape)
    attn = [attn_eight] + attn_far
    down_unit = jnp.concatenate([half_of(down_matrix, core), half_of(output_matrix, core)], axis=0)[None]
    down_unit = tied(down_unit, attn_eight)
    down_far = received(down_unit, 0, shape)

    small = reordered(join([a[:, :, 3 * half :] for a in attn]).astype(F32), inverse(table))
    whole = small[:, : len(vectors), :rows].swapaxes(0, 1).reshape(len(vectors), width)
    up_bias = small[:, :parts, 64 : 64 + rows].reshape(1, -1)
    bias = lax.dynamic_slice_in_dim(whole[:3], core * half, half, 1).reshape(1, -1)
    vector_rows = jnp.pad(whole[3:], ((0, 2), (0, 0)))
    attn = usable(attn, table, (rows,))

    up_four = join([up_unit] + tied_list(up_far, *attn))
    up_far = received(up_four, 1, shape)
    other_q, other_k, other_v, other_norms = project(tied(other_in, up_four, *tables), attn, own_order, bias, other_tables)
    up_eight = join([up_four] + tied_list(up_far, other_q))
    up_far = received(up_eight, 2, shape)
    up_swapped = [swapped(up_eight)]
    other_mixed, other_lse = attend(other_plan, tied(other_q, up_eight), other_k, other_v, other_norms, other_tables[2])
    mixed_theirs = swapped(other_mixed)
    down_four = join([down_unit] + tied_list(down_far, other_mixed))
    down_far = received(down_four, 1, shape)
    q, k, v, norms = project(tied(hidden_in, down_four), attn, own_order, bias, tables)
    up_far = tied_list(up_far, q)
    up_swapped += [swapped(far) for far in up_far]
    down_eight = join([down_four] + tied_list(down_far, q))
    down_far = received(down_eight, 2, shape)
    down_swapped = [swapped(down_eight)]
    mixed, lse = attend(plan, tied(q, down_eight, *up_far), k, v, norms, tables[2])
    down_far = tied_list(down_far, mixed)
    down_swapped += [swapped(far) for far in down_far]
    up_weights = [usable([up_eight] + up_far, table, (rows,)), usable(up_swapped, other_table, (rows,))]
    down_weights = [
        usable([down_eight] + down_far, table, (down_rows, rows)),
        usable(down_swapped, other_table, (down_rows, rows)),
    ]

    (
        hidden_out, normed_low, activated, grad_two, grad_up, grad_one, grad_mine, grad_theirs, both_mixed, sums, up_sum,
    ) = middle(
        place, own_order, their_order, hidden_in, mixed, mixed_theirs, out_grad, tables[2],
        up_weights + down_weights, vector_rows, up_bias,
    )
    other_grad = swapped(grad_theirs)
    places = (place, own_order, their_order)
    slots_of = lambda vectors: vectors.reshape(-1, positions, rows).swapaxes(0, 1)
    left = jnp.pad(slots_of(sums[:6]), ((0, 0), (0, rows - 6), (0, 64 - rows)))
    right = jnp.pad(up_sum.reshape(positions, parts, rows), ((0, 0), (0, rows - parts), (0, 64 - rows)))
    slot_sums = jnp.concatenate([left, right], axis=2)
    slot_mine, slot_theirs = (reordered(slot_sums, t).astype(BF16) for t in (table, other_table))

    down_pair = outer(*places, activated, grad_two, 0)
    down_arrived = swapped(in_blocks(down_pair[1], other_table))
    up_pair = outer(*places, normed_low, tied(grad_up, down_pair[1]), 1)
    up_arrived = swapped(in_blocks(up_pair[1], other_table))
    down_total = summed([in_blocks(down_pair[0], table), tied(down_arrived, up_pair[0])])
    down_sent = sent(down_total, 2, shape)
    output_pair = outer(*places, tied(both_mixed, down_total), grad_one, 1)
    output_theirs = jnp.concatenate([in_blocks(output_pair[1], other_table), slot_theirs], axis=2)
    output_arrived = swapped(output_theirs)
    up_total = summed([in_blocks(up_pair[0], table), tied(up_arrived, output_pair[0])])
    other_d = attend_back(
        other_plan, other_q, other_k, other_v, other_lse, other_mixed,
        tied(other_grad, up_total, output_theirs), other_tables,
    )
    output_mine = jnp.concatenate([in_blocks(output_pair[0], table), slot_mine], axis=2)
    output_total = summed([output_mine, tied(output_arrived, other_d)])
    up_total = jnp.concatenate([up_total, output_total], axis=2)
    up_sent = sent(up_total, 2, shape)
    down_total = summed(tied_list(down_sent, other_d))
    down_sent = sent(down_total, 1, shape)
    own_d = attend_back(plan, q, k, v, lse, mixed, tied(grad_mine, down_total, up_total), tables)
    up_total = summed(tied_list(up_sent, own_d))
    up_sent = sent(up_total, 1, shape)
    down_total = summed(tied_list(down_sent, own_d))
    down_sent = sent(down_total, 0, shape)
    matrices, qkv_sums = qkv_grad(own_order, hidden_in, other_in, tied(own_d, up_total, down_total), other_d)
    own_sums = jnp.zeros((3, width), F32)
    own_sums = lax.dynamic_update_slice_in_dim(own_sums, qkv_sums[0].reshape(3, half), core * half, 1)
    own_sums = jnp.pad(slots_of(own_sums), ((0, 0), (0, rows - 3), (0, 128 - rows)))
    matrices = jnp.concatenate([in_blocks(matrices, table), reordered(own_sums, table).astype(BF16)], axis=2)
    matrices_sent = sent(matrices, 2, shape)
    up_total = summed(tied_list(up_sent, matrices))
    up_sent = sent(up_total, 0, shape)
    down_done = summed(tied_list(down_sent, matrices))[0]
    down_other = swapped(down_done)
    sent_grad = input_part(own_order, tied(other_d, up_total, down_done), attn, width)
    other_part = swapped(sent_grad)
    matrices_total = summed(tied_list(matrices_sent, sent_grad))
    matrices_sent = sent(matrices_total, 1, shape)
    input_grad = input_part(own_order, tied(own_d, matrices_total), attn, width, other_part, grad_one)
    matrices_total = summed(tied_list(matrices_sent, input_grad))
    matrices_sent = sent(matrices_total, 0, shape)
    up_done = summed(tied_list(up_sent, matrices_total))[0]
    up_other = swapped(up_done)
    matrices_done = summed(matrices_sent)[0]

    up_first, up_second = joined(up_done, up_other, core)
    down_first, down_second = joined(down_done, down_other, core)
    first, second = joined(matrices_done, swapped(matrices_done), core)
    wide = lambda a, b: jnp.concatenate([a, b], axis=1).astype(F32)
    pick = lambda n: wide(first[:, n * half : (n + 1) * half], second[:, n * half : (n + 1) * half])
    offsets = first[:3, 3 * half : 3 * half + rows].astype(F32) + second[:3, 3 * half : 3 * half + rows].astype(F32)
    hidden = up_matrix.shape[1] // 2
    others = up_first[:, hidden + half :].astype(F32)
    columns = slice(hidden, hidden + half)
    return (
        hidden_out,
        input_grad,
        pick(0),
        offsets[0],
        pick(1),
        offsets[1],
        pick(2),
        offsets[2],
        wide(up_first[:, columns], up_second[:, columns]),
        others[0, :rows],
        others[1, :rows],
        others[2, :rows],
        wide(up_first[:, :hidden], up_second[:, :hidden]),
        others[:parts, 64 : 64 + rows].reshape(-1),
        wide(down_first, down_second),
        others[3, :rows],
        others[4, :rows],
        others[5, :rows],
    )


def solution(mesh):
    placed = (
        P(("dp", "fsdp"), None),
        P(("dp", "fsdp"), None),
        P(("dp", "fsdp"), None),
        P("fsdp", None),
        P("fsdp"),
        P("fsdp", None),
        P("fsdp"),
        P("fsdp", None),
        P("fsdp"),
        P("fsdp", None),
        P("fsdp"),
        P("fsdp"),
        P("fsdp"),
        P("fsdp", None),
        P("fsdp"),
        P("fsdp", None),
        P("fsdp"),
        P("fsdp"),
        P("fsdp"),
    )
    return jax.shard_map(
        shards,
        mesh=mesh,
        in_specs=placed,
        out_specs=(
            P(("dp", "fsdp"), None),
            P(("dp", "fsdp"), None),
            P("fsdp", None),
            P("fsdp"),
            P("fsdp", None),
            P("fsdp"),
            P("fsdp", None),
            P("fsdp"),
            P("fsdp", None),
            P("fsdp"),
            P("fsdp"),
            P("fsdp"),
            P("fsdp", None),
            P("fsdp"),
            P("fsdp", None),
            P("fsdp"),
            P("fsdp"),
            P("fsdp"),
        ),
        check_vma=False,
    )
```

```python
import math
from functools import partial
import jax, jax.numpy as jnp
from jax import lax
from jax.experimental import pallas as pl
from jax.experimental.pallas import tpu as pltpu
from jax.sharding import PartitionSpec as P

HEAD_DIM = 64
EPSILON = 1e-12
FAR = -1e30
LOG2E = 1.4426950408889634
BLOCK = 256
SAFE = 105.0
F32 = jnp.float32
BF16 = jnp.bfloat16
VMEM_LIMIT = 58 * 2**20


def dot(a, b):
    return jnp.dot(a, b, preferred_element_type=F32)


def dot_right(a, b):
    return lax.dot_general(a, b, (((1,), (1,)), ((), ())), preferred_element_type=F32)


def dot_rows(a, b):
    return lax.dot_general(a, b, (((0,), (0,)), ((), ())), preferred_element_type=F32)


def turned(value, cosines, sines, even_lane):
    partner = jnp.where(even_lane, -pltpu.roll(value, 127, 1), pltpu.roll(value, 1, 1))
    return value * cosines + partner * sines


def lse_lane(head):
    return (HEAD_DIM if head % 2 == 0 else 0) + 8 + 3 * head


def delta_lane(head, heads):
    return lse_lane(head) + 3 * heads


def lanes_of(rows):
    return lax.broadcasted_iota(jnp.int32, (rows, 128), 1)


def load_rows(table_ref, source_refs, target_ref, sem):
    copies = []
    for source in source_refs:
        rows = source.shape[1]
        for i in range(source.shape[0]):
            n = len(copies)
            at = pl.ds(pl.multiple_of(table_ref[n] * rows, math.gcd(rows, 256)), rows)
            copies.append(pltpu.make_async_copy(source.at[i, :, pl.ds(0, target_ref.shape[1])], target_ref.at[at], sem.at[n]))
    for c in copies:
        c.start()
    return copies


def project_kernel(table_ref, x_ref, bias_ref, cos_ref, sin_ref, extq_ref, extk_ref, *refs):
    *w_refs, q_ref, k_ref, v_ref, norm_ref, w_s, sem = refs
    step = pl.program_id(0)

    @pl.when(step == 0)
    def _():
        for c in load_rows(table_ref, w_refs, w_s, sem):
            c.wait()
        norm_ref[...] = jnp.zeros_like(norm_ref)

    heads = q_ref.shape[0]
    width = heads * HEAD_DIM
    lane = lanes_of(BLOCK)
    first_half = lane < HEAD_DIM
    even_lane = lax.rem(lane, 2) == 0
    y = dot(x_ref[...], w_s[...]) + bias_ref[...]
    cosines, sines = cos_ref[...], sin_ref[...]
    extq, extk = extq_ref[...].astype(F32), extk_ref[...].astype(F32)
    row = lax.broadcasted_iota(jnp.int32, (128, BLOCK), 0)
    squares = []
    for p in range(width // 128):
        at = slice(p * 128, p * 128 + 128)
        q = turned(y[:, at], cosines, sines, even_lane) * (HEAD_DIM**-0.5 * LOG2E)
        k = turned(y[:, width + p * 128 : width + p * 128 + 128], cosines, sines, even_lane)
        v = y[:, 2 * width + p * 128 : 2 * width + p * 128 + 128].T
        squares.append(((q * q).astype(BF16), (k * k).astype(BF16)))
        for h in (2 * p, 2 * p + 1):
            own = first_half if h % 2 == 0 else jnp.logical_not(first_half)
            start = lse_lane(h)
            ones = (lane >= start) & (lane < start + 3)
            q_ref[h] = jnp.where(own, q, extq).astype(BF16)
            k_ref[h] = jnp.where(own, k, jnp.where(ones, 1.0, extk)).astype(BF16)
            start = delta_lane(h, heads)
            ones = (row >= start) & (row < start + 3)
            own = row < HEAD_DIM if h % 2 == 0 else row >= HEAD_DIM
            v_ref[h] = jnp.where(own, v, jnp.where(ones, 1.0, 0.0)).astype(BF16)
    column = lax.broadcasted_iota(jnp.int32, (width, 128), 0) // HEAD_DIM
    picks = jnp.where(column == lax.broadcasted_iota(jnp.int32, (width, 128), 1), 1.0, 0.0).astype(BF16)
    sums = [dot(jnp.concatenate([a[n] for a in squares], axis=1), picks) for n in range(2)]
    most = [jnp.max(t, axis=0, keepdims=True) for t in sums]
    norm_ref[...] = jnp.maximum(norm_ref[...], jnp.concatenate(most, axis=1))


def project(x, weights, table, bias, tables):
    count, width = x.shape
    blocks = table.shape[0]
    total = bias.shape[1]
    heads = total // (3 * HEAD_DIM)
    cosines, sines, extq, extk = tables
    row = lambda a: pl.BlockSpec((BLOCK, a.shape[1]), lambda i, t: (i, 0))
    head = pl.BlockSpec((heads, BLOCK, 128), lambda i, t: (0, i, 0))
    shape = jax.ShapeDtypeStruct((heads, count, 128), BF16)
    return pl.pallas_call(
        project_kernel,
        out_shape=(shape, shape, jax.ShapeDtypeStruct((heads, 128, count), BF16), jax.ShapeDtypeStruct((8, 256), F32)),
        grid_spec=pltpu.PrefetchScalarGridSpec(
            num_scalar_prefetch=1,
            grid=(count // BLOCK,),
            in_specs=[
                row(x), pl.BlockSpec((1, total), lambda i, t: (0, 0)), row(cosines), row(sines), row(extq), row(extk),
            ]
            + [pl.BlockSpec(memory_space=pl.ANY)] * len(weights),
            out_specs=[head, head, pl.BlockSpec((heads, 128, BLOCK), lambda i, t: (0, 0, i)), pl.BlockSpec((8, 256), lambda i, t: (0, 0))],
            scratch_shapes=[pltpu.VMEM((width, total), BF16), pltpu.SemaphoreType.DMA((blocks,))],
        ),
        compiler_params=pltpu.CompilerParams(vmem_limit_bytes=VMEM_LIMIT),
        cost_estimate=pl.CostEstimate(flops=10**11, bytes_accessed=1000, transcendentals=0),
        name="project",
    )(table, x, bias, cosines, sines, extq, extk, *weights)


def three_parts(value):
    high = value.astype(BF16).astype(F32)
    rest = value - high
    middle = rest.astype(BF16).astype(F32)
    return high, middle, rest - middle


def attend_kernel(plan_ref, q_ref, k_ref, v_ref, norm_ref, extq_ref, mixed_ref, lse_ref):
    step = pl.program_id(0)
    heads, count, _ = k_ref.shape
    blocks = count // BLOCK
    first, need = plan_ref[2 * step], plan_ref[2 * step + 1]
    safe = jnp.max(norm_ref[:, :128]) * jnp.max(norm_ref[:, 128:]) < SAFE * SAFE
    lane = lanes_of(BLOCK)
    start_lane, any_lane = lane < 0, lane < 0
    for h in range(heads):
        start_lane = start_lane | (lane == lse_lane(h))
        any_lane = any_lane | ((lane >= lse_lane(h)) & (lane < lse_lane(h) + 3))
    pad = extq_ref[:, HEAD_DIM + 4 : HEAD_DIM + 5].astype(F32) > 0.5

    def rows_of(c, plain):
        keys = pl.ds(pl.multiple_of(jnp.minimum(first, blocks - c) * BLOCK, BLOCK), c * BLOCK)
        scores = [dot_right(k_ref[h, keys, :], q_ref[h]) for h in range(heads)]
        outs = []
        packs = [jnp.zeros((24, BLOCK), F32)] * 2
        row = lax.broadcasted_iota(jnp.int32, (24, BLOCK), 0)
        for h in range(heads):
            s = scores[h]
            if not plain:
                peak = jnp.max(s, axis=0, keepdims=True)
                s = s - peak
            o = dot(v_ref[h, :, keys], jnp.exp2(s).astype(BF16))
            ones = delta_lane(h, heads)
            total = o[ones : ones + 1, :]
            outs.append((o[:HEAD_DIM] if h % 2 == 0 else o[HEAD_DIM:]) / total)
            lse = -jnp.log2(total)
            if not plain:
                lse = lse - peak
            for j, part in enumerate(three_parts(lse)):
                packs[h % 2] = jnp.where(row == 3 * h + j, part, packs[h % 2])
        mixed_ref[...] = jnp.concatenate(outs, axis=0).T.astype(BF16)
        gap = lambda n: jnp.zeros((n, BLOCK), F32)
        packed = jnp.concatenate([gap(8), packs[1], gap(40), packs[0], gap(32)], axis=0).T
        lse_ref[...] = jnp.where(pad & any_lane, jnp.where(start_lane, FAR, 0.0), packed).astype(BF16)

    @pl.when(need == 0)
    def _():
        mixed_ref[...] = jnp.zeros_like(mixed_ref)
        lse_ref[...] = jnp.where(start_lane, FAR, 0.0).astype(BF16)

    for c in range(1, blocks + 1):
        pl.when(safe & (need == c))(partial(rows_of, c, True))
    pl.when(jnp.logical_not(safe) & (need > 0))(partial(rows_of, blocks, False))


def attend(plan, q, k, v, norms, extq):
    heads, count, _ = q.shape
    whole = lambda a: pl.BlockSpec(a.shape, lambda i, p: (0,) * a.ndim)
    return pl.pallas_call(
        attend_kernel,
        out_shape=(jax.ShapeDtypeStruct((count, heads * HEAD_DIM), BF16), jax.ShapeDtypeStruct((count, 128), BF16)),
        grid_spec=pltpu.PrefetchScalarGridSpec(
            num_scalar_prefetch=1,
            grid=(count // BLOCK,),
            in_specs=[
                pl.BlockSpec((heads, BLOCK, 128), lambda i, p: (0, i, 0)), whole(k), whole(v), whole(norms),
                pl.BlockSpec((BLOCK, 128), lambda i, p: (i, 0)),
            ],
            out_specs=[pl.BlockSpec((BLOCK, heads * HEAD_DIM), lambda i, p: (i, 0)), pl.BlockSpec((BLOCK, 128), lambda i, p: (i, 0))],
        ),
        compiler_params=pltpu.CompilerParams(vmem_limit_bytes=VMEM_LIMIT),
        cost_estimate=pl.CostEstimate(flops=10**11, bytes_accessed=1000, transcendentals=0),
        name="attend",
    )(plan, q, k, v, norms, extq)


def attend_back_kernel(plan_ref, q_ref, k_ref, v_ref, lse_ref, mixed_ref, grad_ref, cos_ref, sin_ref, cos_all, sin_all,
                       d_ref, dk_s, dv_s):
    step = pl.program_id(0)
    heads, count, _ = k_ref.shape
    width = heads * HEAD_DIM
    blocks = count // BLOCK
    first, need = plan_ref[2 * step], plan_ref[2 * step + 1]
    lane = lanes_of(BLOCK)
    first_half = lane < HEAD_DIM
    even_lane = lax.rem(lane, 2) == 0
    scale = HEAD_DIM**-0.5

    @pl.when(step == 0)
    def _():
        dk_s[...] = jnp.zeros_like(dk_s)
        dv_s[...] = jnp.zeros_like(dv_s)

    def rows_of(c):
        keys = pl.ds(pl.multiple_of(jnp.minimum(first, blocks - c) * BLOCK, BLOCK), c * BLOCK)
        grad = grad_ref[...].astype(F32)
        product = grad * mixed_ref[...].astype(F32)
        high = product.astype(BF16)
        low = (product - high.astype(F32)).astype(BF16)
        column = lax.broadcasted_iota(jnp.int32, (width, 128), 0) // HEAD_DIM
        slot = lax.broadcasted_iota(jnp.int32, (width, 128), 1)
        slot = slot - jnp.where(lax.rem(column, 2) == 0, delta_lane(0, heads), delta_lane(0, heads) - HEAD_DIM)
        picks = jnp.where((slot >= 3 * column) & (slot < 3 * column + 3), 1.0, 0.0).astype(BF16)
        delta = three_parts(-(dot(high, picks) + dot(low, picks)))
        inner = jnp.where(first_half, lane, lane - HEAD_DIM)
        part = lax.rem(inner + 1, 3)
        delta = jnp.where(part == 0, delta[0], jnp.where(part == 1, delta[1], delta[2]))
        extra = jnp.where(inner < 8 + 3 * heads, lse_ref[...].astype(F32), delta)
        dqs = []
        for p in range(width // 128):
            at = slice(p * 128, p * 128 + 128)
            pair = grad[:, at]
            pair_t = pair.T.astype(BF16)
            qs = [q_ref[2 * p].astype(F32), q_ref[2 * p + 1].astype(F32)]
            q_t = jnp.where(first_half, qs[0], qs[1]).T.astype(BF16)
            both = []
            for n in range(2):
                h = 2 * p + n
                own = first_half if n == 0 else jnp.logical_not(first_half)
                side = slice(n * HEAD_DIM, n * HEAD_DIM + HEAD_DIM)
                g = jnp.where(own, pair, extra).astype(BF16)
                q = jnp.where(own | (inner < 8), qs[n], extra).astype(BF16)
                k = k_ref[h, keys, :]
                probs = jnp.exp2(dot_right(q, k))
                shifted = dot(g, v_ref[h, :, keys])
                grads = (probs * shifted).astype(BF16)
                dv_s[h, :, keys] += dot(pair_t[side], probs.astype(BF16))
                dk_s[h, :, keys] += dot(q_t[side], grads)
                both.append(dot(grads, k))
            dq = jnp.where(first_half, both[0], both[1]) * scale
            d_ref[pl.ds(pl.multiple_of(step * BLOCK, BLOCK), BLOCK), at] = turned(dq, cos_ref[...], -sin_ref[...], even_lane).astype(BF16)

    @pl.when(need == 0)
    def _():
        d_ref[pl.ds(pl.multiple_of(step * BLOCK, BLOCK), BLOCK), :width] = jnp.zeros((BLOCK, width), BF16)

    for c in range(1, blocks + 1):
        pl.when(need == c)(partial(rows_of, c))

    @pl.when(step == blocks - 1)
    def _():
        for p in range(width // 128):
            for r in range(blocks):
                at = slice(r * BLOCK, r * BLOCK + BLOCK)
                dv = jnp.concatenate([dv_s[2 * p, :, at], dv_s[2 * p + 1, :, at]], axis=0).T
                dk = jnp.concatenate([dk_s[2 * p, :, at], dk_s[2 * p + 1, :, at]], axis=0).T * (1.0 / LOG2E)
                d_ref[at, 2 * width + p * 128 : 2 * width + p * 128 + 128] = dv.astype(BF16)
                d_ref[at, width + p * 128 : width + p * 128 + 128] = turned(dk, cos_all[at, :], -sin_all[at, :], even_lane).astype(BF16)


def attend_back(plan, q, k, v, lse, mixed, grad, tables):
    heads, count, _ = q.shape
    width = heads * HEAD_DIM
    cosines, sines = tables[:2]
    whole = lambda a: pl.BlockSpec(a.shape, lambda i, p: (0,) * a.ndim)
    row = lambda a: pl.BlockSpec((BLOCK, a.shape[1]), lambda i, p: (i, 0))
    shape = jax.ShapeDtypeStruct((count, 3 * width), BF16)
    return pl.pallas_call(
        attend_back_kernel,
        out_shape=shape,
        grid_spec=pltpu.PrefetchScalarGridSpec(
            num_scalar_prefetch=1,
            grid=(count // BLOCK,),
            in_specs=[
                pl.BlockSpec((heads, BLOCK, 128), lambda i, p: (0, i, 0)), whole(k), whole(v), row(lse), row(mixed), row(grad),
                row(cosines), row(sines), whole(cosines), whole(sines),
            ],
            out_specs=pl.BlockSpec((count, 3 * width), lambda i, p: (0, 0)),
            scratch_shapes=[pltpu.VMEM((heads, HEAD_DIM, count), F32)] * 2,
        ),
        compiler_params=pltpu.CompilerParams(vmem_limit_bytes=VMEM_LIMIT),
        cost_estimate=pl.CostEstimate(flops=10**11, bytes_accessed=1000, transcendentals=0),
        name="attend_back",
    )(plan, q, k, v, lse, mixed, grad, cosines, sines, cosines, sines)


def described(lengths, count):
    total = lengths.shape[0]
    index = jnp.arange(total)
    ends = jnp.sum(jnp.where(index[:, None] >= index[None, :], lengths[None, :], 0), axis=1)
    starts = ends - lengths
    slots = jnp.arange(count, dtype=jnp.int32)
    segment = jnp.sum((slots[:, None] >= ends[None, :]).astype(jnp.int32), axis=1)
    owner = segment[:, None] == jnp.arange(total, dtype=jnp.int32)[None, :]
    begin = jnp.sum(jnp.where(owner, starts[None, :], 0), axis=1)
    position = (slots - begin).astype(F32)
    lane = jnp.arange(128, dtype=jnp.int32)
    inverse = jnp.power(10000.0, -2.0 * (lane % HEAD_DIM // 2).astype(F32) / HEAD_DIM)
    angle = position[:, None] * inverse[None, :]
    cosines, sines = jnp.cos(angle), jnp.sin(angle)
    code = (lane % HEAD_DIM)[None, :]
    extq = jnp.where(code == segment[:, None], 1.0, 0.0).astype(BF16)
    extk = jnp.where((code < total) & (code != segment[:, None]), FAR, 0.0).astype(BF16)
    filled = jnp.sum(lengths)
    opens = jnp.arange(count // BLOCK, dtype=jnp.int32) * BLOCK
    closes = jnp.minimum(opens + BLOCK, filled)
    low = jnp.max(jnp.where(ends[None, :] <= opens[:, None], ends[None, :], 0), axis=1)
    high = jnp.min(jnp.where(ends[None, :] >= closes[:, None], ends[None, :], filled), axis=1)
    first = low // BLOCK
    need = jnp.where(opens < filled, (high + BLOCK - 1) // BLOCK - first, 0)
    plan = jnp.stack([first, need], axis=1).reshape(-1)
    valid = (segment < total).astype(F32)
    return (cosines, sines, extq, extk), plan, valid


def normed_of(value):
    center = value - jnp.mean(value, axis=1, keepdims=True)
    scale = lax.rsqrt(jnp.mean(center * center, axis=1, keepdims=True) + EPSILON)
    return center * scale, scale


def norm_back(grad, gain, normed, scale):
    scaled = grad * gain
    return (scaled - jnp.mean(scaled, axis=1, keepdims=True) - normed * jnp.mean(scaled * normed, axis=1, keepdims=True)) * scale


def gelu_and_slope(value):
    bell = jnp.exp2(value * value * (-0.5 * LOG2E))
    t = 1.0 / (1.0 + (0.3275911 * 0.5**0.5) * jnp.abs(value))
    tail = t * (0.5 * 0.254829592 + t * (0.5 * -0.284496736 + t * (0.5 * 1.421413741 + t * (0.5 * -1.453152027 + t * (0.5 * 1.061405429)))))
    tail = tail * bell
    below = jnp.where(value < 0.0, tail, 1.0 - tail)
    return value * below, below + value * bell * (2.0 * math.pi) ** -0.5


CHUNK = 1024
MIDDLE = 512


def place_halves(place_ref, orders, sources, first, rows, target_ref, sem):
    copies = []
    for n, (order, refs) in enumerate(zip(orders, sources)):
        side = place_ref[0] if n == 0 else 1 - place_ref[0]
        blocks = 0
        for ref in refs:
            width = ref.shape[2]
            for i in range(ref.shape[0]):
                at = pl.ds(pl.multiple_of(order[blocks] * rows, math.gcd(rows, 256)), rows)
                columns = pl.ds(pl.multiple_of(side * width, 128), width)
                copies.append(pltpu.make_async_copy(ref.at[i, pl.ds(first, rows)], target_ref.at[at, columns], sem.at[len(copies)]))
                blocks += 1
    return copies


def middle_kernel(counts, place_ref, table_ref, other_ref, down_table_ref, other_down_ref, x_ref, mine_ref, theirs_ref, og_ref, valid_ref, vec_ref, bu_ref, *refs):
    weight_refs, refs = refs[: sum(counts)], refs[sum(counts) :]
    (
        out_ref, low_ref, act_ref, gtwo_ref, gup_ref, gone_ref, gm_mine_ref, gm_theirs_ref, mixed_ref, sums_ref, upsum_ref,
        wo, wu, wd, mixed_s, slope_s, gm_s, so, su, sd,
    ) = refs
    step = pl.program_id(0)
    sequences = 4
    core = place_ref[0]
    half = mine_ref.shape[1]
    width = 2 * half
    hidden = bu_ref.shape[1]
    lists = [weight_refs[sum(counts[:n]) : sum(counts[: n + 1])] for n in range(4)]
    orders, down_orders = (table_ref, other_ref), (down_table_ref, other_down_ref)
    blocks = table_ref.shape[0]
    down_rows, rows = hidden // blocks, width // blocks
    o_copies = place_halves(place_ref, down_orders, lists[2:], down_rows, rows, wo, so)
    u_copies = place_halves(place_ref, orders, lists[:2], 0, rows, wu, su)
    d_copies = place_halves(place_ref, down_orders, lists[2:], 0, down_rows, wd, sd)

    @pl.when(step == 0)
    def _():
        for c in o_copies + u_copies + d_copies:
            c.start()
        sums_ref[...] = jnp.zeros_like(sums_ref)
        upsum_ref[...] = jnp.zeros_like(upsum_ref)
        for c in o_copies:
            c.wait()

    vec = lambda i: vec_ref[i : i + 1, :]
    total = lambda v: jnp.sum(v, axis=0, keepdims=True)
    mine = pl.ds(pl.multiple_of(core * half, 128), half)
    theirs = pl.ds(pl.multiple_of((1 - core) * half, 128), half)
    mixed_s[:, mine] = mine_ref[...]
    mixed_s[:, theirs] = theirs_ref[...]
    mixed_ref[...] = mixed_s[...]
    groups = [slice(g * BLOCK, g * BLOCK + BLOCK) for g in range(x_ref.shape[0] // BLOCK)]
    chunks = [slice(c * CHUNK, c * CHUNK + CHUNK) for c in range(hidden // CHUNK)]
    firsts = [x_ref[g, :].astype(F32) + (dot(mixed_s[g, :], wo[...]) + vec(0)) for g in groups]
    ones = [normed_of(f) for f in firsts]
    normeds = [n * vec(1) + vec(2) for n, _ in ones]
    lows = [n.astype(BF16) for n in normeds]
    for g, low in zip(groups, lows):
        low_ref[g, :] = low

    @pl.when(step == 0)
    def _():
        for c in u_copies:
            c.wait()

    seconds = [n + vec(3) for n in normeds]
    aheads = [dot(low, wu[:, chunks[0]]) for low in lows]
    for c, at in enumerate(chunks):
        for n, g in enumerate(groups):
            upward = aheads[n] + bu_ref[:, at]
            if c + 1 < len(chunks):
                aheads[n] = dot(lows[n], wu[:, chunks[c + 1]])
            activated, slope = gelu_and_slope(upward)
            activated = activated.astype(BF16)
            act_ref[g, at] = activated
            slope_s[g, at] = slope.astype(BF16)
            if c == n == 0:

                @pl.when(step == 0)
                def _():
                    for copy in d_copies:
                        copy.wait()

            seconds[n] = seconds[n] + dot(activated, wd[at, :])
    sums = [0.0] * 6
    twos, grads = [], []
    for n, g in enumerate(groups):
        normal, scale = normed_of(seconds[n])
        valid = 1.0 - valid_ref[g, sequences : sequences + 1].astype(F32)
        out_ref[g, :] = (valid * (normal * vec(4) + vec(5))).astype(BF16)
        grad = og_ref[g, :].astype(F32) * valid
        grad_second = norm_back(grad, vec(4), normal, scale)
        grad_two = grad_second.astype(BF16)
        gtwo_ref[g, :] = grad_two
        sums[4] += total(grad * normal)
        sums[5] += total(grad)
        sums[3] += total(grad_two.astype(F32))
        twos.append(grad_two)
        grads.append(grad_second)
    aheads = [dot_right(two, wd[chunks[0], :]) for two in twos]
    for c, at in enumerate(chunks):
        for n, g in enumerate(groups):
            now = aheads[n]
            if c + 1 < len(chunks):
                aheads[n] = dot_right(twos[n], wd[chunks[c + 1], :])
            grad_up = (now * slope_s[g, at].astype(F32)).astype(BF16)
            gup_ref[g, at] = grad_up
            upsum_ref[:, at] += total(grad_up.astype(F32))
            grads[n] = grads[n] + dot_right(grad_up, wu[:, at])
    for n, g in enumerate(groups):
        normal, scale = ones[n]
        sums[1] += total(grads[n] * normal)
        sums[2] += total(grads[n])
        grad_one = norm_back(grads[n], vec(1), normal, scale).astype(BF16)
        gone_ref[g, :] = grad_one
        sums[0] += total(grad_one.astype(F32))
        gm_s[g, :] = dot_right(grad_one, wo[...]).astype(BF16)
    for i in range(6):
        sums_ref[i : i + 1, :] += sums[i]
    gm_mine_ref[...] = gm_s[:, mine]
    gm_theirs_ref[...] = gm_s[:, theirs]


def middle(place, table, other, down_table, other_down, x, mine, theirs, out_grad, valid, weights, vectors, up_bias):
    count, width = x.shape
    half = width // 2
    hidden = up_bias.shape[1]
    blocks = table.shape[0]
    row = lambda a: pl.BlockSpec((MIDDLE, a.shape[1]), lambda i, *_: (i, 0))
    rows_of = lambda n: pl.BlockSpec((MIDDLE, n), lambda i, *_: (i, 0))
    whole = lambda a: pl.BlockSpec(a.shape, lambda i, *_: (0, 0))
    anywhere = pl.BlockSpec(memory_space=pl.ANY)
    shape = lambda n: jax.ShapeDtypeStruct((count, n), BF16)
    sums, upsum = jax.ShapeDtypeStruct((8, width), F32), jax.ShapeDtypeStruct((1, hidden), F32)
    return pl.pallas_call(
        partial(middle_kernel, tuple(map(len, weights))),
        out_shape=(shape(width), shape(width), shape(hidden), shape(width), shape(hidden), shape(width), shape(half), shape(half), shape(width), sums, upsum),
        grid_spec=pltpu.PrefetchScalarGridSpec(
            num_scalar_prefetch=5,
            grid=(count // MIDDLE,),
            in_specs=[row(x), row(mine), row(theirs), row(out_grad), row(valid), whole(vectors), whole(up_bias)] + [anywhere] * sum(map(len, weights)),
            out_specs=[rows_of(width), rows_of(width), rows_of(hidden), rows_of(width), rows_of(hidden), rows_of(width), rows_of(half), rows_of(half), rows_of(width), whole(sums), whole(upsum)],
            scratch_shapes=[
                pltpu.VMEM((width, width), BF16), pltpu.VMEM((width, hidden), BF16), pltpu.VMEM((hidden, width), BF16),
                pltpu.VMEM((MIDDLE, width), BF16), pltpu.VMEM((MIDDLE, hidden), BF16), pltpu.VMEM((MIDDLE, width), BF16),
            ] + [pltpu.SemaphoreType.DMA((2 * blocks,))] * 3,
        ),
        compiler_params=pltpu.CompilerParams(vmem_limit_bytes=VMEM_LIMIT),
        cost_estimate=pl.CostEstimate(flops=10**11, bytes_accessed=1000, transcendentals=0),
        name="middle",
    )(place, table, other, down_table, other_down, x, mine, theirs, out_grad, valid, vectors, up_bias, *(w for group in weights for w in group))


def outer_kernel(split, extra, place_ref, table_ref, other_ref, left_ref, right_ref, *refs):
    slots_ref, (mine_ref, theirs_ref, total_s, sem, slot_sem) = (refs[0] if extra else None), refs[-5:]
    step = pl.program_id(0)
    steps = pl.num_programs(0)
    blocks, block_rows, width = mine_ref.shape
    width -= 128 * extra
    columns = 2 * width

    def slot_copies():
        return [
            pltpu.make_async_copy(slots_ref.at[order[i]], target.at[i, :, pl.ds(width, 128)], slot_sem.at[n * blocks + i])
            for n, (order, target) in enumerate(((table_ref, mine_ref), (other_ref, theirs_ref)))
            for i in range(blocks)
        ]

    if extra:

        @pl.when(step == 0)
        def _():
            for c in slot_copies():
                c.start()

    product = dot_rows(left_ref[...], right_ref[...]).astype(BF16)
    if split:
        total_s[:, pl.ds(pl.multiple_of(step * product.shape[1], 128), product.shape[1])] = product
    else:
        total_s[pl.ds(pl.multiple_of(step * product.shape[0], 256), product.shape[0]), :] = product

    def copies(first, count):
        made = []
        for n, (order, target) in enumerate(((other_ref, theirs_ref), (table_ref, mine_ref))):
            side = 1 - place_ref[0] if n == 0 else place_ref[0]
            for i in range(blocks):
                at = pl.ds(pl.multiple_of(order[i] * block_rows, math.gcd(block_rows, 256)), block_rows)
                source = total_s.at[at, pl.ds(pl.multiple_of(side * width + first, 128), count)]
                made.append(pltpu.make_async_copy(source, target.at[i, :, pl.ds(first, count)], sem.at[n * blocks + i]))
        return made

    @pl.when(step == steps - 1)
    def _():
        for c in copies(0, width):
            c.start()
        for c in copies(0, width):
            c.wait()
        if extra:
            for c in slot_copies():
                c.wait()


def outer(place, table, other, left, right, split, slots=()):
    count, rows = left.shape
    columns = right.shape[1]
    blocks = table.shape[0]
    extra = len(slots)
    shape = jax.ShapeDtypeStruct((blocks, rows // blocks, columns // 2 + 128 * extra), BF16)
    anywhere = pl.BlockSpec(memory_space=pl.ANY)
    if split:
        steps = max(1, columns // 768)
        specs = [pl.BlockSpec((count, rows), lambda i, *_: (0, 0)), pl.BlockSpec((count, columns // steps), lambda i, *_: (0, i))]
    else:
        steps = max(1, rows // 768)
        specs = [pl.BlockSpec((count, rows // steps), lambda i, *_: (0, i)), pl.BlockSpec((count, columns), lambda i, *_: (0, 0))]
    return pl.pallas_call(
        partial(outer_kernel, split, extra),
        out_shape=(shape, shape),
        grid_spec=pltpu.PrefetchScalarGridSpec(
            num_scalar_prefetch=3,
            grid=(steps,),
            in_specs=specs + [pl.BlockSpec(s.shape, lambda i, *_: (0, 0, 0)) for s in slots],
            out_specs=[anywhere, anywhere],
            scratch_shapes=[pltpu.VMEM((rows, columns), BF16), pltpu.SemaphoreType.DMA((2 * blocks,)), pltpu.SemaphoreType.DMA((2 * blocks,))],
        ),
        compiler_params=pltpu.CompilerParams(vmem_limit_bytes=VMEM_LIMIT),
        cost_estimate=pl.CostEstimate(flops=10**11, bytes_accessed=1000, transcendentals=0),
        name="outer",
    )(place, table, other, left, right, *slots)


def qkv_grad_kernel(slotted, place_ref, table_ref, own_ref, other_ref, d_ref, dother_ref, out_ref, sums_ref, total_s, sums_s, slots_s, sem, slot_sem):
    step = pl.program_id(0)
    product = (dot_rows(own_ref[...], d_ref[...]) + dot_rows(other_ref[...], dother_ref[...])).astype(BF16)
    ones = jnp.ones((8, own_ref.shape[0]), BF16)
    sums_s[step] = dot(ones, d_ref[...]) + dot(ones, dother_ref[...])
    columns = product.shape[1]
    total_s[:, pl.ds(pl.multiple_of(step * columns, 128), columns)] = product

    @pl.when(step == pl.num_programs(0) - 1)
    def _():
        blocks, rows, _ = out_ref.shape
        copies = []
        for i in range(blocks):
            at = pl.ds(pl.multiple_of(table_ref[i] * rows, math.gcd(rows, 256)), rows)
            copies.append(pltpu.make_async_copy(total_s.at[at], out_ref.at[i, :, pl.ds(0, total_s.shape[1])], sem.at[i]))
        for c in copies:
            c.start()
        sums_ref[...] = sums_s[...]
        if slotted:
            slots_s[...] = jnp.zeros_like(slots_s)
            for n in range(blocks // 2):
                values = [sums_s[j, :1, n * rows : n * rows + rows] for j in range(3)]
                slots_s[place_ref[0] * (blocks // 2) + n, :3, :rows] = jnp.concatenate(values, axis=0).astype(BF16)
            slots = [
                pltpu.make_async_copy(slots_s.at[table_ref[i]], out_ref.at[i, :, pl.ds(total_s.shape[1], 128)], slot_sem.at[i])
                for i in range(blocks)
            ]
            for c in slots:
                c.start()
            copies = copies + slots
        for c in copies:
            c.wait()


def qkv_grad(place, table, own, other, grad_own, grad_other, slotted):
    count, rows = own.shape
    columns = grad_own.shape[1]
    half = columns // 3
    blocks = table.shape[0]
    whole = pl.BlockSpec((count, rows), lambda i, *_: (0, 0))
    tile = pl.BlockSpec((count, half), lambda i, *_: (0, i))
    return pl.pallas_call(
        partial(qkv_grad_kernel, slotted),
        out_shape=(
            jax.ShapeDtypeStruct((blocks, rows // blocks, columns + 128 * slotted), BF16),
            jax.ShapeDtypeStruct((3, 8, half), F32),
        ),
        grid_spec=pltpu.PrefetchScalarGridSpec(
            num_scalar_prefetch=2,
            grid=(3,),
            in_specs=[whole, whole, tile, tile],
            out_specs=[pl.BlockSpec(memory_space=pl.ANY), pl.BlockSpec((3, 8, half), lambda i, *_: (0, 0, 0))],
            scratch_shapes=[
                pltpu.VMEM((rows, columns), BF16), pltpu.VMEM((3, 8, half), F32),
                pltpu.VMEM((blocks, rows // blocks, 128) if slotted else (1, 16, 128), BF16),
                pltpu.SemaphoreType.DMA((blocks,)), pltpu.SemaphoreType.DMA((blocks,)),
            ],
        ),
        compiler_params=pltpu.CompilerParams(vmem_limit_bytes=VMEM_LIMIT),
        cost_estimate=pl.CostEstimate(flops=10**11, bytes_accessed=1000, transcendentals=0),
        name="qkv_grad",
    )(place, table, own, other, grad_own, grad_other)


def finish_kernel(place_ref, own_ref, other_ref, *outs):
    half = outs[0].shape[1] // 2
    mine = pl.ds(pl.multiple_of(place_ref[0] * half, 128), half)
    theirs = pl.ds(pl.multiple_of((1 - place_ref[0]) * half, 128), half)
    for n, out in enumerate(outs[:3]):
        at = slice(n * half, n * half + half)
        out[:, mine] = own_ref[:, at].astype(F32)
        out[:, theirs] = other_ref[:, at].astype(F32)
    outs[3][...] = own_ref[:, 3 * half :].astype(F32) + other_ref[:, 3 * half :].astype(F32)


def finish(place, own, other):
    rows, columns = own.shape
    shape = jax.ShapeDtypeStruct((rows, (columns - 128) // 3 * 2), F32)
    whole = lambda s: pl.BlockSpec(s.shape, lambda i, *_: (0, 0))
    small = jax.ShapeDtypeStruct((rows, 128), F32)
    return pl.pallas_call(
        finish_kernel,
        out_shape=(shape, shape, shape, small),
        grid_spec=pltpu.PrefetchScalarGridSpec(
            num_scalar_prefetch=1,
            grid=(1,),
            in_specs=[whole(own), whole(other)],
            out_specs=[whole(shape)] * 3 + [whole(small)],
        ),
        name="finish",
    )(place, own, other)


def input_kernel(added, table_ref, grad_ref, *refs):
    added_refs, w_refs, (out_ref, w_s, sem) = refs[:added], refs[added:-3], refs[-3:]

    @pl.when(pl.program_id(0) == 0)
    def _():
        for c in load_rows(table_ref, w_refs, w_s, sem):
            c.wait()

    total = dot_right(grad_ref[...], w_s[...])
    for ref in added_refs:
        total = total + ref[...].astype(F32)
    out_ref[...] = total.astype(BF16)


def input_part(table, grad, weights, width, *added):
    count, columns = grad.shape
    blocks = table.shape[0]
    row = lambda n: pl.BlockSpec((BLOCK, n), lambda i, *_: (i, 0))
    return pl.pallas_call(
        partial(input_kernel, len(added)),
        out_shape=jax.ShapeDtypeStruct((count, width), BF16),
        grid_spec=pltpu.PrefetchScalarGridSpec(
            num_scalar_prefetch=1,
            grid=(count // BLOCK,),
            in_specs=[row(columns)] + [row(width)] * len(added) + [pl.BlockSpec(memory_space=pl.ANY)] * len(weights),
            out_specs=row(width),
            scratch_shapes=[pltpu.VMEM((width, columns), BF16), pltpu.SemaphoreType.DMA((blocks,))],
        ),
        compiler_params=pltpu.CompilerParams(vmem_limit_bytes=VMEM_LIMIT),
        cost_estimate=pl.CostEstimate(flops=10**11, bytes_accessed=1000, transcendentals=0),
        name="input_part",
    )(table, grad, *added, *weights)


def copy_block(table_ref, source_ref, target_ref):
    target_ref[...] = source_ref[...]


def picked(blocks, table):
    block = (1, *blocks.shape[1:])
    return pl.pallas_call(
        copy_block,
        out_shape=jax.ShapeDtypeStruct(blocks.shape, blocks.dtype),
        grid_spec=pltpu.PrefetchScalarGridSpec(
            num_scalar_prefetch=1,
            grid=(blocks.shape[0],),
            in_specs=[pl.BlockSpec(block, lambda i, t: (t[i], 0, 0))],
            out_specs=pl.BlockSpec(block, lambda i, t: (i, 0, 0)),
        ),
        name="picked",
    )(table, blocks)


def sides(count):
    side = math.isqrt(count // 4)
    if count % 4 == 0 and 4 * side * side == count:
        return (4, side, side)
    return (count, 1, 1)


def hop(value, leg, step, shape):
    deep, tall, wide = shape
    count = deep * tall * wide
    pairs = []
    for core in range(2):
        for here in range(count):
            z, y, x = here // (tall * wide), here // wide % tall, here % wide
            if leg == 0:
                z = (z + step) % deep
            elif (leg == 1) == (core == 0):
                y = (y + step) % tall
            else:
                x = (x + step) % wide
            there = (z * tall + y) * wide + x
            pairs.append((core * count + there, core * count + here))
    return lax.ppermute(value, ("dp", "fsdp"), pairs)


def swapped(value):
    return lax.ppermute(value, "dp", [(0, 1), (1, 0)])


def received(blocks, leg, shape):
    return [hop(blocks, leg, s, shape) for s in range(1, shape[leg])]


def sent(total, leg, shape):
    pieces = total.reshape(shape[leg], -1, *total.shape[1:])
    return [pieces[0]] + [hop(pieces[s], leg, shape[leg] - s, shape) for s in range(1, shape[leg])]


def summed(values):
    return sum(v.astype(F32) for v in values).astype(BF16)


def staged(*values):
    return lax.optimization_barrier(values)


def join(pieces):
    return jnp.concatenate(pieces, axis=0)


def order(core, shape, legs=(0, 1, 2)):
    deep, tall, wide = shape
    here = lax.axis_index("fsdp")
    z, y, x = here // (tall * wide), here // wide % tall, here % wide
    slot = jnp.arange(deep * tall * wide, dtype=jnp.int32)
    steps = {}
    for leg in legs:
        steps[leg] = slot % shape[leg]
        slot = slot // shape[leg]
    z = (z + steps[0]) % deep
    y = (y + jnp.where(core == 0, steps[1], steps[2])) % tall
    x = (x + jnp.where(core == 0, steps[2], steps[1])) % wide
    return (z * tall + y) * wide + x


def inverse(table):
    slots = jnp.arange(table.shape[0], dtype=jnp.int32)
    return jnp.sum(jnp.where(table[None, :] == slots[:, None], slots[None, :], 0), axis=1)


def half_of(array, side):
    width = array.shape[1] // 2
    return lax.dynamic_slice_in_dim(array, side * width, width, 1)


def joined(mine, theirs, core):
    first = jnp.where(core == 0, mine, theirs)
    second = jnp.where(core == 0, theirs, mine)
    return first, second


def reordered(small, table):
    slots = jnp.arange(table.shape[0], dtype=jnp.int32)
    chosen = (table[:, None] == slots[None, :]).astype(F32)
    flat = small.reshape(table.shape[0], -1)
    return jnp.dot(chosen, flat, precision=lax.Precision.HIGHEST).reshape(small.shape)


def shards(
    hidden_in,
    lengths,
    out_grad,
    query_matrix,
    query_offset,
    key_matrix,
    key_offset,
    value_matrix,
    value_offset,
    output_matrix,
    output_offset,
    first_gain,
    first_offset,
    up_matrix,
    up_offset,
    down_matrix,
    down_offset,
    second_gain,
    second_offset,
):
    count, width = hidden_in.shape
    half = width // 2
    rows = query_matrix.shape[0]
    parts = up_offset.shape[0] // rows
    core = lax.axis_index("dp")
    shape = sides(lax.axis_size("fsdp"))
    positions = math.prod(shape)
    table, other_table = order(core, shape), order(1 - core, shape)
    down_legs = (1, 0, 2)
    down_table, other_down_table = order(core, shape, down_legs), order(1 - core, shape, down_legs)
    direct = rows % 16 == 0
    place = jnp.reshape(core, (1,)).astype(jnp.int32)
    zero = jnp.zeros((1,), jnp.int32)
    own_order, their_order = (table, other_table) if direct else (zero, zero)
    own_down_order, their_down_order = (down_table, other_down_table) if direct else (zero, zero)
    down_rows = down_matrix.shape[0]

    def usable(pieces, places, cuts):
        if direct:
            return pieces
        blocks, parts, first = jnp.concatenate(pieces, axis=0), [], 0
        for cut in cuts:
            parts.append(picked(blocks[:, first : first + cut], inverse(places)).reshape(1, -1, blocks.shape[2]))
            first += cut
        return [jnp.concatenate(parts, axis=1)]

    def in_blocks(array, places):
        return array if direct else picked(array.reshape(positions, -1, array.shape[2]), places)

    vectors = (
        query_offset, key_offset, value_offset, output_offset, first_gain, first_offset,
        down_offset, second_gain, second_offset,
    )
    left = jnp.pad(jnp.stack(vectors), ((0, rows - len(vectors)), (0, 64 - rows)))
    right = jnp.pad(up_offset.reshape(parts, rows), ((0, rows - parts), (0, 64 - rows)))
    halves = [half_of(m, core) for m in (query_matrix, key_matrix, value_matrix)]
    unit = jnp.concatenate(halves + [left, right], axis=1)[None]
    attn_far = received(unit, 0, shape)
    other_lengths = swapped(lengths)
    down_unit = jnp.concatenate([half_of(down_matrix, core), half_of(output_matrix, core)], axis=0)[None]
    down_far = received(down_unit, 1, shape)
    other_in = swapped(hidden_in)
    tables, plan, _ = described(lengths[0], count)

    attn_far, up_matrix, other_lengths, down_far = staged(attn_far, up_matrix, other_lengths, down_far)
    attn_four = join([unit] + attn_far)
    attn_far = received(attn_four, 1, shape)
    up_unit = half_of(up_matrix, core)[None]
    up_far = received(up_unit, 0, shape)
    other_tables, other_plan, _ = described(other_lengths[0], count)

    attn_far, attn_four = staged(attn_far, attn_four)
    attn_eight = join([attn_four] + attn_far)
    attn_far = received(attn_eight, 2, shape)
    down_two = join([down_unit] + down_far)

    attn_far, up_far, down_two = staged(attn_far, up_far, down_two)
    attn = [attn_eight] + attn_far
    small = jnp.concatenate([a[:, :, 3 * half :] for a in attn], axis=0).astype(F32)
    small = reordered(small, inverse(table))
    whole = small[:, : len(vectors), :rows].swapaxes(0, 1).reshape(len(vectors), width)
    up_bias = small[:, :parts, 64 : 64 + rows].reshape(1, -1)
    bias = lax.dynamic_slice_in_dim(whole[:3], core * half, half, 1).reshape(1, -1)
    vector_rows = jnp.pad(whole[3:], ((0, 2), (0, 0)))
    attn = usable(attn, table, (rows,))
    up_four = join([up_unit] + up_far)
    up_far = received(up_four, 1, shape)
    down_far = received(down_two, 0, shape)
    other_q, other_k, other_v, other_norms = project(other_in, attn, own_order, bias, other_tables)

    up_far, other_q, hidden_in = staged(up_far, other_q, hidden_in)
    up_eight = join([up_four] + up_far)
    up_far = received(up_eight, 2, shape)
    up_swapped = swapped(up_eight)
    other_mixed, other_lse = attend(other_plan, other_q, other_k, other_v, other_norms, other_tables[2])

    up_swapped, other_mixed, hidden_in = staged(up_swapped, other_mixed, hidden_in)
    mixed_theirs = swapped(other_mixed)
    q, k, v, norms = project(hidden_in, attn, own_order, bias, tables)

    up_far, down_far, mixed_theirs, q = staged(up_far, down_far, mixed_theirs, q)
    down_eight = join([down_two] + down_far)
    down_far = received(down_eight, 2, shape)
    up_swapped = [up_swapped] + [swapped(far) for far in up_far]
    down_swapped = swapped(down_eight)
    mixed, lse = attend(plan, q, k, v, norms, tables[2])

    up_swapped, down_swapped, down_far, mixed, vector_rows, up_bias = staged(
        up_swapped, down_swapped, down_far, mixed, vector_rows, up_bias
    )
    down_swapped = [down_swapped] + [swapped(far) for far in down_far]
    up_weights = [usable([up_eight] + up_far, table, (rows,)), usable(up_swapped, other_table, (rows,))]
    down_weights = [
        usable([down_eight] + down_far, down_table, (down_rows, rows)),
        usable(down_swapped, other_down_table, (down_rows, rows)),
    ]
    (
        hidden_out, normed_low, activated, grad_two, grad_up, grad_one, grad_mine, grad_theirs, both_mixed, sums, up_sum,
    ) = middle(
        place, own_order, their_order, own_down_order, their_down_order, hidden_in, mixed, mixed_theirs, out_grad, tables[2],
        up_weights + down_weights, vector_rows, up_bias,
    )
    other_grad = swapped(grad_theirs)
    places, down_places = (place, own_order, their_order), (place, own_down_order, their_down_order)
    slots_of = lambda vectors: vectors.reshape(-1, positions, rows).swapaxes(0, 1)
    left = jnp.pad(slots_of(sums[:6]), ((0, 0), (0, rows - 6), (0, 64 - rows)))
    right = jnp.pad(up_sum.reshape(positions, parts, rows), ((0, 0), (0, rows - parts), (0, 64 - rows)))
    slot_sums = jnp.concatenate([left, right], axis=2)

    def with_slots(pair, slots):
        if direct:
            return pair
        return [
            jnp.concatenate([in_blocks(p, t), reordered(slots, t).astype(BF16)], axis=2)
            for p, t in zip(pair, (table, other_table))
        ]


    down_pair = outer(*down_places, activated, grad_two, 0)

    down_pair, other_grad, grad_up = staged(down_pair, other_grad, grad_up)
    down_arrived = swapped(in_blocks(down_pair[1], other_down_table))
    up_pair = outer(*places, normed_low, grad_up, 1)

    up_pair, down_arrived, both_mixed = staged(up_pair, down_arrived, both_mixed)
    down_sent = sent(summed([in_blocks(down_pair[0], down_table), down_arrived]), 2, shape)
    up_arrived = swapped(in_blocks(up_pair[1], other_table))
    output_pair = outer(*places, both_mixed, grad_one, 1, (slot_sums.astype(BF16),) if direct else ())
    output_pair = with_slots(output_pair, slot_sums)

    output_pair, up_arrived, other_grad = staged(output_pair, up_arrived, other_grad)
    output_arrived = swapped(output_pair[1])
    up_total = summed([in_blocks(up_pair[0], table), up_arrived])
    output_mine = output_pair[0]
    other_grad, up_total = staged(other_grad, up_total)
    other_d = attend_back(other_plan, other_q, other_k, other_v, other_lse, other_mixed, other_grad, other_tables)

    output_arrived, down_sent, other_d, grad_mine = staged(output_arrived, down_sent, other_d, grad_mine)
    up_sent = sent(jnp.concatenate([up_total, summed([output_mine, output_arrived])], axis=2), 2, shape)
    down_sent = sent(summed(down_sent), 0, shape)
    own_d = attend_back(plan, q, k, v, lse, mixed, grad_mine, tables)

    up_sent, down_sent, own_d = staged(up_sent, down_sent, own_d)
    up_sent = sent(summed(up_sent), 1, shape)
    down_sent = sent(summed(down_sent), 1, shape)
    matrices, qkv_sums = qkv_grad(place, own_order, hidden_in, other_in, own_d, other_d, direct)

    up_sent, down_sent, matrices, other_d = staged(up_sent, down_sent, matrices, other_d)
    if not direct:
        own_sums = jnp.zeros((3, width), F32)
        own_sums = lax.dynamic_update_slice_in_dim(own_sums, qkv_sums[:, 0], core * half, 1)
        own_sums = jnp.pad(slots_of(own_sums), ((0, 0), (0, rows - 3), (0, 128 - rows)))
        matrices = jnp.concatenate([in_blocks(matrices, table), reordered(own_sums, table).astype(BF16)], axis=2)
    matrices_sent = sent(matrices, 2, shape)
    up_sent = sent(summed(up_sent), 0, shape)
    down_done = summed(down_sent)[0]
    down_other = swapped(down_done)
    sent_grad = input_part(own_order, other_d, attn, width)

    matrices_sent, up_sent, down_other, sent_grad = staged(matrices_sent, up_sent, down_other, sent_grad)
    matrices_sent = sent(summed(matrices_sent), 1, shape)
    up_done = summed(up_sent)[0]
    up_other = swapped(up_done)
    other_part = swapped(sent_grad)

    matrices_sent, up_other, other_part, own_d = staged(matrices_sent, up_other, other_part, own_d)
    matrices_sent = sent(summed(matrices_sent), 0, shape)
    input_grad = input_part(own_order, own_d, attn, width, other_part, grad_one)

    matrices_sent, input_grad = staged(matrices_sent, input_grad)
    matrices_done = summed(matrices_sent)[0]

    up_first, up_second = joined(up_done, up_other, core)
    down_first, down_second = joined(down_done, down_other, core)
    query_grad, key_grad, value_grad, offsets = finish(place, matrices_done, swapped(matrices_done))
    wide = lambda a, b: jnp.concatenate([a, b], axis=1).astype(F32)
    hidden = up_matrix.shape[1] // 2
    others = up_first[:, hidden + half :].astype(F32)
    columns = slice(hidden, hidden + half)
    return (
        hidden_out,
        input_grad,
        query_grad,
        offsets[0, :rows],
        key_grad,
        offsets[1, :rows],
        value_grad,
        offsets[2, :rows],
        wide(up_first[:, columns], up_second[:, columns]),
        others[0, :rows],
        others[1, :rows],
        others[2, :rows],
        wide(up_first[:, :hidden], up_second[:, :hidden]),
        others[:parts, 64 : 64 + rows].reshape(-1),
        wide(down_first, down_second),
        others[3, :rows],
        others[4, :rows],
        others[5, :rows],
    )


def solution(mesh):
    placed = (
        P(("dp", "fsdp"), None),
        P(("dp", "fsdp"), None),
        P(("dp", "fsdp"), None),
        P("fsdp", None),
        P("fsdp"),
        P("fsdp", None),
        P("fsdp"),
        P("fsdp", None),
        P("fsdp"),
        P("fsdp", None),
        P("fsdp"),
        P("fsdp"),
        P("fsdp"),
        P("fsdp", None),
        P("fsdp"),
        P("fsdp", None),
        P("fsdp"),
        P("fsdp"),
        P("fsdp"),
    )
    return jax.shard_map(
        shards,
        mesh=mesh,
        in_specs=placed,
        out_specs=(
            P(("dp", "fsdp"), None),
            P(("dp", "fsdp"), None),
            P("fsdp", None),
            P("fsdp"),
            P("fsdp", None),
            P("fsdp"),
            P("fsdp", None),
            P("fsdp"),
            P("fsdp", None),
            P("fsdp"),
            P("fsdp"),
            P("fsdp"),
            P("fsdp", None),
            P("fsdp"),
            P("fsdp", None),
            P("fsdp"),
            P("fsdp"),
            P("fsdp"),
        ),
        check_vma=False,
    )
```

```python
import math
from functools import partial
import jax, jax.numpy as jnp
from jax import lax
from jax.experimental import pallas as pl
from jax.experimental.pallas import tpu as pltpu
from jax.sharding import PartitionSpec as P

HEAD_DIM = 64
EPSILON = 1e-12
FAR = -1e30
LOG2E = 1.4426950408889634
BLOCK = 256
SAFE = 105.0
F32 = jnp.float32
BF16 = jnp.bfloat16
VMEM_LIMIT = 58 * 2**20


def dot(a, b):
    return jnp.dot(a, b, preferred_element_type=F32)


def dot_right(a, b):
    return lax.dot_general(a, b, (((1,), (1,)), ((), ())), preferred_element_type=F32)


def dot_rows(a, b):
    return lax.dot_general(a, b, (((0,), (0,)), ((), ())), preferred_element_type=F32)


def turned(value, cosines, sines, even_lane):
    partner = jnp.where(even_lane, -pltpu.roll(value, 127, 1), pltpu.roll(value, 1, 1))
    return value * cosines + partner * sines


def lse_lane(head):
    return (HEAD_DIM if head % 2 == 0 else 0) + 8 + 3 * head


def delta_lane(head, heads):
    return lse_lane(head) + 3 * heads


def lanes_of(rows):
    return lax.broadcasted_iota(jnp.int32, (rows, 128), 1)


def load_rows(table_ref, source_refs, target_ref, sem):
    copies = []
    for source in source_refs:
        rows = source.shape[1]
        for i in range(source.shape[0]):
            n = len(copies)
            at = pl.ds(pl.multiple_of(table_ref[n] * rows, math.gcd(rows, 256)), rows)
            copies.append(pltpu.make_async_copy(source.at[i, :, pl.ds(0, target_ref.shape[1])], target_ref.at[at], sem.at[n]))
    for c in copies:
        c.start()
    return copies


def project_kernel(table_ref, x_ref, bias_ref, cos_ref, sin_ref, extq_ref, extk_ref, *refs):
    *w_refs, q_ref, k_ref, v_ref, norm_ref, w_s, sem = refs
    step = pl.program_id(0)

    @pl.when(step == 0)
    def _():
        for c in load_rows(table_ref, w_refs, w_s, sem):
            c.wait()
        norm_ref[...] = jnp.zeros_like(norm_ref)

    heads = q_ref.shape[0]
    width = heads * HEAD_DIM
    lane = lanes_of(BLOCK)
    first_half = lane < HEAD_DIM
    even_lane = lax.rem(lane, 2) == 0
    y = dot(x_ref[...], w_s[...]) + bias_ref[...]
    cosines, sines = cos_ref[...], sin_ref[...]
    extq, extk = extq_ref[...].astype(F32), extk_ref[...].astype(F32)
    row = lax.broadcasted_iota(jnp.int32, (128, BLOCK), 0)
    squares = []
    for p in range(width // 128):
        at = slice(p * 128, p * 128 + 128)
        q = turned(y[:, at], cosines, sines, even_lane) * (HEAD_DIM**-0.5 * LOG2E)
        k = turned(y[:, width + p * 128 : width + p * 128 + 128], cosines, sines, even_lane)
        v = y[:, 2 * width + p * 128 : 2 * width + p * 128 + 128].T
        squares.append(((q * q).astype(BF16), (k * k).astype(BF16)))
        for h in (2 * p, 2 * p + 1):
            own = first_half if h % 2 == 0 else jnp.logical_not(first_half)
            start = lse_lane(h)
            ones = (lane >= start) & (lane < start + 3)
            q_ref[h] = jnp.where(own, q, extq).astype(BF16)
            k_ref[h] = jnp.where(own, k, jnp.where(ones, 1.0, extk)).astype(BF16)
            start = delta_lane(h, heads)
            ones = (row >= start) & (row < start + 3)
            own = row < HEAD_DIM if h % 2 == 0 else row >= HEAD_DIM
            v_ref[h] = jnp.where(own, v, jnp.where(ones, 1.0, 0.0)).astype(BF16)
    column = lax.broadcasted_iota(jnp.int32, (width, 128), 0) // HEAD_DIM
    picks = jnp.where(column == lax.broadcasted_iota(jnp.int32, (width, 128), 1), 1.0, 0.0).astype(BF16)
    sums = [dot(jnp.concatenate([a[n] for a in squares], axis=1), picks) for n in range(2)]
    most = [jnp.max(t, axis=0, keepdims=True) for t in sums]
    norm_ref[...] = jnp.maximum(norm_ref[...], jnp.concatenate(most, axis=1))


def project(x, weights, table, bias, tables):
    count, width = x.shape
    blocks = table.shape[0]
    total = bias.shape[1]
    heads = total // (3 * HEAD_DIM)
    cosines, sines, extq, extk = tables
    row = lambda a: pl.BlockSpec((BLOCK, a.shape[1]), lambda i, t: (i, 0))
    head = pl.BlockSpec((heads, BLOCK, 128), lambda i, t: (0, i, 0))
    shape = jax.ShapeDtypeStruct((heads, count, 128), BF16)
    return pl.pallas_call(
        project_kernel,
        out_shape=(shape, shape, jax.ShapeDtypeStruct((heads, 128, count), BF16), jax.ShapeDtypeStruct((8, 256), F32)),
        grid_spec=pltpu.PrefetchScalarGridSpec(
            num_scalar_prefetch=1,
            grid=(count // BLOCK,),
            in_specs=[
                row(x), pl.BlockSpec((1, total), lambda i, t: (0, 0)), row(cosines), row(sines), row(extq), row(extk),
            ]
            + [pl.BlockSpec(memory_space=pl.ANY)] * len(weights),
            out_specs=[head, head, pl.BlockSpec((heads, 128, BLOCK), lambda i, t: (0, 0, i)), pl.BlockSpec((8, 256), lambda i, t: (0, 0))],
            scratch_shapes=[pltpu.VMEM((width, total), BF16), pltpu.SemaphoreType.DMA((blocks,))],
        ),
        compiler_params=pltpu.CompilerParams(vmem_limit_bytes=VMEM_LIMIT),
        cost_estimate=pl.CostEstimate(flops=10**11, bytes_accessed=1000, transcendentals=0),
        name="project",
    )(table, x, bias, cosines, sines, extq, extk, *weights)


def three_parts(value):
    high = value.astype(BF16).astype(F32)
    rest = value - high
    middle = rest.astype(BF16).astype(F32)
    return high, middle, rest - middle


def attend_kernel(plan_ref, q_ref, k_ref, v_ref, norm_ref, extq_ref, mixed_ref, lse_ref):
    step = pl.program_id(0)
    heads, count, _ = k_ref.shape
    blocks = count // BLOCK
    first, need = plan_ref[2 * step], plan_ref[2 * step + 1]
    safe = jnp.max(norm_ref[:, :128]) * jnp.max(norm_ref[:, 128:]) < SAFE * SAFE
    lane = lanes_of(BLOCK)
    start_lane, any_lane = lane < 0, lane < 0
    for h in range(heads):
        start_lane = start_lane | (lane == lse_lane(h))
        any_lane = any_lane | ((lane >= lse_lane(h)) & (lane < lse_lane(h) + 3))
    pad = extq_ref[:, HEAD_DIM + 4 : HEAD_DIM + 5].astype(F32) > 0.5

    def rows_of(c, plain):
        keys = pl.ds(pl.multiple_of(jnp.minimum(first, blocks - c) * BLOCK, BLOCK), c * BLOCK)
        scores = [dot_right(k_ref[h, keys, :], q_ref[h]) for h in range(heads)]
        outs = []
        packs = [jnp.zeros((24, BLOCK), F32)] * 2
        row = lax.broadcasted_iota(jnp.int32, (24, BLOCK), 0)
        for h in range(heads):
            s = scores[h]
            if not plain:
                peak = jnp.max(s, axis=0, keepdims=True)
                s = s - peak
            o = dot(v_ref[h, :, keys], jnp.exp2(s).astype(BF16))
            ones = delta_lane(h, heads)
            total = o[ones : ones + 1, :]
            outs.append((o[:HEAD_DIM] if h % 2 == 0 else o[HEAD_DIM:]) / total)
            lse = -jnp.log2(total)
            if not plain:
                lse = lse - peak
            for j, part in enumerate(three_parts(lse)):
                packs[h % 2] = jnp.where(row == 3 * h + j, part, packs[h % 2])
        mixed_ref[...] = jnp.concatenate(outs, axis=0).T.astype(BF16)
        gap = lambda n: jnp.zeros((n, BLOCK), F32)
        packed = jnp.concatenate([gap(8), packs[1], gap(40), packs[0], gap(32)], axis=0).T
        lse_ref[...] = jnp.where(pad & any_lane, jnp.where(start_lane, FAR, 0.0), packed).astype(BF16)

    @pl.when(need == 0)
    def _():
        mixed_ref[...] = jnp.zeros_like(mixed_ref)
        lse_ref[...] = jnp.where(start_lane, FAR, 0.0).astype(BF16)

    for c in range(1, blocks + 1):
        pl.when(safe & (need == c))(partial(rows_of, c, True))
    pl.when(jnp.logical_not(safe) & (need > 0))(partial(rows_of, blocks, False))


def attend(plan, q, k, v, norms, extq):
    heads, count, _ = q.shape
    whole = lambda a: pl.BlockSpec(a.shape, lambda i, p: (0,) * a.ndim)
    return pl.pallas_call(
        attend_kernel,
        out_shape=(jax.ShapeDtypeStruct((count, heads * HEAD_DIM), BF16), jax.ShapeDtypeStruct((count, 128), BF16)),
        grid_spec=pltpu.PrefetchScalarGridSpec(
            num_scalar_prefetch=1,
            grid=(count // BLOCK,),
            in_specs=[
                pl.BlockSpec((heads, BLOCK, 128), lambda i, p: (0, i, 0)), whole(k), whole(v), whole(norms),
                pl.BlockSpec((BLOCK, 128), lambda i, p: (i, 0)),
            ],
            out_specs=[pl.BlockSpec((BLOCK, heads * HEAD_DIM), lambda i, p: (i, 0)), pl.BlockSpec((BLOCK, 128), lambda i, p: (i, 0))],
        ),
        compiler_params=pltpu.CompilerParams(vmem_limit_bytes=VMEM_LIMIT),
        cost_estimate=pl.CostEstimate(flops=10**11, bytes_accessed=1000, transcendentals=0),
        name="attend",
    )(plan, q, k, v, norms, extq)


def attend_back_kernel(plan_ref, q_ref, k_ref, v_ref, lse_ref, mixed_ref, grad_ref, cos_ref, sin_ref, cos_all, sin_all,
                       d_ref, dk_s, dv_s):
    step = pl.program_id(0)
    heads, count, _ = k_ref.shape
    width = heads * HEAD_DIM
    blocks = count // BLOCK
    first, need = plan_ref[2 * step], plan_ref[2 * step + 1]
    lane = lanes_of(BLOCK)
    first_half = lane < HEAD_DIM
    even_lane = lax.rem(lane, 2) == 0
    scale = HEAD_DIM**-0.5

    @pl.when(step == 0)
    def _():
        dk_s[...] = jnp.zeros_like(dk_s)
        dv_s[...] = jnp.zeros_like(dv_s)

    def rows_of(c):
        keys = pl.ds(pl.multiple_of(jnp.minimum(first, blocks - c) * BLOCK, BLOCK), c * BLOCK)
        grad = grad_ref[...].astype(F32)
        product = grad * mixed_ref[...].astype(F32)
        high = product.astype(BF16)
        low = (product - high.astype(F32)).astype(BF16)
        column = lax.broadcasted_iota(jnp.int32, (width, 128), 0) // HEAD_DIM
        slot = lax.broadcasted_iota(jnp.int32, (width, 128), 1)
        slot = slot - jnp.where(lax.rem(column, 2) == 0, delta_lane(0, heads), delta_lane(0, heads) - HEAD_DIM)
        picks = jnp.where((slot >= 3 * column) & (slot < 3 * column + 3), 1.0, 0.0).astype(BF16)
        delta = three_parts(-(dot(high, picks) + dot(low, picks)))
        inner = jnp.where(first_half, lane, lane - HEAD_DIM)
        part = lax.rem(inner + 1, 3)
        delta = jnp.where(part == 0, delta[0], jnp.where(part == 1, delta[1], delta[2]))
        extra = jnp.where(inner < 8 + 3 * heads, lse_ref[...].astype(F32), delta)
        dqs = []
        for p in range(width // 128):
            at = slice(p * 128, p * 128 + 128)
            pair = grad[:, at]
            pair_t = pair.T.astype(BF16)
            qs = [q_ref[2 * p].astype(F32), q_ref[2 * p + 1].astype(F32)]
            q_t = jnp.where(first_half, qs[0], qs[1]).T.astype(BF16)
            both = []
            for n in range(2):
                h = 2 * p + n
                own = first_half if n == 0 else jnp.logical_not(first_half)
                side = slice(n * HEAD_DIM, n * HEAD_DIM + HEAD_DIM)
                g = jnp.where(own, pair, extra).astype(BF16)
                q = jnp.where(own | (inner < 8), qs[n], extra).astype(BF16)
                k = k_ref[h, keys, :]
                probs = jnp.exp2(dot_right(q, k))
                shifted = dot(g, v_ref[h, :, keys])
                grads = (probs * shifted).astype(BF16)
                dv_s[h, :, keys] += dot(pair_t[side], probs.astype(BF16))
                dk_s[h, :, keys] += dot(q_t[side], grads)
                both.append(dot(grads, k))
            dq = jnp.where(first_half, both[0], both[1]) * scale
            d_ref[pl.ds(pl.multiple_of(step * BLOCK, BLOCK), BLOCK), at] = turned(dq, cos_ref[...], -sin_ref[...], even_lane).astype(BF16)

    @pl.when(need == 0)
    def _():
        d_ref[pl.ds(pl.multiple_of(step * BLOCK, BLOCK), BLOCK), :width] = jnp.zeros((BLOCK, width), BF16)

    for c in range(1, blocks + 1):
        pl.when(need == c)(partial(rows_of, c))

    @pl.when(step == blocks - 1)
    def _():
        for p in range(width // 128):
            for r in range(blocks):
                at = slice(r * BLOCK, r * BLOCK + BLOCK)
                dv = jnp.concatenate([dv_s[2 * p, :, at], dv_s[2 * p + 1, :, at]], axis=0).T
                dk = jnp.concatenate([dk_s[2 * p, :, at], dk_s[2 * p + 1, :, at]], axis=0).T * (1.0 / LOG2E)
                d_ref[at, 2 * width + p * 128 : 2 * width + p * 128 + 128] = dv.astype(BF16)
                d_ref[at, width + p * 128 : width + p * 128 + 128] = turned(dk, cos_all[at, :], -sin_all[at, :], even_lane).astype(BF16)


def attend_back(plan, q, k, v, lse, mixed, grad, tables):
    heads, count, _ = q.shape
    width = heads * HEAD_DIM
    cosines, sines = tables[:2]
    whole = lambda a: pl.BlockSpec(a.shape, lambda i, p: (0,) * a.ndim)
    row = lambda a: pl.BlockSpec((BLOCK, a.shape[1]), lambda i, p: (i, 0))
    shape = jax.ShapeDtypeStruct((count, 3 * width), BF16)
    return pl.pallas_call(
        attend_back_kernel,
        out_shape=shape,
        grid_spec=pltpu.PrefetchScalarGridSpec(
            num_scalar_prefetch=1,
            grid=(count // BLOCK,),
            in_specs=[
                pl.BlockSpec((heads, BLOCK, 128), lambda i, p: (0, i, 0)), whole(k), whole(v), row(lse), row(mixed), row(grad),
                row(cosines), row(sines), whole(cosines), whole(sines),
            ],
            out_specs=pl.BlockSpec((count, 3 * width), lambda i, p: (0, 0)),
            scratch_shapes=[pltpu.VMEM((heads, HEAD_DIM, count), F32)] * 2,
        ),
        compiler_params=pltpu.CompilerParams(vmem_limit_bytes=40 * 2**20),
        cost_estimate=pl.CostEstimate(flops=10**11, bytes_accessed=1000, transcendentals=0),
        name="attend_back",
    )(plan, q, k, v, lse, mixed, grad, cosines, sines, cosines, sines)


def described(lengths, count):
    total = lengths.shape[0]
    index = jnp.arange(total)
    ends = jnp.sum(jnp.where(index[:, None] >= index[None, :], lengths[None, :], 0), axis=1)
    starts = ends - lengths
    slots = jnp.arange(count, dtype=jnp.int32)
    segment = jnp.sum((slots[:, None] >= ends[None, :]).astype(jnp.int32), axis=1)
    owner = segment[:, None] == jnp.arange(total, dtype=jnp.int32)[None, :]
    begin = jnp.sum(jnp.where(owner, starts[None, :], 0), axis=1)
    position = (slots - begin).astype(F32)
    lane = jnp.arange(128, dtype=jnp.int32)
    inverse = jnp.power(10000.0, -2.0 * (lane % HEAD_DIM // 2).astype(F32) / HEAD_DIM)
    angle = position[:, None] * inverse[None, :]
    cosines, sines = jnp.cos(angle), jnp.sin(angle)
    code = (lane % HEAD_DIM)[None, :]
    extq = jnp.where(code == segment[:, None], 1.0, 0.0).astype(BF16)
    extk = jnp.where((code < total) & (code != segment[:, None]), FAR, 0.0).astype(BF16)
    filled = jnp.sum(lengths)
    opens = jnp.arange(count // BLOCK, dtype=jnp.int32) * BLOCK
    closes = jnp.minimum(opens + BLOCK, filled)
    low = jnp.max(jnp.where(ends[None, :] <= opens[:, None], ends[None, :], 0), axis=1)
    high = jnp.min(jnp.where(ends[None, :] >= closes[:, None], ends[None, :], filled), axis=1)
    first = low // BLOCK
    need = jnp.where(opens < filled, (high + BLOCK - 1) // BLOCK - first, 0)
    plan = jnp.stack([first, need], axis=1).reshape(-1)
    valid = (segment < total).astype(F32)
    return (cosines, sines, extq, extk), plan, valid


def normed_of(value):
    center = value - jnp.mean(value, axis=1, keepdims=True)
    scale = lax.rsqrt(jnp.mean(center * center, axis=1, keepdims=True) + EPSILON)
    return center * scale, scale


def norm_back(grad, gain, normed, scale):
    scaled = grad * gain
    return (scaled - jnp.mean(scaled, axis=1, keepdims=True) - normed * jnp.mean(scaled * normed, axis=1, keepdims=True)) * scale


def gelu_and_slope(value):
    bell = jnp.exp2(value * value * (-0.5 * LOG2E))
    t = 1.0 / (1.0 + (0.3275911 * 0.5**0.5) * jnp.abs(value))
    tail = t * (0.5 * 0.254829592 + t * (0.5 * -0.284496736 + t * (0.5 * 1.421413741 + t * (0.5 * -1.453152027 + t * (0.5 * 1.061405429)))))
    tail = tail * bell
    below = jnp.where(value < 0.0, tail, 1.0 - tail)
    return value * below, below + value * bell * (2.0 * math.pi) ** -0.5


CHUNK = 1024
MIDDLE = 512


def place_halves(place_ref, orders, sources, first, rows, target_ref, sem):
    copies = []
    for n, (order, refs) in enumerate(zip(orders, sources)):
        side = place_ref[0] if n == 0 else 1 - place_ref[0]
        blocks = 0
        for ref in refs:
            width = ref.shape[2]
            for i in range(ref.shape[0]):
                at = pl.ds(pl.multiple_of(order[blocks] * rows, math.gcd(rows, 256)), rows)
                columns = pl.ds(pl.multiple_of(side * width, 128), width)
                copies.append(pltpu.make_async_copy(ref.at[i, pl.ds(first, rows)], target_ref.at[at, columns], sem.at[len(copies)]))
                blocks += 1
    return copies


def middle_kernel(counts, place_ref, table_ref, other_ref, down_table_ref, other_down_ref, x_ref, mine_ref, theirs_ref, og_ref, valid_ref, vec_ref, bu_ref, *refs):
    weight_refs, refs = refs[: sum(counts)], refs[sum(counts) :]
    (
        out_ref, low_ref, act_ref, gtwo_ref, gup_ref, gone_ref, gm_mine_ref, gm_theirs_ref, mixed_ref, sums_ref, upsum_ref,
        wo, wu, wd, mixed_s, slope_s, gm_s, so, su, sd,
    ) = refs
    step = pl.program_id(0)
    sequences = 4
    core = place_ref[0]
    half = mine_ref.shape[1]
    width = 2 * half
    hidden = bu_ref.shape[1]
    lists = [weight_refs[sum(counts[:n]) : sum(counts[: n + 1])] for n in range(4)]
    orders, down_orders = (table_ref, other_ref), (down_table_ref, other_down_ref)
    blocks = table_ref.shape[0]
    down_rows, rows = hidden // blocks, width // blocks
    o_copies = place_halves(place_ref, down_orders, lists[2:], down_rows, rows, wo, so)
    u_copies = place_halves(place_ref, orders, lists[:2], 0, rows, wu, su)
    d_copies = place_halves(place_ref, down_orders, lists[2:], 0, down_rows, wd, sd)

    @pl.when(step == 0)
    def _():
        for c in o_copies + u_copies + d_copies:
            c.start()
        sums_ref[...] = jnp.zeros_like(sums_ref)
        upsum_ref[...] = jnp.zeros_like(upsum_ref)
        for c in o_copies:
            c.wait()

    vec = lambda i: vec_ref[i : i + 1, :]
    total = lambda v: jnp.sum(v, axis=0, keepdims=True)
    mine = pl.ds(pl.multiple_of(core * half, 128), half)
    theirs = pl.ds(pl.multiple_of((1 - core) * half, 128), half)
    mixed_s[:, mine] = mine_ref[...]
    mixed_s[:, theirs] = theirs_ref[...]
    mixed_ref[...] = mixed_s[...]
    groups = [slice(g * BLOCK, g * BLOCK + BLOCK) for g in range(x_ref.shape[0] // BLOCK)]
    chunks = [slice(c * CHUNK, c * CHUNK + CHUNK) for c in range(hidden // CHUNK)]
    firsts = [x_ref[g, :].astype(F32) + (dot(mixed_s[g, :], wo[...]) + vec(0)) for g in groups]
    ones = [normed_of(f) for f in firsts]
    normeds = [n * vec(1) + vec(2) for n, _ in ones]
    lows = [n.astype(BF16) for n in normeds]
    for g, low in zip(groups, lows):
        low_ref[g, :] = low

    @pl.when(step == 0)
    def _():
        for c in u_copies:
            c.wait()

    seconds = [n + vec(3) for n in normeds]
    aheads = [dot(low, wu[:, chunks[0]]) for low in lows]
    for c, at in enumerate(chunks):
        for n, g in enumerate(groups):
            upward = aheads[n] + bu_ref[:, at]
            if c + 1 < len(chunks):
                aheads[n] = dot(lows[n], wu[:, chunks[c + 1]])
            activated, slope = gelu_and_slope(upward)
            activated = activated.astype(BF16)
            act_ref[g, at] = activated
            slope_s[g, at] = slope.astype(BF16)
            if c == n == 0:

                @pl.when(step == 0)
                def _():
                    for copy in d_copies:
                        copy.wait()

            seconds[n] = seconds[n] + dot(activated, wd[at, :])
    sums = [0.0] * 6
    twos, grads = [], []
    for n, g in enumerate(groups):
        normal, scale = normed_of(seconds[n])
        valid = 1.0 - valid_ref[g, sequences : sequences + 1].astype(F32)
        out_ref[g, :] = (valid * (normal * vec(4) + vec(5))).astype(BF16)
        grad = og_ref[g, :].astype(F32) * valid
        grad_second = norm_back(grad, vec(4), normal, scale)
        grad_two = grad_second.astype(BF16)
        gtwo_ref[g, :] = grad_two
        sums[4] += total(grad * normal)
        sums[5] += total(grad)
        sums[3] += total(grad_two.astype(F32))
        twos.append(grad_two)
        grads.append(grad_second)
    aheads = [dot_right(two, wd[chunks[0], :]) for two in twos]
    for c, at in enumerate(chunks):
        for n, g in enumerate(groups):
            now = aheads[n]
            if c + 1 < len(chunks):
                aheads[n] = dot_right(twos[n], wd[chunks[c + 1], :])
            grad_up = (now * slope_s[g, at].astype(F32)).astype(BF16)
            gup_ref[g, at] = grad_up
            upsum_ref[:, at] += total(grad_up.astype(F32))
            grads[n] = grads[n] + dot_right(grad_up, wu[:, at])
    for n, g in enumerate(groups):
        normal, scale = ones[n]
        sums[1] += total(grads[n] * normal)
        sums[2] += total(grads[n])
        grad_one = norm_back(grads[n], vec(1), normal, scale).astype(BF16)
        gone_ref[g, :] = grad_one
        sums[0] += total(grad_one.astype(F32))
        gm_s[g, :] = dot_right(grad_one, wo[...]).astype(BF16)
    for i in range(6):
        sums_ref[i : i + 1, :] += sums[i]
    gm_mine_ref[...] = gm_s[:, mine]
    gm_theirs_ref[...] = gm_s[:, theirs]


def middle(place, table, other, down_table, other_down, x, mine, theirs, out_grad, valid, weights, vectors, up_bias):
    count, width = x.shape
    half = width // 2
    hidden = up_bias.shape[1]
    blocks = table.shape[0]
    row = lambda a: pl.BlockSpec((MIDDLE, a.shape[1]), lambda i, *_: (i, 0))
    rows_of = lambda n: pl.BlockSpec((MIDDLE, n), lambda i, *_: (i, 0))
    whole = lambda a: pl.BlockSpec(a.shape, lambda i, *_: (0, 0))
    anywhere = pl.BlockSpec(memory_space=pl.ANY)
    shape = lambda n: jax.ShapeDtypeStruct((count, n), BF16)
    sums, upsum = jax.ShapeDtypeStruct((8, width), F32), jax.ShapeDtypeStruct((1, hidden), F32)
    return pl.pallas_call(
        partial(middle_kernel, tuple(map(len, weights))),
        out_shape=(shape(width), shape(width), shape(hidden), shape(width), shape(hidden), shape(width), shape(half), shape(half), shape(width), sums, upsum),
        grid_spec=pltpu.PrefetchScalarGridSpec(
            num_scalar_prefetch=5,
            grid=(count // MIDDLE,),
            in_specs=[row(x), row(mine), row(theirs), row(out_grad), row(valid), whole(vectors), whole(up_bias)] + [anywhere] * sum(map(len, weights)),
            out_specs=[rows_of(width), rows_of(width), rows_of(hidden), rows_of(width), rows_of(hidden), rows_of(width), rows_of(half), rows_of(half), rows_of(width), whole(sums), whole(upsum)],
            scratch_shapes=[
                pltpu.VMEM((width, width), BF16), pltpu.VMEM((width, hidden), BF16), pltpu.VMEM((hidden, width), BF16),
                pltpu.VMEM((MIDDLE, width), BF16), pltpu.VMEM((MIDDLE, hidden), BF16), pltpu.VMEM((MIDDLE, width), BF16),
            ] + [pltpu.SemaphoreType.DMA((2 * blocks,))] * 3,
        ),
        compiler_params=pltpu.CompilerParams(vmem_limit_bytes=VMEM_LIMIT),
        cost_estimate=pl.CostEstimate(flops=10**11, bytes_accessed=1000, transcendentals=0),
        name="middle",
    )(place, table, other, down_table, other_down, x, mine, theirs, out_grad, valid, vectors, up_bias, *(w for group in weights for w in group))


def outer_kernel(split, extra, place_ref, table_ref, other_ref, left_ref, right_ref, *refs):
    slots_ref, (mine_ref, theirs_ref, total_s, sem, slot_sem) = (refs[0] if extra else None), refs[-5:]
    step = pl.program_id(0)
    steps = pl.num_programs(0)
    blocks, block_rows, width = mine_ref.shape
    width -= 128 * extra
    columns = 2 * width

    def slot_copies():
        return [
            pltpu.make_async_copy(slots_ref.at[order[i]], target.at[i, :, pl.ds(width, 128)], slot_sem.at[n * blocks + i])
            for n, (order, target) in enumerate(((table_ref, mine_ref), (other_ref, theirs_ref)))
            for i in range(blocks)
        ]

    if extra:

        @pl.when(step == 0)
        def _():
            for c in slot_copies():
                c.start()

    product = dot_rows(left_ref[...], right_ref[...]).astype(BF16)
    if split:
        total_s[:, pl.ds(pl.multiple_of(step * product.shape[1], 128), product.shape[1])] = product
    else:
        total_s[pl.ds(pl.multiple_of(step * product.shape[0], 256), product.shape[0]), :] = product

    def copies(first, count):
        made = []
        for n, (order, target) in enumerate(((other_ref, theirs_ref), (table_ref, mine_ref))):
            side = 1 - place_ref[0] if n == 0 else place_ref[0]
            for i in range(blocks):
                at = pl.ds(pl.multiple_of(order[i] * block_rows, math.gcd(block_rows, 256)), block_rows)
                source = total_s.at[at, pl.ds(pl.multiple_of(side * width + first, 128), count)]
                made.append(pltpu.make_async_copy(source, target.at[i, :, pl.ds(first, count)], sem.at[n * blocks + i]))
        return made

    @pl.when(step == steps - 1)
    def _():
        for c in copies(0, width):
            c.start()
        for c in copies(0, width):
            c.wait()
        if extra:
            for c in slot_copies():
                c.wait()


def outer(place, table, other, left, right, split, slots=()):
    count, rows = left.shape
    columns = right.shape[1]
    blocks = table.shape[0]
    extra = len(slots)
    shape = jax.ShapeDtypeStruct((blocks, rows // blocks, columns // 2 + 128 * extra), BF16)
    anywhere = pl.BlockSpec(memory_space=pl.ANY)
    if split:
        steps = max(1, columns // 768)
        specs = [pl.BlockSpec((count, rows), lambda i, *_: (0, 0)), pl.BlockSpec((count, columns // steps), lambda i, *_: (0, i))]
    else:
        steps = max(1, rows // 768)
        specs = [pl.BlockSpec((count, rows // steps), lambda i, *_: (0, i)), pl.BlockSpec((count, columns), lambda i, *_: (0, 0))]
    return pl.pallas_call(
        partial(outer_kernel, split, extra),
        out_shape=(shape, shape),
        grid_spec=pltpu.PrefetchScalarGridSpec(
            num_scalar_prefetch=3,
            grid=(steps,),
            in_specs=specs + [pl.BlockSpec(s.shape, lambda i, *_: (0, 0, 0)) for s in slots],
            out_specs=[anywhere, anywhere],
            scratch_shapes=[pltpu.VMEM((rows, columns), BF16), pltpu.SemaphoreType.DMA((2 * blocks,)), pltpu.SemaphoreType.DMA((2 * blocks,))],
        ),
        compiler_params=pltpu.CompilerParams(vmem_limit_bytes=28 * 2**20),
        cost_estimate=pl.CostEstimate(flops=10**11, bytes_accessed=1000, transcendentals=0),
        name="outer",
    )(place, table, other, left, right, *slots)


def qkv_grad_kernel(slotted, place_ref, table_ref, own_ref, other_ref, d_ref, dother_ref, out_ref, sums_ref, total_s, sums_s, slots_s, sem, slot_sem):
    step = pl.program_id(0)
    product = (dot_rows(own_ref[...], d_ref[...]) + dot_rows(other_ref[...], dother_ref[...])).astype(BF16)
    ones = jnp.ones((8, own_ref.shape[0]), BF16)
    sums_s[step] = dot(ones, d_ref[...]) + dot(ones, dother_ref[...])
    columns = product.shape[1]
    total_s[:, pl.ds(pl.multiple_of(step * columns, 128), columns)] = product

    @pl.when(step == pl.num_programs(0) - 1)
    def _():
        blocks, rows, _ = out_ref.shape
        copies = []
        for i in range(blocks):
            at = pl.ds(pl.multiple_of(table_ref[i] * rows, math.gcd(rows, 256)), rows)
            copies.append(pltpu.make_async_copy(total_s.at[at], out_ref.at[i, :, pl.ds(0, total_s.shape[1])], sem.at[i]))
        for c in copies:
            c.start()
        sums_ref[...] = sums_s[...]
        if slotted:
            slots_s[...] = jnp.zeros_like(slots_s)
            for n in range(blocks // 2):
                values = [sums_s[j, :1, n * rows : n * rows + rows] for j in range(3)]
                slots_s[place_ref[0] * (blocks // 2) + n, :3, :rows] = jnp.concatenate(values, axis=0).astype(BF16)
            slots = [
                pltpu.make_async_copy(slots_s.at[table_ref[i]], out_ref.at[i, :, pl.ds(total_s.shape[1], 128)], slot_sem.at[i])
                for i in range(blocks)
            ]
            for c in slots:
                c.start()
            copies = copies + slots
        for c in copies:
            c.wait()


def qkv_grad(place, table, own, other, grad_own, grad_other, slotted):
    count, rows = own.shape
    columns = grad_own.shape[1]
    half = columns // 3
    blocks = table.shape[0]
    whole = pl.BlockSpec((count, rows), lambda i, *_: (0, 0))
    tile = pl.BlockSpec((count, half), lambda i, *_: (0, i))
    return pl.pallas_call(
        partial(qkv_grad_kernel, slotted),
        out_shape=(
            jax.ShapeDtypeStruct((blocks, rows // blocks, columns + 128 * slotted), BF16),
            jax.ShapeDtypeStruct((3, 8, half), F32),
        ),
        grid_spec=pltpu.PrefetchScalarGridSpec(
            num_scalar_prefetch=2,
            grid=(3,),
            in_specs=[whole, whole, tile, tile],
            out_specs=[pl.BlockSpec(memory_space=pl.ANY), pl.BlockSpec((3, 8, half), lambda i, *_: (0, 0, 0))],
            scratch_shapes=[
                pltpu.VMEM((rows, columns), BF16), pltpu.VMEM((3, 8, half), F32),
                pltpu.VMEM((blocks, rows // blocks, 128) if slotted else (1, 16, 128), BF16),
                pltpu.SemaphoreType.DMA((blocks,)), pltpu.SemaphoreType.DMA((blocks,)),
            ],
        ),
        compiler_params=pltpu.CompilerParams(vmem_limit_bytes=28 * 2**20),
        cost_estimate=pl.CostEstimate(flops=10**11, bytes_accessed=1000, transcendentals=0),
        name="qkv_grad",
    )(place, table, own, other, grad_own, grad_other)


def pack_kernel(place_ref, *refs):
    *matrices, small_ref, out_ref = refs
    half = matrices[0].shape[1] // 2
    mine = pl.ds(pl.multiple_of(place_ref[0] * half, 128), half)
    for n, ref in enumerate(matrices):
        out_ref[0, :, n * half : n * half + half] = ref[:, mine]
    out_ref[0, :, len(matrices) * half :] = small_ref[...]


def pack(place, matrices, small):
    rows, width = matrices[0].shape
    whole = lambda a: pl.BlockSpec(a.shape, lambda i, *_: (0,) * len(a.shape))
    shape = jax.ShapeDtypeStruct((1, rows, len(matrices) * width // 2 + 128), BF16)
    return pl.pallas_call(
        pack_kernel,
        out_shape=shape,
        grid_spec=pltpu.PrefetchScalarGridSpec(
            num_scalar_prefetch=1,
            grid=(1,),
            in_specs=[whole(a) for a in (*matrices, small)],
            out_specs=whole(shape),
        ),
        name="pack",
    )(place, *matrices, small)


def finish_kernel(place_ref, own_ref, other_ref, *outs):
    half = outs[0].shape[1] // 2
    mine = pl.ds(pl.multiple_of(place_ref[0] * half, 128), half)
    theirs = pl.ds(pl.multiple_of((1 - place_ref[0]) * half, 128), half)
    for n, out in enumerate(outs[:3]):
        at = slice(n * half, n * half + half)
        out[:, mine] = own_ref[:, at].astype(F32)
        out[:, theirs] = other_ref[:, at].astype(F32)
    outs[3][...] = own_ref[:, 3 * half :].astype(F32) + other_ref[:, 3 * half :].astype(F32)


def finish(place, own, other):
    rows, columns = own.shape
    shape = jax.ShapeDtypeStruct((rows, (columns - 128) // 3 * 2), F32)
    whole = lambda s: pl.BlockSpec(s.shape, lambda i, *_: (0, 0))
    small = jax.ShapeDtypeStruct((rows, 128), F32)
    return pl.pallas_call(
        finish_kernel,
        out_shape=(shape, shape, shape, small),
        grid_spec=pltpu.PrefetchScalarGridSpec(
            num_scalar_prefetch=1,
            grid=(1,),
            in_specs=[whole(own), whole(other)],
            out_specs=[whole(shape)] * 3 + [whole(small)],
        ),
        name="finish",
    )(place, own, other)


def input_kernel(added, table_ref, grad_ref, *refs):
    added_refs, w_refs, (out_ref, w_s, sem) = refs[:added], refs[added:-3], refs[-3:]

    @pl.when(pl.program_id(0) == 0)
    def _():
        for c in load_rows(table_ref, w_refs, w_s, sem):
            c.wait()

    total = dot_right(grad_ref[...], w_s[...])
    for ref in added_refs:
        total = total + ref[...].astype(F32)
    out_ref[...] = total.astype(BF16)


def input_part(table, grad, weights, width, *added):
    count, columns = grad.shape
    blocks = table.shape[0]
    row = lambda n: pl.BlockSpec((BLOCK, n), lambda i, *_: (i, 0))
    return pl.pallas_call(
        partial(input_kernel, len(added)),
        out_shape=jax.ShapeDtypeStruct((count, width), BF16),
        grid_spec=pltpu.PrefetchScalarGridSpec(
            num_scalar_prefetch=1,
            grid=(count // BLOCK,),
            in_specs=[row(columns)] + [row(width)] * len(added) + [pl.BlockSpec(memory_space=pl.ANY)] * len(weights),
            out_specs=row(width),
            scratch_shapes=[pltpu.VMEM((width, columns), BF16), pltpu.SemaphoreType.DMA((blocks,))],
        ),
        compiler_params=pltpu.CompilerParams(vmem_limit_bytes=16 * 2**20),
        cost_estimate=pl.CostEstimate(flops=10**11, bytes_accessed=1000, transcendentals=0),
        name="input_part",
    )(table, grad, *added, *weights)


def copy_block(table_ref, source_ref, target_ref):
    target_ref[...] = source_ref[...]


def picked(blocks, table):
    block = (1, *blocks.shape[1:])
    return pl.pallas_call(
        copy_block,
        out_shape=jax.ShapeDtypeStruct(blocks.shape, blocks.dtype),
        grid_spec=pltpu.PrefetchScalarGridSpec(
            num_scalar_prefetch=1,
            grid=(blocks.shape[0],),
            in_specs=[pl.BlockSpec(block, lambda i, t: (t[i], 0, 0))],
            out_specs=pl.BlockSpec(block, lambda i, t: (i, 0, 0)),
        ),
        name="picked",
    )(table, blocks)


def sides(count):
    side = math.isqrt(count // 4)
    if count % 4 == 0 and 4 * side * side == count:
        return (4, side, side)
    return (count, 1, 1)


def hop(value, leg, step, shape):
    deep, tall, wide = shape
    count = deep * tall * wide
    pairs = []
    for core in range(2):
        for here in range(count):
            z, y, x = here // (tall * wide), here // wide % tall, here % wide
            if leg == 0:
                z = (z + step) % deep
            elif (leg == 1) == (core == 0):
                y = (y + step) % tall
            else:
                x = (x + step) % wide
            there = (z * tall + y) * wide + x
            pairs.append((core * count + there, core * count + here))
    return lax.ppermute(value, ("dp", "fsdp"), pairs)


def swapped(value):
    return lax.ppermute(value, "dp", [(0, 1), (1, 0)])


def received(blocks, leg, shape):
    return [hop(blocks, leg, s, shape) for s in range(1, shape[leg])]


def sent(total, leg, shape):
    pieces = total.reshape(shape[leg], -1, *total.shape[1:])
    return [pieces[0]] + [hop(pieces[s], leg, shape[leg] - s, shape) for s in range(1, shape[leg])]


def summed(values):
    return sum(v.astype(F32) for v in values).astype(BF16)


def staged(*values):
    return lax.optimization_barrier(values)


def join(pieces):
    return jnp.concatenate(pieces, axis=0)


def order(core, shape, legs=(0, 1, 2)):
    deep, tall, wide = shape
    here = lax.axis_index("fsdp")
    z, y, x = here // (tall * wide), here // wide % tall, here % wide
    slot = jnp.arange(deep * tall * wide, dtype=jnp.int32)
    steps = {}
    for leg in legs:
        steps[leg] = slot % shape[leg]
        slot = slot // shape[leg]
    z = (z + steps[0]) % deep
    y = (y + jnp.where(core == 0, steps[1], steps[2])) % tall
    x = (x + jnp.where(core == 0, steps[2], steps[1])) % wide
    return (z * tall + y) * wide + x


def inverse(table):
    slots = jnp.arange(table.shape[0], dtype=jnp.int32)
    return jnp.sum(jnp.where(table[None, :] == slots[:, None], slots[None, :], 0), axis=1)


def half_of(array, side):
    width = array.shape[1] // 2
    return lax.dynamic_slice_in_dim(array, side * width, width, 1)


def joined(mine, theirs, core):
    first = jnp.where(core == 0, mine, theirs)
    second = jnp.where(core == 0, theirs, mine)
    return first, second


def reordered(small, table):
    slots = jnp.arange(table.shape[0], dtype=jnp.int32)
    chosen = (table[:, None] == slots[None, :]).astype(F32)
    flat = small.reshape(table.shape[0], -1)
    return jnp.dot(chosen, flat, precision=lax.Precision.HIGHEST).reshape(small.shape)


def shards(
    hidden_in,
    lengths,
    out_grad,
    query_matrix,
    query_offset,
    key_matrix,
    key_offset,
    value_matrix,
    value_offset,
    output_matrix,
    output_offset,
    first_gain,
    first_offset,
    up_matrix,
    up_offset,
    down_matrix,
    down_offset,
    second_gain,
    second_offset,
):
    count, width = hidden_in.shape
    half = width // 2
    rows = query_matrix.shape[0]
    parts = up_offset.shape[0] // rows
    core = lax.axis_index("dp")
    shape = sides(lax.axis_size("fsdp"))
    positions = math.prod(shape)
    table, other_table = order(core, shape), order(1 - core, shape)
    down_legs = (1, 0, 2)
    down_table, other_down_table = order(core, shape, down_legs), order(1 - core, shape, down_legs)
    direct = rows % 16 == 0
    place = jnp.reshape(core, (1,)).astype(jnp.int32)
    zero = jnp.zeros((1,), jnp.int32)
    own_order, their_order = (table, other_table) if direct else (zero, zero)
    own_down_order, their_down_order = (down_table, other_down_table) if direct else (zero, zero)
    down_rows = down_matrix.shape[0]

    def usable(pieces, places, cuts):
        if direct:
            return pieces
        blocks, parts, first = jnp.concatenate(pieces, axis=0), [], 0
        for cut in cuts:
            parts.append(picked(blocks[:, first : first + cut], inverse(places)).reshape(1, -1, blocks.shape[2]))
            first += cut
        return [jnp.concatenate(parts, axis=1)]

    def in_blocks(array, places):
        return array if direct else picked(array.reshape(positions, -1, array.shape[2]), places)

    vectors = (
        query_offset, key_offset, value_offset, output_offset, first_gain, first_offset,
        down_offset, second_gain, second_offset,
    )
    left = jnp.pad(jnp.stack(vectors), ((0, rows - len(vectors)), (0, 64 - rows)))
    right = jnp.pad(up_offset.reshape(parts, rows), ((0, rows - parts), (0, 64 - rows)))
    unit = pack(place, (query_matrix, key_matrix, value_matrix), jnp.concatenate([left, right], axis=1))
    attn_far = received(unit, 0, shape)
    other_lengths = swapped(lengths)
    down_unit = jnp.concatenate([half_of(down_matrix, core), half_of(output_matrix, core)], axis=0)[None]
    down_far = received(down_unit, 1, shape)
    other_in = swapped(hidden_in)
    tables, plan, _ = described(lengths[0], count)

    attn_far, up_matrix, other_lengths, down_far = staged(attn_far, up_matrix, other_lengths, down_far)
    attn_four = join([unit] + attn_far)
    attn_far = received(attn_four, 1, shape)
    up_unit = half_of(up_matrix, core)[None]
    up_far = received(up_unit, 0, shape)
    other_tables, other_plan, _ = described(other_lengths[0], count)

    attn_far, attn_four = staged(attn_far, attn_four)
    attn_eight = join([attn_four] + attn_far)
    attn_far = received(attn_eight, 2, shape)
    down_two = join([down_unit] + down_far)

    attn_far, up_far, down_two = staged(attn_far, up_far, down_two)
    attn = [attn_eight] + attn_far
    small = jnp.concatenate([a[:, :, 3 * half :] for a in attn], axis=0).astype(F32)
    small = reordered(small, inverse(table))
    whole = small[:, : len(vectors), :rows].swapaxes(0, 1).reshape(len(vectors), width)
    up_bias = small[:, :parts, 64 : 64 + rows].reshape(1, -1)
    bias = lax.dynamic_slice_in_dim(whole[:3], core * half, half, 1).reshape(1, -1)
    vector_rows = jnp.pad(whole[3:], ((0, 2), (0, 0)))
    attn = usable(attn, table, (rows,))
    up_four = join([up_unit] + up_far)
    up_far = received(up_four, 1, shape)
    down_far = received(down_two, 0, shape)
    other_q, other_k, other_v, other_norms = project(other_in, attn, own_order, bias, other_tables)

    up_far, up_four, other_q, hidden_in = staged(up_far, up_four, other_q, hidden_in)
    up_eight = join([up_four] + up_far)
    up_far = received(up_eight, 2, shape)
    up_swapped = swapped(up_eight)
    other_mixed, other_lse = attend(other_plan, other_q, other_k, other_v, other_norms, other_tables[2])

    up_swapped, other_mixed, hidden_in = staged(up_swapped, other_mixed, hidden_in)
    mixed_theirs = swapped(other_mixed)
    q, k, v, norms = project(hidden_in, attn, own_order, bias, tables)

    up_far, down_far, mixed_theirs, q = staged(up_far, down_far, mixed_theirs, q)
    down_eight = join([down_two] + down_far)
    down_far = received(down_eight, 2, shape)
    up_swapped = [up_swapped] + [swapped(far) for far in up_far]
    down_swapped = swapped(down_eight)
    mixed, lse = attend(plan, q, k, v, norms, tables[2])

    up_swapped, down_swapped, down_far, mixed, vector_rows, up_bias = staged(
        up_swapped, down_swapped, down_far, mixed, vector_rows, up_bias
    )
    down_swapped = [down_swapped] + [swapped(far) for far in down_far]
    up_weights = [usable([up_eight] + up_far, table, (rows,)), usable(up_swapped, other_table, (rows,))]
    down_weights = [
        usable([down_eight] + down_far, down_table, (down_rows, rows)),
        usable(down_swapped, other_down_table, (down_rows, rows)),
    ]
    (
        hidden_out, normed_low, activated, grad_two, grad_up, grad_one, grad_mine, grad_theirs, both_mixed, sums, up_sum,
    ) = middle(
        place, own_order, their_order, own_down_order, their_down_order, hidden_in, mixed, mixed_theirs, out_grad, tables[2],
        up_weights + down_weights, vector_rows, up_bias,
    )
    other_grad = swapped(grad_theirs)
    places = (place, own_order, their_order)
    slots_of = lambda vectors: vectors.reshape(-1, positions, rows).swapaxes(0, 1)
    left = jnp.pad(slots_of(sums[:6]), ((0, 0), (0, rows - 6), (0, 64 - rows)))
    right = jnp.pad(up_sum.reshape(positions, parts, rows), ((0, 0), (0, rows - parts), (0, 64 - rows)))
    slot_sums = jnp.concatenate([left, right], axis=2)

    def with_slots(pair, slots):
        if direct:
            return pair
        return [
            jnp.concatenate([in_blocks(p, t), reordered(slots, t).astype(BF16)], axis=2)
            for p, t in zip(pair, (table, other_table))
        ]

    output_pair = outer(*places, both_mixed, grad_one, 1, (slot_sums.astype(BF16),) if direct else ())
    output_pair = with_slots(output_pair, slot_sums)

    output_pair, grad_up = staged(output_pair, grad_up)
    output_arrived = swapped(output_pair[1])
    up_pair = outer(*places, normed_low, grad_up, 1)

    up_pair, output_arrived, activated = staged(up_pair, output_arrived, activated)
    up_arrived = swapped(in_blocks(up_pair[1], other_table))
    down_pair = outer(*places, activated, grad_two, 0)

    down_pair, up_arrived, other_grad = staged(down_pair, up_arrived, other_grad)
    up_total = [summed([in_blocks(up_pair[0], table), up_arrived]), summed([output_pair[0], output_arrived])]
    up_sent = sent(jnp.concatenate(up_total, axis=2), 2, shape)
    down_arrived = swapped(in_blocks(down_pair[1], other_table))
    other_d = attend_back(other_plan, other_q, other_k, other_v, other_lse, other_mixed, other_grad, other_tables)

    up_sent, down_arrived, other_d, grad_mine = staged(up_sent, down_arrived, other_d, grad_mine)
    down_sent = sent(summed([in_blocks(down_pair[0], table), down_arrived]), 2, shape)
    up_sent = sent(summed(up_sent), 1, shape)
    own_d = attend_back(plan, q, k, v, lse, mixed, grad_mine, tables)

    up_sent, down_sent, own_d = staged(up_sent, down_sent, own_d)
    up_sent = sent(summed(up_sent), 0, shape)
    down_sent = sent(summed(down_sent), 1, shape)
    matrices, qkv_sums = qkv_grad(place, own_order, hidden_in, other_in, own_d, other_d, direct)

    down_sent, matrices, other_d = staged(down_sent, matrices, other_d)
    if not direct:
        own_sums = jnp.zeros((3, width), F32)
        own_sums = lax.dynamic_update_slice_in_dim(own_sums, qkv_sums[:, 0], core * half, 1)
        own_sums = jnp.pad(slots_of(own_sums), ((0, 0), (0, rows - 3), (0, 128 - rows)))
        matrices = jnp.concatenate([in_blocks(matrices, table), reordered(own_sums, table).astype(BF16)], axis=2)
    matrices_sent = sent(matrices, 2, shape)
    down_sent = sent(summed(down_sent), 0, shape)
    sent_grad = input_part(own_order, other_d, attn, width)

    matrices_sent, up_sent, sent_grad = staged(matrices_sent, up_sent, sent_grad)
    matrices_sent = sent(summed(matrices_sent), 1, shape)
    up_done = summed(up_sent)[0]
    up_other = swapped(up_done)
    other_part = swapped(sent_grad)

    matrices_sent, down_sent, up_other, other_part, own_d = staged(matrices_sent, down_sent, up_other, other_part, own_d)
    matrices_sent = sent(summed(matrices_sent), 0, shape)
    down_done = summed(down_sent)[0]
    down_other = swapped(down_done)
    input_grad = input_part(own_order, own_d, attn, width, other_part, grad_one)

    matrices_sent, down_other, input_grad = staged(matrices_sent, down_other, input_grad)
    matrices_done = summed(matrices_sent)[0]

    up_first, up_second = joined(up_done, up_other, core)
    down_first, down_second = joined(down_done, down_other, core)
    query_grad, key_grad, value_grad, offsets = finish(place, matrices_done, swapped(matrices_done))
    wide = lambda a, b: jnp.concatenate([a, b], axis=1).astype(F32)
    hidden = up_matrix.shape[1] // 2
    others = up_first[:, hidden + half :].astype(F32)
    columns = slice(hidden, hidden + half)
    return (
        hidden_out,
        input_grad,
        query_grad,
        offsets[0, :rows],
        key_grad,
        offsets[1, :rows],
        value_grad,
        offsets[2, :rows],
        wide(up_first[:, columns], up_second[:, columns]),
        others[0, :rows],
        others[1, :rows],
        others[2, :rows],
        wide(up_first[:, :hidden], up_second[:, :hidden]),
        others[:parts, 64 : 64 + rows].reshape(-1),
        wide(down_first, down_second),
        others[3, :rows],
        others[4, :rows],
        others[5, :rows],
    )


def solution(mesh):
    placed = (
        P(("dp", "fsdp"), None),
        P(("dp", "fsdp"), None),
        P(("dp", "fsdp"), None),
        P("fsdp", None),
        P("fsdp"),
        P("fsdp", None),
        P("fsdp"),
        P("fsdp", None),
        P("fsdp"),
        P("fsdp", None),
        P("fsdp"),
        P("fsdp"),
        P("fsdp"),
        P("fsdp", None),
        P("fsdp"),
        P("fsdp", None),
        P("fsdp"),
        P("fsdp"),
        P("fsdp"),
    )
    return jax.shard_map(
        shards,
        mesh=mesh,
        in_specs=placed,
        out_specs=(
            P(("dp", "fsdp"), None),
            P(("dp", "fsdp"), None),
            P("fsdp", None),
            P("fsdp"),
            P("fsdp", None),
            P("fsdp"),
            P("fsdp", None),
            P("fsdp"),
            P("fsdp", None),
            P("fsdp"),
            P("fsdp"),
            P("fsdp"),
            P("fsdp", None),
            P("fsdp"),
            P("fsdp", None),
            P("fsdp"),
            P("fsdp"),
            P("fsdp"),
        ),
        check_vma=False,
    )
```

```python
import math
from functools import partial
import jax, jax.numpy as jnp
from jax import lax
from jax.experimental import pallas as pl
from jax.experimental.pallas import tpu as pltpu
from jax.sharding import PartitionSpec as P

HEAD_DIM = 64
EPSILON = 1e-12
FAR = -1e30
LOG2E = 1.4426950408889634
BLOCK = 256
SAFE = 105.0
F32 = jnp.float32
BF16 = jnp.bfloat16
VMEM_LIMIT = 58 * 2**20


def dot(a, b):
    return jnp.dot(a, b, preferred_element_type=F32)


def dot_right(a, b):
    return lax.dot_general(a, b, (((1,), (1,)), ((), ())), preferred_element_type=F32)


def dot_rows(a, b):
    return lax.dot_general(a, b, (((0,), (0,)), ((), ())), preferred_element_type=F32)


def turned(value, cosines, sines, even_lane):
    partner = jnp.where(even_lane, -pltpu.roll(value, 127, 1), pltpu.roll(value, 1, 1))
    return value * cosines + partner * sines


def lse_lane(head):
    return (HEAD_DIM if head % 2 == 0 else 0) + 8 + 3 * head


def delta_lane(head, heads):
    return lse_lane(head) + 3 * heads


def lanes_of(rows):
    return lax.broadcasted_iota(jnp.int32, (rows, 128), 1)


def load_rows(table_ref, source_refs, target_ref, sem):
    copies = []
    for source in source_refs:
        rows = source.shape[1]
        for i in range(source.shape[0]):
            n = len(copies)
            at = pl.ds(pl.multiple_of(table_ref[n] * rows, math.gcd(rows, 256)), rows)
            copies.append(pltpu.make_async_copy(source.at[i, :, pl.ds(0, target_ref.shape[1])], target_ref.at[at], sem.at[n]))
    for c in copies:
        c.start()
    return copies


def project_kernel(table_ref, x_ref, bias_ref, cos_ref, sin_ref, extq_ref, extk_ref, *refs):
    *w_refs, q_ref, k_ref, v_ref, norm_ref, w_s, sem = refs
    step = pl.program_id(0)

    @pl.when(step == 0)
    def _():
        for c in load_rows(table_ref, w_refs, w_s, sem):
            c.wait()
        norm_ref[...] = jnp.zeros_like(norm_ref)

    heads = q_ref.shape[0]
    width = heads * HEAD_DIM
    lane = lanes_of(BLOCK)
    first_half = lane < HEAD_DIM
    even_lane = lax.rem(lane, 2) == 0
    y = dot(x_ref[...], w_s[...]) + bias_ref[...]
    cosines, sines = cos_ref[...], sin_ref[...]
    extq, extk = extq_ref[...].astype(F32), extk_ref[...].astype(F32)
    row = lax.broadcasted_iota(jnp.int32, (128, BLOCK), 0)
    squares = []
    for p in range(width // 128):
        at = slice(p * 128, p * 128 + 128)
        q = turned(y[:, at], cosines, sines, even_lane) * (HEAD_DIM**-0.5 * LOG2E)
        k = turned(y[:, width + p * 128 : width + p * 128 + 128], cosines, sines, even_lane)
        v = y[:, 2 * width + p * 128 : 2 * width + p * 128 + 128].T
        squares.append(((q * q).astype(BF16), (k * k).astype(BF16)))
        for h in (2 * p, 2 * p + 1):
            own = first_half if h % 2 == 0 else jnp.logical_not(first_half)
            start = lse_lane(h)
            ones = (lane >= start) & (lane < start + 3)
            q_ref[h] = jnp.where(own, q, extq).astype(BF16)
            k_ref[h] = jnp.where(own, k, jnp.where(ones, 1.0, extk)).astype(BF16)
            start = delta_lane(h, heads)
            ones = (row >= start) & (row < start + 3)
            own = row < HEAD_DIM if h % 2 == 0 else row >= HEAD_DIM
            v_ref[h] = jnp.where(own, v, jnp.where(ones, 1.0, 0.0)).astype(BF16)
    column = lax.broadcasted_iota(jnp.int32, (width, 128), 0) // HEAD_DIM
    picks = jnp.where(column == lax.broadcasted_iota(jnp.int32, (width, 128), 1), 1.0, 0.0).astype(BF16)
    sums = [dot(jnp.concatenate([a[n] for a in squares], axis=1), picks) for n in range(2)]
    most = [jnp.max(t, axis=0, keepdims=True) for t in sums]
    norm_ref[...] = jnp.maximum(norm_ref[...], jnp.concatenate(most, axis=1))


def project(x, weights, table, bias, tables):
    count, width = x.shape
    blocks = table.shape[0]
    total = bias.shape[1]
    heads = total // (3 * HEAD_DIM)
    cosines, sines, extq, extk = tables
    row = lambda a: pl.BlockSpec((BLOCK, a.shape[1]), lambda i, t: (i, 0))
    head = pl.BlockSpec((heads, BLOCK, 128), lambda i, t: (0, i, 0))
    shape = jax.ShapeDtypeStruct((heads, count, 128), BF16)
    return pl.pallas_call(
        project_kernel,
        out_shape=(shape, shape, jax.ShapeDtypeStruct((heads, 128, count), BF16), jax.ShapeDtypeStruct((8, 256), F32)),
        grid_spec=pltpu.PrefetchScalarGridSpec(
            num_scalar_prefetch=1,
            grid=(count // BLOCK,),
            in_specs=[
                row(x), pl.BlockSpec((1, total), lambda i, t: (0, 0)), row(cosines), row(sines), row(extq), row(extk),
            ]
            + [pl.BlockSpec(memory_space=pl.ANY)] * len(weights),
            out_specs=[head, head, pl.BlockSpec((heads, 128, BLOCK), lambda i, t: (0, 0, i)), pl.BlockSpec((8, 256), lambda i, t: (0, 0))],
            scratch_shapes=[pltpu.VMEM((width, total), BF16), pltpu.SemaphoreType.DMA((blocks,))],
        ),
        compiler_params=pltpu.CompilerParams(vmem_limit_bytes=VMEM_LIMIT),
        cost_estimate=pl.CostEstimate(flops=10**11, bytes_accessed=1000, transcendentals=0),
        name="project",
    )(table, x, bias, cosines, sines, extq, extk, *weights)


def three_parts(value):
    high = value.astype(BF16).astype(F32)
    rest = value - high
    middle = rest.astype(BF16).astype(F32)
    return high, middle, rest - middle


def attend_kernel(plan_ref, q_ref, k_ref, v_ref, norm_ref, extq_ref, mixed_ref, lse_ref):
    step = pl.program_id(0)
    heads, count, _ = k_ref.shape
    blocks = count // BLOCK
    first, need = plan_ref[2 * step], plan_ref[2 * step + 1]
    safe = jnp.max(norm_ref[:, :128]) * jnp.max(norm_ref[:, 128:]) < SAFE * SAFE
    lane = lanes_of(BLOCK)
    start_lane, any_lane = lane < 0, lane < 0
    for h in range(heads):
        start_lane = start_lane | (lane == lse_lane(h))
        any_lane = any_lane | ((lane >= lse_lane(h)) & (lane < lse_lane(h) + 3))
    pad = extq_ref[:, HEAD_DIM + 4 : HEAD_DIM + 5].astype(F32) > 0.5

    def rows_of(c, plain):
        keys = pl.ds(pl.multiple_of(jnp.minimum(first, blocks - c) * BLOCK, BLOCK), c * BLOCK)
        scores = [dot_right(k_ref[h, keys, :], q_ref[h]) for h in range(heads)]
        outs = []
        packs = [jnp.zeros((24, BLOCK), F32)] * 2
        row = lax.broadcasted_iota(jnp.int32, (24, BLOCK), 0)
        for h in range(heads):
            s = scores[h]
            if not plain:
                peak = jnp.max(s, axis=0, keepdims=True)
                s = s - peak
            o = dot(v_ref[h, :, keys], jnp.exp2(s).astype(BF16))
            ones = delta_lane(h, heads)
            total = o[ones : ones + 1, :]
            outs.append((o[:HEAD_DIM] if h % 2 == 0 else o[HEAD_DIM:]) / total)
            lse = -jnp.log2(total)
            if not plain:
                lse = lse - peak
            for j, part in enumerate(three_parts(lse)):
                packs[h % 2] = jnp.where(row == 3 * h + j, part, packs[h % 2])
        mixed_ref[...] = jnp.concatenate(outs, axis=0).T.astype(BF16)
        gap = lambda n: jnp.zeros((n, BLOCK), F32)
        packed = jnp.concatenate([gap(8), packs[1], gap(40), packs[0], gap(32)], axis=0).T
        lse_ref[...] = jnp.where(pad & any_lane, jnp.where(start_lane, FAR, 0.0), packed).astype(BF16)

    @pl.when(need == 0)
    def _():
        mixed_ref[...] = jnp.zeros_like(mixed_ref)
        lse_ref[...] = jnp.where(start_lane, FAR, 0.0).astype(BF16)

    for c in range(1, blocks + 1):
        pl.when(safe & (need == c))(partial(rows_of, c, True))
    pl.when(jnp.logical_not(safe) & (need > 0))(partial(rows_of, blocks, False))


def attend(plan, q, k, v, norms, extq):
    heads, count, _ = q.shape
    whole = lambda a: pl.BlockSpec(a.shape, lambda i, p: (0,) * a.ndim)
    return pl.pallas_call(
        attend_kernel,
        out_shape=(jax.ShapeDtypeStruct((count, heads * HEAD_DIM), BF16), jax.ShapeDtypeStruct((count, 128), BF16)),
        grid_spec=pltpu.PrefetchScalarGridSpec(
            num_scalar_prefetch=1,
            grid=(count // BLOCK,),
            in_specs=[
                pl.BlockSpec((heads, BLOCK, 128), lambda i, p: (0, i, 0)), whole(k), whole(v), whole(norms),
                pl.BlockSpec((BLOCK, 128), lambda i, p: (i, 0)),
            ],
            out_specs=[pl.BlockSpec((BLOCK, heads * HEAD_DIM), lambda i, p: (i, 0)), pl.BlockSpec((BLOCK, 128), lambda i, p: (i, 0))],
        ),
        compiler_params=pltpu.CompilerParams(vmem_limit_bytes=VMEM_LIMIT),
        cost_estimate=pl.CostEstimate(flops=10**11, bytes_accessed=1000, transcendentals=0),
        name="attend",
    )(plan, q, k, v, norms, extq)


def attend_back_kernel(plan_ref, q_ref, k_ref, v_ref, lse_ref, mixed_ref, grad_ref, cos_ref, sin_ref, cos_all, sin_all,
                       d_ref, dk_s, dv_s):
    step = pl.program_id(0)
    heads, count, _ = k_ref.shape
    width = heads * HEAD_DIM
    blocks = count // BLOCK
    first, need = plan_ref[2 * step], plan_ref[2 * step + 1]
    lane = lanes_of(BLOCK)
    first_half = lane < HEAD_DIM
    even_lane = lax.rem(lane, 2) == 0
    scale = HEAD_DIM**-0.5

    @pl.when(step == 0)
    def _():
        dk_s[...] = jnp.zeros_like(dk_s)
        dv_s[...] = jnp.zeros_like(dv_s)

    def rows_of(c):
        keys = pl.ds(pl.multiple_of(jnp.minimum(first, blocks - c) * BLOCK, BLOCK), c * BLOCK)
        grad = grad_ref[...].astype(F32)
        product = grad * mixed_ref[...].astype(F32)
        high = product.astype(BF16)
        low = (product - high.astype(F32)).astype(BF16)
        column = lax.broadcasted_iota(jnp.int32, (width, 128), 0) // HEAD_DIM
        slot = lax.broadcasted_iota(jnp.int32, (width, 128), 1)
        slot = slot - jnp.where(lax.rem(column, 2) == 0, delta_lane(0, heads), delta_lane(0, heads) - HEAD_DIM)
        picks = jnp.where((slot >= 3 * column) & (slot < 3 * column + 3), 1.0, 0.0).astype(BF16)
        delta = three_parts(-(dot(high, picks) + dot(low, picks)))
        inner = jnp.where(first_half, lane, lane - HEAD_DIM)
        part = lax.rem(inner + 1, 3)
        delta = jnp.where(part == 0, delta[0], jnp.where(part == 1, delta[1], delta[2]))
        extra = jnp.where(inner < 8 + 3 * heads, lse_ref[...].astype(F32), delta)
        dqs = []
        for p in range(width // 128):
            at = slice(p * 128, p * 128 + 128)
            pair = grad[:, at]
            pair_t = pair.T.astype(BF16)
            qs = [q_ref[2 * p].astype(F32), q_ref[2 * p + 1].astype(F32)]
            q_t = jnp.where(first_half, qs[0], qs[1]).T.astype(BF16)
            both = []
            for n in range(2):
                h = 2 * p + n
                own = first_half if n == 0 else jnp.logical_not(first_half)
                side = slice(n * HEAD_DIM, n * HEAD_DIM + HEAD_DIM)
                g = jnp.where(own, pair, extra).astype(BF16)
                q = jnp.where(own | (inner < 8), qs[n], extra).astype(BF16)
                k = k_ref[h, keys, :]
                probs = jnp.exp2(dot_right(q, k))
                shifted = dot(g, v_ref[h, :, keys])
                grads = (probs * shifted).astype(BF16)
                dv_s[h, :, keys] += dot(pair_t[side], probs.astype(BF16))
                dk_s[h, :, keys] += dot(q_t[side], grads)
                both.append(dot(grads, k))
            dq = jnp.where(first_half, both[0], both[1]) * scale
            d_ref[pl.ds(pl.multiple_of(step * BLOCK, BLOCK), BLOCK), at] = turned(dq, cos_ref[...], -sin_ref[...], even_lane).astype(BF16)

    @pl.when(need == 0)
    def _():
        d_ref[pl.ds(pl.multiple_of(step * BLOCK, BLOCK), BLOCK), :width] = jnp.zeros((BLOCK, width), BF16)

    for c in range(1, blocks + 1):
        pl.when(need == c)(partial(rows_of, c))

    @pl.when(step == blocks - 1)
    def _():
        for p in range(width // 128):
            for r in range(blocks):
                at = slice(r * BLOCK, r * BLOCK + BLOCK)
                dv = jnp.concatenate([dv_s[2 * p, :, at], dv_s[2 * p + 1, :, at]], axis=0).T
                dk = jnp.concatenate([dk_s[2 * p, :, at], dk_s[2 * p + 1, :, at]], axis=0).T * (1.0 / LOG2E)
                d_ref[at, 2 * width + p * 128 : 2 * width + p * 128 + 128] = dv.astype(BF16)
                d_ref[at, width + p * 128 : width + p * 128 + 128] = turned(dk, cos_all[at, :], -sin_all[at, :], even_lane).astype(BF16)


def attend_back(plan, q, k, v, lse, mixed, grad, tables):
    heads, count, _ = q.shape
    width = heads * HEAD_DIM
    cosines, sines = tables[:2]
    whole = lambda a: pl.BlockSpec(a.shape, lambda i, p: (0,) * a.ndim)
    row = lambda a: pl.BlockSpec((BLOCK, a.shape[1]), lambda i, p: (i, 0))
    shape = jax.ShapeDtypeStruct((count, 3 * width), BF16)
    return pl.pallas_call(
        attend_back_kernel,
        out_shape=shape,
        grid_spec=pltpu.PrefetchScalarGridSpec(
            num_scalar_prefetch=1,
            grid=(count // BLOCK,),
            in_specs=[
                pl.BlockSpec((heads, BLOCK, 128), lambda i, p: (0, i, 0)), whole(k), whole(v), row(lse), row(mixed), row(grad),
                row(cosines), row(sines), whole(cosines), whole(sines),
            ],
            out_specs=pl.BlockSpec((count, 3 * width), lambda i, p: (0, 0)),
            scratch_shapes=[pltpu.VMEM((heads, HEAD_DIM, count), F32)] * 2,
        ),
        compiler_params=pltpu.CompilerParams(vmem_limit_bytes=40 * 2**20),
        cost_estimate=pl.CostEstimate(flops=10**11, bytes_accessed=1000, transcendentals=0),
        name="attend_back",
    )(plan, q, k, v, lse, mixed, grad, cosines, sines, cosines, sines)


def described(lengths, count):
    total = lengths.shape[0]
    index = jnp.arange(total)
    ends = jnp.sum(jnp.where(index[:, None] >= index[None, :], lengths[None, :], 0), axis=1)
    starts = ends - lengths
    slots = jnp.arange(count, dtype=jnp.int32)
    segment = jnp.sum((slots[:, None] >= ends[None, :]).astype(jnp.int32), axis=1)
    owner = segment[:, None] == jnp.arange(total, dtype=jnp.int32)[None, :]
    begin = jnp.sum(jnp.where(owner, starts[None, :], 0), axis=1)
    position = (slots - begin).astype(F32)
    lane = jnp.arange(128, dtype=jnp.int32)
    inverse = jnp.power(10000.0, -2.0 * (lane % HEAD_DIM // 2).astype(F32) / HEAD_DIM)
    angle = position[:, None] * inverse[None, :]
    cosines, sines = jnp.cos(angle), jnp.sin(angle)
    code = (lane % HEAD_DIM)[None, :]
    extq = jnp.where(code == segment[:, None], 1.0, 0.0).astype(BF16)
    extk = jnp.where((code < total) & (code != segment[:, None]), FAR, 0.0).astype(BF16)
    filled = jnp.sum(lengths)
    opens = jnp.arange(count // BLOCK, dtype=jnp.int32) * BLOCK
    closes = jnp.minimum(opens + BLOCK, filled)
    low = jnp.max(jnp.where(ends[None, :] <= opens[:, None], ends[None, :], 0), axis=1)
    high = jnp.min(jnp.where(ends[None, :] >= closes[:, None], ends[None, :], filled), axis=1)
    first = low // BLOCK
    need = jnp.where(opens < filled, (high + BLOCK - 1) // BLOCK - first, 0)
    plan = jnp.stack([first, need], axis=1).reshape(-1)
    valid = (segment < total).astype(F32)
    return (cosines, sines, extq, extk), plan, valid


def normed_of(value):
    center = value - jnp.mean(value, axis=1, keepdims=True)
    scale = lax.rsqrt(jnp.mean(center * center, axis=1, keepdims=True) + EPSILON)
    return center * scale, scale


def norm_back(grad, gain, normed, scale):
    scaled = grad * gain
    return (scaled - jnp.mean(scaled, axis=1, keepdims=True) - normed * jnp.mean(scaled * normed, axis=1, keepdims=True)) * scale


def gelu_and_slope(value):
    bell = jnp.exp2(value * value * (-0.5 * LOG2E))
    t = 1.0 / (1.0 + (0.3275911 * 0.5**0.5) * jnp.abs(value))
    tail = t * (0.5 * 0.254829592 + t * (0.5 * -0.284496736 + t * (0.5 * 1.421413741 + t * (0.5 * -1.453152027 + t * (0.5 * 1.061405429)))))
    tail = tail * bell
    below = jnp.where(value < 0.0, tail, 1.0 - tail)
    return value * below, below + value * bell * (2.0 * math.pi) ** -0.5


CHUNK = 1024
MIDDLE = 512


def place_halves(place_ref, orders, sources, first, rows, target_ref, sem):
    copies = []
    for n, (order, refs) in enumerate(zip(orders, sources)):
        side = place_ref[0] if n == 0 else 1 - place_ref[0]
        blocks = 0
        for ref in refs:
            width = ref.shape[2]
            for i in range(ref.shape[0]):
                at = pl.ds(pl.multiple_of(order[blocks] * rows, math.gcd(rows, 256)), rows)
                columns = pl.ds(pl.multiple_of(side * width, 128), width)
                copies.append(pltpu.make_async_copy(ref.at[i, pl.ds(first, rows)], target_ref.at[at, columns], sem.at[len(copies)]))
                blocks += 1
    return copies


def middle_kernel(counts, place_ref, table_ref, other_ref, down_table_ref, other_down_ref, x_ref, mine_ref, theirs_ref, og_ref, valid_ref, vec_ref, bu_ref, *refs):
    weight_refs, refs = refs[: sum(counts)], refs[sum(counts) :]
    (
        out_ref, low_ref, act_ref, gtwo_ref, gup_ref, gone_ref, gm_mine_ref, gm_theirs_ref, mixed_ref, sums_ref, upsum_ref,
        wo, wu, wd, mixed_s, slope_s, gm_s, so, su, sd,
    ) = refs
    step = pl.program_id(0)
    sequences = 4
    core = place_ref[0]
    half = mine_ref.shape[1]
    width = 2 * half
    hidden = bu_ref.shape[1]
    lists = [weight_refs[sum(counts[:n]) : sum(counts[: n + 1])] for n in range(4)]
    orders, down_orders = (table_ref, other_ref), (down_table_ref, other_down_ref)
    blocks = table_ref.shape[0]
    down_rows, rows = hidden // blocks, width // blocks
    o_copies = place_halves(place_ref, down_orders, lists[2:], down_rows, rows, wo, so)
    u_copies = place_halves(place_ref, orders, lists[:2], 0, rows, wu, su)
    d_copies = place_halves(place_ref, down_orders, lists[2:], 0, down_rows, wd, sd)

    @pl.when(step == 0)
    def _():
        for c in o_copies + u_copies + d_copies:
            c.start()
        sums_ref[...] = jnp.zeros_like(sums_ref)
        upsum_ref[...] = jnp.zeros_like(upsum_ref)
        for c in o_copies:
            c.wait()

    vec = lambda i: vec_ref[i : i + 1, :]
    total = lambda v: jnp.sum(v, axis=0, keepdims=True)
    mine = pl.ds(pl.multiple_of(core * half, 128), half)
    theirs = pl.ds(pl.multiple_of((1 - core) * half, 128), half)
    mixed_s[:, mine] = mine_ref[...]
    mixed_s[:, theirs] = theirs_ref[...]
    mixed_ref[...] = mixed_s[...]
    groups = [slice(g * BLOCK, g * BLOCK + BLOCK) for g in range(x_ref.shape[0] // BLOCK)]
    chunks = [slice(c * CHUNK, c * CHUNK + CHUNK) for c in range(hidden // CHUNK)]
    firsts = [x_ref[g, :].astype(F32) + (dot(mixed_s[g, :], wo[...]) + vec(0)) for g in groups]
    ones = [normed_of(f) for f in firsts]
    normeds = [n * vec(1) + vec(2) for n, _ in ones]
    lows = [n.astype(BF16) for n in normeds]
    for g, low in zip(groups, lows):
        low_ref[g, :] = low

    @pl.when(step == 0)
    def _():
        for c in u_copies:
            c.wait()

    seconds = [n + vec(3) for n in normeds]
    aheads = [dot(low, wu[:, chunks[0]]) for low in lows]
    for c, at in enumerate(chunks):
        for n, g in enumerate(groups):
            upward = aheads[n] + bu_ref[:, at]
            if c + 1 < len(chunks):
                aheads[n] = dot(lows[n], wu[:, chunks[c + 1]])
            activated, slope = gelu_and_slope(upward)
            activated = activated.astype(BF16)
            act_ref[g, at] = activated
            slope_s[g, at] = slope.astype(BF16)
            if c == n == 0:

                @pl.when(step == 0)
                def _():
                    for copy in d_copies:
                        copy.wait()

            seconds[n] = seconds[n] + dot(activated, wd[at, :])
    sums = [0.0] * 6
    twos, grads = [], []
    for n, g in enumerate(groups):
        normal, scale = normed_of(seconds[n])
        valid = 1.0 - valid_ref[g, sequences : sequences + 1].astype(F32)
        out_ref[g, :] = (valid * (normal * vec(4) + vec(5))).astype(BF16)
        grad = og_ref[g, :].astype(F32) * valid
        grad_second = norm_back(grad, vec(4), normal, scale)
        grad_two = grad_second.astype(BF16)
        gtwo_ref[g, :] = grad_two
        sums[4] += total(grad * normal)
        sums[5] += total(grad)
        sums[3] += total(grad_two.astype(F32))
        twos.append(grad_two)
        grads.append(grad_second)
    aheads = [dot_right(two, wd[chunks[0], :]) for two in twos]
    for c, at in enumerate(chunks):
        for n, g in enumerate(groups):
            now = aheads[n]
            if c + 1 < len(chunks):
                aheads[n] = dot_right(twos[n], wd[chunks[c + 1], :])
            grad_up = (now * slope_s[g, at].astype(F32)).astype(BF16)
            gup_ref[g, at] = grad_up
            upsum_ref[:, at] += total(grad_up.astype(F32))
            grads[n] = grads[n] + dot_right(grad_up, wu[:, at])
    for n, g in enumerate(groups):
        normal, scale = ones[n]
        sums[1] += total(grads[n] * normal)
        sums[2] += total(grads[n])
        grad_one = norm_back(grads[n], vec(1), normal, scale).astype(BF16)
        gone_ref[g, :] = grad_one
        sums[0] += total(grad_one.astype(F32))
        gm_s[g, :] = dot_right(grad_one, wo[...]).astype(BF16)
    for i in range(6):
        sums_ref[i : i + 1, :] += sums[i]
    gm_mine_ref[...] = gm_s[:, mine]
    gm_theirs_ref[...] = gm_s[:, theirs]


def middle(place, table, other, down_table, other_down, x, mine, theirs, out_grad, valid, weights, vectors, up_bias):
    count, width = x.shape
    half = width // 2
    hidden = up_bias.shape[1]
    blocks = table.shape[0]
    row = lambda a: pl.BlockSpec((MIDDLE, a.shape[1]), lambda i, *_: (i, 0))
    rows_of = lambda n: pl.BlockSpec((MIDDLE, n), lambda i, *_: (i, 0))
    whole = lambda a: pl.BlockSpec(a.shape, lambda i, *_: (0, 0))
    anywhere = pl.BlockSpec(memory_space=pl.ANY)
    shape = lambda n: jax.ShapeDtypeStruct((count, n), BF16)
    sums, upsum = jax.ShapeDtypeStruct((8, width), F32), jax.ShapeDtypeStruct((1, hidden), F32)
    return pl.pallas_call(
        partial(middle_kernel, tuple(map(len, weights))),
        out_shape=(shape(width), shape(width), shape(hidden), shape(width), shape(hidden), shape(width), shape(half), shape(half), shape(width), sums, upsum),
        grid_spec=pltpu.PrefetchScalarGridSpec(
            num_scalar_prefetch=5,
            grid=(count // MIDDLE,),
            in_specs=[row(x), row(mine), row(theirs), row(out_grad), row(valid), whole(vectors), whole(up_bias)] + [anywhere] * sum(map(len, weights)),
            out_specs=[rows_of(width), rows_of(width), rows_of(hidden), rows_of(width), rows_of(hidden), rows_of(width), rows_of(half), rows_of(half), rows_of(width), whole(sums), whole(upsum)],
            scratch_shapes=[
                pltpu.VMEM((width, width), BF16), pltpu.VMEM((width, hidden), BF16), pltpu.VMEM((hidden, width), BF16),
                pltpu.VMEM((MIDDLE, width), BF16), pltpu.VMEM((MIDDLE, hidden), BF16), pltpu.VMEM((MIDDLE, width), BF16),
            ] + [pltpu.SemaphoreType.DMA((2 * blocks,))] * 3,
        ),
        compiler_params=pltpu.CompilerParams(vmem_limit_bytes=VMEM_LIMIT),
        cost_estimate=pl.CostEstimate(flops=10**11, bytes_accessed=1000, transcendentals=0),
        name="middle",
    )(place, table, other, down_table, other_down, x, mine, theirs, out_grad, valid, vectors, up_bias, *(w for group in weights for w in group))


def outer_kernel(split, extra, place_ref, table_ref, other_ref, left_ref, right_ref, *refs):
    slots_ref, (mine_ref, theirs_ref, total_s, sem, slot_sem) = (refs[0] if extra else None), refs[-5:]
    step = pl.program_id(0)
    steps = pl.num_programs(0)
    blocks, block_rows, width = mine_ref.shape
    width -= 128 * extra
    columns = 2 * width

    def slot_copies():
        return [
            pltpu.make_async_copy(slots_ref.at[order[i]], target.at[i, :, pl.ds(width, 128)], slot_sem.at[n * blocks + i])
            for n, (order, target) in enumerate(((table_ref, mine_ref), (other_ref, theirs_ref)))
            for i in range(blocks)
        ]

    if extra:

        @pl.when(step == 0)
        def _():
            for c in slot_copies():
                c.start()

    product = dot_rows(left_ref[...], right_ref[...]).astype(BF16)
    if split:
        total_s[:, pl.ds(pl.multiple_of(step * product.shape[1], 128), product.shape[1])] = product
    else:
        total_s[pl.ds(pl.multiple_of(step * product.shape[0], 256), product.shape[0]), :] = product

    def copies(first, count):
        made = []
        for n, (order, target) in enumerate(((other_ref, theirs_ref), (table_ref, mine_ref))):
            side = 1 - place_ref[0] if n == 0 else place_ref[0]
            for i in range(blocks):
                at = pl.ds(pl.multiple_of(order[i] * block_rows, math.gcd(block_rows, 256)), block_rows)
                source = total_s.at[at, pl.ds(pl.multiple_of(side * width + first, 128), count)]
                made.append(pltpu.make_async_copy(source, target.at[i, :, pl.ds(first, count)], sem.at[n * blocks + i]))
        return made

    @pl.when(step == steps - 1)
    def _():
        for c in copies(0, width):
            c.start()
        for c in copies(0, width):
            c.wait()
        if extra:
            for c in slot_copies():
                c.wait()


def outer(place, table, other, left, right, split, slots=()):
    count, rows = left.shape
    columns = right.shape[1]
    blocks = table.shape[0]
    extra = len(slots)
    shape = jax.ShapeDtypeStruct((blocks, rows // blocks, columns // 2 + 128 * extra), BF16)
    anywhere = pl.BlockSpec(memory_space=pl.ANY)
    if split:
        steps = max(1, columns // 768)
        specs = [pl.BlockSpec((count, rows), lambda i, *_: (0, 0)), pl.BlockSpec((count, columns // steps), lambda i, *_: (0, i))]
    else:
        steps = max(1, rows // 768)
        specs = [pl.BlockSpec((count, rows // steps), lambda i, *_: (0, i)), pl.BlockSpec((count, columns), lambda i, *_: (0, 0))]
    return pl.pallas_call(
        partial(outer_kernel, split, extra),
        out_shape=(shape, shape),
        grid_spec=pltpu.PrefetchScalarGridSpec(
            num_scalar_prefetch=3,
            grid=(steps,),
            in_specs=specs + [pl.BlockSpec(s.shape, lambda i, *_: (0, 0, 0)) for s in slots],
            out_specs=[anywhere, anywhere],
            scratch_shapes=[pltpu.VMEM((rows, columns), BF16), pltpu.SemaphoreType.DMA((2 * blocks,)), pltpu.SemaphoreType.DMA((2 * blocks,))],
        ),
        compiler_params=pltpu.CompilerParams(vmem_limit_bytes=28 * 2**20),
        cost_estimate=pl.CostEstimate(flops=10**11, bytes_accessed=1000, transcendentals=0),
        name="outer",
    )(place, table, other, left, right, *slots)


def qkv_grad_kernel(slotted, place_ref, table_ref, own_ref, other_ref, d_ref, dother_ref, out_ref, sums_ref, total_s, sums_s, slots_s, sem, slot_sem):
    step = pl.program_id(0)
    product = (dot_rows(own_ref[...], d_ref[...]) + dot_rows(other_ref[...], dother_ref[...])).astype(BF16)
    ones = jnp.ones((8, own_ref.shape[0]), BF16)
    sums_s[step] = dot(ones, d_ref[...]) + dot(ones, dother_ref[...])
    columns = product.shape[1]
    total_s[:, pl.ds(pl.multiple_of(step * columns, 128), columns)] = product

    @pl.when(step == pl.num_programs(0) - 1)
    def _():
        blocks, rows, _ = out_ref.shape
        copies = []
        for i in range(blocks):
            at = pl.ds(pl.multiple_of(table_ref[i] * rows, math.gcd(rows, 256)), rows)
            copies.append(pltpu.make_async_copy(total_s.at[at], out_ref.at[i, :, pl.ds(0, total_s.shape[1])], sem.at[i]))
        for c in copies:
            c.start()
        sums_ref[...] = sums_s[...]
        if slotted:
            slots_s[...] = jnp.zeros_like(slots_s)
            for n in range(blocks // 2):
                values = [sums_s[j, :1, n * rows : n * rows + rows] for j in range(3)]
                slots_s[place_ref[0] * (blocks // 2) + n, :3, :rows] = jnp.concatenate(values, axis=0).astype(BF16)
            slots = [
                pltpu.make_async_copy(slots_s.at[table_ref[i]], out_ref.at[i, :, pl.ds(total_s.shape[1], 128)], slot_sem.at[i])
                for i in range(blocks)
            ]
            for c in slots:
                c.start()
            copies = copies + slots
        for c in copies:
            c.wait()


def qkv_grad(place, table, own, other, grad_own, grad_other, slotted):
    count, rows = own.shape
    columns = grad_own.shape[1]
    half = columns // 3
    blocks = table.shape[0]
    whole = pl.BlockSpec((count, rows), lambda i, *_: (0, 0))
    tile = pl.BlockSpec((count, half), lambda i, *_: (0, i))
    return pl.pallas_call(
        partial(qkv_grad_kernel, slotted),
        out_shape=(
            jax.ShapeDtypeStruct((blocks, rows // blocks, columns + 128 * slotted), BF16),
            jax.ShapeDtypeStruct((3, 8, half), F32),
        ),
        grid_spec=pltpu.PrefetchScalarGridSpec(
            num_scalar_prefetch=2,
            grid=(3,),
            in_specs=[whole, whole, tile, tile],
            out_specs=[pl.BlockSpec(memory_space=pl.ANY), pl.BlockSpec((3, 8, half), lambda i, *_: (0, 0, 0))],
            scratch_shapes=[
                pltpu.VMEM((rows, columns), BF16), pltpu.VMEM((3, 8, half), F32),
                pltpu.VMEM((blocks, rows // blocks, 128) if slotted else (1, 16, 128), BF16),
                pltpu.SemaphoreType.DMA((blocks,)), pltpu.SemaphoreType.DMA((blocks,)),
            ],
        ),
        compiler_params=pltpu.CompilerParams(vmem_limit_bytes=28 * 2**20),
        cost_estimate=pl.CostEstimate(flops=10**11, bytes_accessed=1000, transcendentals=0),
        name="qkv_grad",
    )(place, table, own, other, grad_own, grad_other)


def pack_kernel(place_ref, *refs):
    *matrices, small_ref, out_ref = refs
    half = matrices[0].shape[1] // 2
    mine = pl.ds(pl.multiple_of(place_ref[0] * half, 128), half)
    for n, ref in enumerate(matrices):
        out_ref[0, :, n * half : n * half + half] = ref[:, mine]
    out_ref[0, :, len(matrices) * half :] = small_ref[...]


def pack(place, matrices, small):
    rows, width = matrices[0].shape
    whole = lambda a: pl.BlockSpec(a.shape, lambda i, *_: (0,) * len(a.shape))
    shape = jax.ShapeDtypeStruct((1, rows, len(matrices) * width // 2 + 128), BF16)
    return pl.pallas_call(
        pack_kernel,
        out_shape=shape,
        grid_spec=pltpu.PrefetchScalarGridSpec(
            num_scalar_prefetch=1,
            grid=(1,),
            in_specs=[whole(a) for a in (*matrices, small)],
            out_specs=whole(shape),
        ),
        name="pack",
    )(place, *matrices, small)


def finish_kernel(place_ref, own_ref, other_ref, *outs):
    half = outs[0].shape[1] // 2
    mine = pl.ds(pl.multiple_of(place_ref[0] * half, 128), half)
    theirs = pl.ds(pl.multiple_of((1 - place_ref[0]) * half, 128), half)
    for n, out in enumerate(outs[:3]):
        at = slice(n * half, n * half + half)
        out[:, mine] = own_ref[:, at].astype(F32)
        out[:, theirs] = other_ref[:, at].astype(F32)
    outs[3][...] = own_ref[:, 3 * half :].astype(F32) + other_ref[:, 3 * half :].astype(F32)


def finish(place, own, other):
    rows, columns = own.shape
    shape = jax.ShapeDtypeStruct((rows, (columns - 128) // 3 * 2), F32)
    whole = lambda s: pl.BlockSpec(s.shape, lambda i, *_: (0, 0))
    small = jax.ShapeDtypeStruct((rows, 128), F32)
    return pl.pallas_call(
        finish_kernel,
        out_shape=(shape, shape, shape, small),
        grid_spec=pltpu.PrefetchScalarGridSpec(
            num_scalar_prefetch=1,
            grid=(1,),
            in_specs=[whole(own), whole(other)],
            out_specs=[whole(shape)] * 3 + [whole(small)],
        ),
        name="finish",
    )(place, own, other)


def input_kernel(added, table_ref, grad_ref, *refs):
    added_refs, w_refs, (out_ref, w_s, sem) = refs[:added], refs[added:-3], refs[-3:]

    @pl.when(pl.program_id(0) == 0)
    def _():
        for c in load_rows(table_ref, w_refs, w_s, sem):
            c.wait()

    total = dot_right(grad_ref[...], w_s[...])
    for ref in added_refs:
        total = total + ref[...].astype(F32)
    out_ref[...] = total.astype(BF16)


def input_part(table, grad, weights, width, *added):
    count, columns = grad.shape
    blocks = table.shape[0]
    row = lambda n: pl.BlockSpec((BLOCK, n), lambda i, *_: (i, 0))
    return pl.pallas_call(
        partial(input_kernel, len(added)),
        out_shape=jax.ShapeDtypeStruct((count, width), BF16),
        grid_spec=pltpu.PrefetchScalarGridSpec(
            num_scalar_prefetch=1,
            grid=(count // BLOCK,),
            in_specs=[row(columns)] + [row(width)] * len(added) + [pl.BlockSpec(memory_space=pl.ANY)] * len(weights),
            out_specs=row(width),
            scratch_shapes=[pltpu.VMEM((width, columns), BF16), pltpu.SemaphoreType.DMA((blocks,))],
        ),
        compiler_params=pltpu.CompilerParams(vmem_limit_bytes=16 * 2**20),
        cost_estimate=pl.CostEstimate(flops=10**11, bytes_accessed=1000, transcendentals=0),
        name="input_part",
    )(table, grad, *added, *weights)


def copy_block(table_ref, source_ref, target_ref):
    target_ref[...] = source_ref[...]


def picked(blocks, table):
    block = (1, *blocks.shape[1:])
    return pl.pallas_call(
        copy_block,
        out_shape=jax.ShapeDtypeStruct(blocks.shape, blocks.dtype),
        grid_spec=pltpu.PrefetchScalarGridSpec(
            num_scalar_prefetch=1,
            grid=(blocks.shape[0],),
            in_specs=[pl.BlockSpec(block, lambda i, t: (t[i], 0, 0))],
            out_specs=pl.BlockSpec(block, lambda i, t: (i, 0, 0)),
        ),
        name="picked",
    )(table, blocks)


def sides(count):
    side = math.isqrt(count // 4)
    if count % 4 == 0 and 4 * side * side == count:
        return (4, side, side)
    return (count, 1, 1)


def hop(value, leg, step, shape):
    deep, tall, wide = shape
    count = deep * tall * wide
    pairs = []
    for core in range(2):
        for here in range(count):
            z, y, x = here // (tall * wide), here // wide % tall, here % wide
            if leg == 0:
                z = (z + step) % deep
            elif (leg == 1) == (core == 0):
                y = (y + step) % tall
            else:
                x = (x + step) % wide
            there = (z * tall + y) * wide + x
            pairs.append((core * count + there, core * count + here))
    return lax.ppermute(value, ("dp", "fsdp"), pairs)


def swapped(value):
    return lax.ppermute(value, "dp", [(0, 1), (1, 0)])


def received(blocks, leg, shape):
    return [hop(blocks, leg, s, shape) for s in range(1, shape[leg])]


def sent(total, leg, shape):
    pieces = total.reshape(shape[leg], -1, *total.shape[1:])
    return [pieces[0]] + [hop(pieces[s], leg, shape[leg] - s, shape) for s in range(1, shape[leg])]


def summed(values):
    return sum(v.astype(F32) for v in values).astype(BF16)


def staged(*values):
    return lax.optimization_barrier(values)


def join_kernel(*refs):
    *pieces, whole = refs
    first = 0
    for piece in pieces:
        whole[first : first + piece.shape[0]] = piece[...]
        first += piece.shape[0]


def join(pieces):
    spec = lambda s: pl.BlockSpec(s, lambda i: (0, 0, 0))
    shape = (sum(p.shape[0] for p in pieces), *pieces[0].shape[1:])
    return pl.pallas_call(
        join_kernel,
        out_shape=jax.ShapeDtypeStruct(shape, BF16),
        grid=(1,),
        in_specs=[spec(p.shape) for p in pieces],
        out_specs=spec(shape),
        compiler_params=pltpu.CompilerParams(vmem_limit_bytes=32 * 2**20),
        name="join",
    )(*pieces)


def order(core, shape, legs=(0, 1, 2)):
    deep, tall, wide = shape
    here = lax.axis_index("fsdp")
    z, y, x = here // (tall * wide), here // wide % tall, here % wide
    slot = jnp.arange(deep * tall * wide, dtype=jnp.int32)
    steps = {}
    for leg in legs:
        steps[leg] = slot % shape[leg]
        slot = slot // shape[leg]
    z = (z + steps[0]) % deep
    y = (y + jnp.where(core == 0, steps[1], steps[2])) % tall
    x = (x + jnp.where(core == 0, steps[2], steps[1])) % wide
    return (z * tall + y) * wide + x


def inverse(table):
    slots = jnp.arange(table.shape[0], dtype=jnp.int32)
    return jnp.sum(jnp.where(table[None, :] == slots[:, None], slots[None, :], 0), axis=1)


def half_of(array, side):
    width = array.shape[1] // 2
    return lax.dynamic_slice_in_dim(array, side * width, width, 1)


def joined(mine, theirs, core):
    first = jnp.where(core == 0, mine, theirs)
    second = jnp.where(core == 0, theirs, mine)
    return first, second


def reordered(small, table):
    slots = jnp.arange(table.shape[0], dtype=jnp.int32)
    chosen = (table[:, None] == slots[None, :]).astype(F32)
    flat = small.reshape(table.shape[0], -1)
    return jnp.dot(chosen, flat, precision=lax.Precision.HIGHEST).reshape(small.shape)


def shards(
    hidden_in,
    lengths,
    out_grad,
    query_matrix,
    query_offset,
    key_matrix,
    key_offset,
    value_matrix,
    value_offset,
    output_matrix,
    output_offset,
    first_gain,
    first_offset,
    up_matrix,
    up_offset,
    down_matrix,
    down_offset,
    second_gain,
    second_offset,
):
    count, width = hidden_in.shape
    half = width // 2
    rows = query_matrix.shape[0]
    parts = up_offset.shape[0] // rows
    core = lax.axis_index("dp")
    shape = sides(lax.axis_size("fsdp"))
    positions = math.prod(shape)
    table, other_table = order(core, shape), order(1 - core, shape)
    down_legs = (1, 0, 2)
    down_table, other_down_table = order(core, shape, down_legs), order(1 - core, shape, down_legs)
    direct = rows % 16 == 0
    place = jnp.reshape(core, (1,)).astype(jnp.int32)
    zero = jnp.zeros((1,), jnp.int32)
    own_order, their_order = (table, other_table) if direct else (zero, zero)
    own_down_order, their_down_order = (down_table, other_down_table) if direct else (zero, zero)
    down_rows = down_matrix.shape[0]

    def usable(pieces, places, cuts):
        if direct:
            return pieces
        blocks, parts, first = jnp.concatenate(pieces, axis=0), [], 0
        for cut in cuts:
            parts.append(picked(blocks[:, first : first + cut], inverse(places)).reshape(1, -1, blocks.shape[2]))
            first += cut
        return [jnp.concatenate(parts, axis=1)]

    def in_blocks(array, places):
        return array if direct else picked(array.reshape(positions, -1, array.shape[2]), places)

    vectors = (
        query_offset, key_offset, value_offset, output_offset, first_gain, first_offset,
        down_offset, second_gain, second_offset,
    )
    left = jnp.pad(jnp.stack(vectors), ((0, rows - len(vectors)), (0, 64 - rows)))
    right = jnp.pad(up_offset.reshape(parts, rows), ((0, rows - parts), (0, 64 - rows)))
    unit = pack(place, (query_matrix, key_matrix, value_matrix), jnp.concatenate([left, right], axis=1))
    attn_far = received(unit, 0, shape)
    other_lengths = swapped(lengths)
    down_unit = jnp.concatenate([half_of(down_matrix, core), half_of(output_matrix, core)], axis=0)[None]
    down_far = received(down_unit, 1, shape)
    other_in = swapped(hidden_in)
    tables, plan, _ = described(lengths[0], count)

    attn_far, up_matrix, other_lengths, down_far, other_in = staged(attn_far, up_matrix, other_lengths, down_far, other_in)
    attn_four = join([unit] + attn_far)
    attn_far = received(attn_four, 1, shape)
    down_two = join([down_unit] + down_far)
    down_far = received(down_two, 0, shape)
    other_tables, other_plan, _ = described(other_lengths[0], count)

    attn_far, attn_four, up_matrix = staged(attn_far, attn_four, up_matrix)
    attn_eight = join([attn_four] + attn_far)
    attn_far = received(attn_eight, 2, shape)
    up_unit = half_of(up_matrix, core)[None]

    attn_far, up_unit = staged(attn_far, up_unit)
    attn = [attn_eight] + attn_far
    small = jnp.concatenate([a[:, :, 3 * half :] for a in attn], axis=0).astype(F32)
    small = reordered(small, inverse(table))
    whole = small[:, : len(vectors), :rows].swapaxes(0, 1).reshape(len(vectors), width)
    up_bias = small[:, :parts, 64 : 64 + rows].reshape(1, -1)
    bias = lax.dynamic_slice_in_dim(whole[:3], core * half, half, 1).reshape(1, -1)
    vector_rows = jnp.pad(whole[3:], ((0, 2), (0, 0)))
    attn = usable(attn, table, (rows,))
    up_far = received(up_unit, 0, shape)
    other_q, other_k, other_v, other_norms = project(other_in, attn, own_order, bias, other_tables)

    down_far, up_far, other_q, hidden_in = staged(down_far, up_far, other_q, hidden_in)
    up_four = join([up_unit] + up_far)
    up_far = received(up_four, 1, shape)
    down_eight = join([down_two] + down_far)
    down_far = received(down_eight, 2, shape)
    other_mixed, other_lse = attend(other_plan, other_q, other_k, other_v, other_norms, other_tables[2])

    up_far, up_four, other_mixed, hidden_in = staged(up_far, up_four, other_mixed, hidden_in)
    up_eight = join([up_four] + up_far)
    up_far = received(up_eight, 2, shape)
    mixed_theirs = swapped(other_mixed)
    down_swapped = swapped(down_eight)
    q, k, v, norms = project(hidden_in, attn, own_order, bias, tables)

    down_far, down_swapped, mixed_theirs, q = staged(down_far, down_swapped, mixed_theirs, q)
    up_swapped = swapped(up_eight)
    down_swapped = [down_swapped] + [swapped(far) for far in down_far]
    mixed, lse = attend(plan, q, k, v, norms, tables[2])

    up_far, up_swapped, down_swapped, mixed, vector_rows, up_bias = staged(
        up_far, up_swapped, down_swapped, mixed, vector_rows, up_bias
    )
    up_swapped = [up_swapped] + [swapped(far) for far in up_far]
    up_weights = [usable([up_eight] + up_far, table, (rows,)), usable(up_swapped, other_table, (rows,))]
    down_weights = [
        usable([down_eight] + down_far, down_table, (down_rows, rows)),
        usable(down_swapped, other_down_table, (down_rows, rows)),
    ]
    (
        hidden_out, normed_low, activated, grad_two, grad_up, grad_one, grad_mine, grad_theirs, both_mixed, sums, up_sum,
    ) = middle(
        place, own_order, their_order, own_down_order, their_down_order, hidden_in, mixed, mixed_theirs, out_grad, tables[2],
        up_weights + down_weights, vector_rows, up_bias,
    )
    other_grad = swapped(grad_theirs)
    places = (place, own_order, their_order)
    slots_of = lambda vectors: vectors.reshape(-1, positions, rows).swapaxes(0, 1)
    left = jnp.pad(slots_of(sums[:6]), ((0, 0), (0, rows - 6), (0, 64 - rows)))
    right = jnp.pad(up_sum.reshape(positions, parts, rows), ((0, 0), (0, rows - parts), (0, 64 - rows)))
    slot_sums = jnp.concatenate([left, right], axis=2)

    def with_slots(pair, slots):
        if direct:
            return pair
        return [
            jnp.concatenate([in_blocks(p, t), reordered(slots, t).astype(BF16)], axis=2)
            for p, t in zip(pair, (table, other_table))
        ]

    output_pair = outer(*places, both_mixed, grad_one, 1, (slot_sums.astype(BF16),) if direct else ())
    output_pair = with_slots(output_pair, slot_sums)

    output_pair, grad_up = staged(output_pair, grad_up)
    output_arrived = swapped(output_pair[1])
    up_pair = outer(*places, normed_low, grad_up, 1)

    up_pair, output_arrived, activated = staged(up_pair, output_arrived, activated)
    up_arrived = swapped(in_blocks(up_pair[1], other_table))
    down_pair = outer(*places, activated, grad_two, 0)

    down_pair, up_arrived, other_grad = staged(down_pair, up_arrived, other_grad)
    up_total = [summed([in_blocks(up_pair[0], table), up_arrived]), summed([output_pair[0], output_arrived])]
    up_sent = sent(jnp.concatenate(up_total, axis=2), 2, shape)
    down_arrived = swapped(in_blocks(down_pair[1], other_table))
    other_d = attend_back(other_plan, other_q, other_k, other_v, other_lse, other_mixed, other_grad, other_tables)

    up_sent, down_arrived, other_d, grad_mine = staged(up_sent, down_arrived, other_d, grad_mine)
    down_sent = sent(summed([in_blocks(down_pair[0], table), down_arrived]), 2, shape)
    up_sent = sent(summed(up_sent), 1, shape)
    own_d = attend_back(plan, q, k, v, lse, mixed, grad_mine, tables)

    up_sent, down_sent, own_d = staged(up_sent, down_sent, own_d)
    up_sent = sent(summed(up_sent), 0, shape)
    down_sent = sent(summed(down_sent), 1, shape)
    matrices, qkv_sums = qkv_grad(place, own_order, hidden_in, other_in, own_d, other_d, direct)

    down_sent, matrices, other_d = staged(down_sent, matrices, other_d)
    if not direct:
        own_sums = jnp.zeros((3, width), F32)
        own_sums = lax.dynamic_update_slice_in_dim(own_sums, qkv_sums[:, 0], core * half, 1)
        own_sums = jnp.pad(slots_of(own_sums), ((0, 0), (0, rows - 3), (0, 128 - rows)))
        matrices = jnp.concatenate([in_blocks(matrices, table), reordered(own_sums, table).astype(BF16)], axis=2)
    matrices_sent = sent(matrices, 2, shape)
    down_sent = sent(summed(down_sent), 0, shape)
    sent_grad = input_part(own_order, other_d, attn, width)

    matrices_sent, up_sent, sent_grad = staged(matrices_sent, up_sent, sent_grad)
    matrices_sent = sent(summed(matrices_sent), 1, shape)
    up_done = summed(up_sent)[0]
    up_other = swapped(up_done)
    other_part = swapped(sent_grad)

    matrices_sent, down_sent, up_other, other_part, own_d = staged(matrices_sent, down_sent, up_other, other_part, own_d)
    matrices_sent = sent(summed(matrices_sent), 0, shape)
    down_done = summed(down_sent)[0]
    down_other = swapped(down_done)
    input_grad = input_part(own_order, own_d, attn, width, other_part, grad_one)

    matrices_sent, down_other, input_grad = staged(matrices_sent, down_other, input_grad)
    matrices_done = summed(matrices_sent)[0]

    up_first, up_second = joined(up_done, up_other, core)
    down_first, down_second = joined(down_done, down_other, core)
    query_grad, key_grad, value_grad, offsets = finish(place, matrices_done, swapped(matrices_done))
    wide = lambda a, b: jnp.concatenate([a, b], axis=1).astype(F32)
    hidden = up_matrix.shape[1] // 2
    others = up_first[:, hidden + half :].astype(F32)
    columns = slice(hidden, hidden + half)
    return (
        hidden_out,
        input_grad,
        query_grad,
        offsets[0, :rows],
        key_grad,
        offsets[1, :rows],
        value_grad,
        offsets[2, :rows],
        wide(up_first[:, columns], up_second[:, columns]),
        others[0, :rows],
        others[1, :rows],
        others[2, :rows],
        wide(up_first[:, :hidden], up_second[:, :hidden]),
        others[:parts, 64 : 64 + rows].reshape(-1),
        wide(down_first, down_second),
        others[3, :rows],
        others[4, :rows],
        others[5, :rows],
    )


def solution(mesh):
    placed = (
        P(("dp", "fsdp"), None),
        P(("dp", "fsdp"), None),
        P(("dp", "fsdp"), None),
        P("fsdp", None),
        P("fsdp"),
        P("fsdp", None),
        P("fsdp"),
        P("fsdp", None),
        P("fsdp"),
        P("fsdp", None),
        P("fsdp"),
        P("fsdp"),
        P("fsdp"),
        P("fsdp", None),
        P("fsdp"),
        P("fsdp", None),
        P("fsdp"),
        P("fsdp"),
        P("fsdp"),
    )
    return jax.shard_map(
        shards,
        mesh=mesh,
        in_specs=placed,
        out_specs=(
            P(("dp", "fsdp"), None),
            P(("dp", "fsdp"), None),
            P("fsdp", None),
            P("fsdp"),
            P("fsdp", None),
            P("fsdp"),
            P("fsdp", None),
            P("fsdp"),
            P("fsdp", None),
            P("fsdp"),
            P("fsdp"),
            P("fsdp"),
            P("fsdp", None),
            P("fsdp"),
            P("fsdp", None),
            P("fsdp"),
            P("fsdp"),
            P("fsdp"),
        ),
        check_vma=False,
    )
```

```python
import math
from functools import partial
import jax, jax.numpy as jnp
from jax import lax
from jax.experimental import pallas as pl
from jax.experimental.pallas import tpu as pltpu
from jax.sharding import PartitionSpec as P

HEAD_DIM = 64
EPSILON = 1e-12
FAR = -1e30
LOG2E = 1.4426950408889634
BLOCK = 256
SAFE = 105.0
F32 = jnp.float32
BF16 = jnp.bfloat16
VMEM_LIMIT = 58 * 2**20


def dot(a, b):
    return jnp.dot(a, b, preferred_element_type=F32)


def dot_right(a, b):
    return lax.dot_general(a, b, (((1,), (1,)), ((), ())), preferred_element_type=F32)


def dot_rows(a, b):
    return lax.dot_general(a, b, (((0,), (0,)), ((), ())), preferred_element_type=F32)


def turned(value, cosines, sines, even_lane):
    partner = jnp.where(even_lane, -pltpu.roll(value, 127, 1), pltpu.roll(value, 1, 1))
    return value * cosines + partner * sines


def lse_lane(head):
    return (HEAD_DIM if head % 2 == 0 else 0) + 8 + 3 * head


def delta_lane(head, heads):
    return lse_lane(head) + 3 * heads


def lanes_of(rows):
    return lax.broadcasted_iota(jnp.int32, (rows, 128), 1)


def load_rows(table_ref, source_refs, target_ref, sem):
    copies = []
    for source in source_refs:
        rows = source.shape[1]
        for i in range(source.shape[0]):
            n = len(copies)
            at = pl.ds(pl.multiple_of(table_ref[n] * rows, math.gcd(rows, 256)), rows)
            copies.append(pltpu.make_async_copy(source.at[i, :, pl.ds(0, target_ref.shape[1])], target_ref.at[at], sem.at[n]))
    for c in copies:
        c.start()
    return copies


def project_kernel(table_ref, x_ref, bias_ref, cos_ref, sin_ref, extq_ref, extk_ref, *refs):
    *w_refs, q_ref, k_ref, v_ref, norm_ref, w_s, sem = refs
    step = pl.program_id(0)

    @pl.when(step == 0)
    def _():
        for c in load_rows(table_ref, w_refs, w_s, sem):
            c.wait()
        norm_ref[...] = jnp.zeros_like(norm_ref)

    heads = q_ref.shape[0]
    width = heads * HEAD_DIM
    lane = lanes_of(BLOCK)
    first_half = lane < HEAD_DIM
    even_lane = lax.rem(lane, 2) == 0
    y = dot(x_ref[...], w_s[...]) + bias_ref[...]
    cosines, sines = cos_ref[...], sin_ref[...]
    extq, extk = extq_ref[...].astype(F32), extk_ref[...].astype(F32)
    row = lax.broadcasted_iota(jnp.int32, (128, BLOCK), 0)
    squares = []
    for p in range(width // 128):
        at = slice(p * 128, p * 128 + 128)
        q = turned(y[:, at], cosines, sines, even_lane) * (HEAD_DIM**-0.5 * LOG2E)
        k = turned(y[:, width + p * 128 : width + p * 128 + 128], cosines, sines, even_lane)
        v = y[:, 2 * width + p * 128 : 2 * width + p * 128 + 128].T
        squares.append(((q * q).astype(BF16), (k * k).astype(BF16)))
        for h in (2 * p, 2 * p + 1):
            own = first_half if h % 2 == 0 else jnp.logical_not(first_half)
            start = lse_lane(h)
            ones = (lane >= start) & (lane < start + 3)
            q_ref[h] = jnp.where(own, q, extq).astype(BF16)
            k_ref[h] = jnp.where(own, k, jnp.where(ones, 1.0, extk)).astype(BF16)
            start = delta_lane(h, heads)
            ones = (row >= start) & (row < start + 3)
            own = row < HEAD_DIM if h % 2 == 0 else row >= HEAD_DIM
            v_ref[h] = jnp.where(own, v, jnp.where(ones, 1.0, 0.0)).astype(BF16)
    column = lax.broadcasted_iota(jnp.int32, (width, 128), 0) // HEAD_DIM
    picks = jnp.where(column == lax.broadcasted_iota(jnp.int32, (width, 128), 1), 1.0, 0.0).astype(BF16)
    sums = [dot(jnp.concatenate([a[n] for a in squares], axis=1), picks) for n in range(2)]
    most = [jnp.max(t, axis=0, keepdims=True) for t in sums]
    norm_ref[...] = jnp.maximum(norm_ref[...], jnp.concatenate(most, axis=1))


def project(x, weights, table, bias, tables):
    count, width = x.shape
    blocks = table.shape[0]
    total = bias.shape[1]
    heads = total // (3 * HEAD_DIM)
    cosines, sines, extq, extk = tables
    row = lambda a: pl.BlockSpec((BLOCK, a.shape[1]), lambda i, t: (i, 0))
    head = pl.BlockSpec((heads, BLOCK, 128), lambda i, t: (0, i, 0))
    shape = jax.ShapeDtypeStruct((heads, count, 128), BF16)
    return pl.pallas_call(
        project_kernel,
        out_shape=(shape, shape, jax.ShapeDtypeStruct((heads, 128, count), BF16), jax.ShapeDtypeStruct((8, 256), F32)),
        grid_spec=pltpu.PrefetchScalarGridSpec(
            num_scalar_prefetch=1,
            grid=(count // BLOCK,),
            in_specs=[
                row(x), pl.BlockSpec((1, total), lambda i, t: (0, 0)), row(cosines), row(sines), row(extq), row(extk),
            ]
            + [pl.BlockSpec(memory_space=pl.ANY)] * len(weights),
            out_specs=[head, head, pl.BlockSpec((heads, 128, BLOCK), lambda i, t: (0, 0, i)), pl.BlockSpec((8, 256), lambda i, t: (0, 0))],
            scratch_shapes=[pltpu.VMEM((width, total), BF16), pltpu.SemaphoreType.DMA((blocks,))],
        ),
        compiler_params=pltpu.CompilerParams(vmem_limit_bytes=VMEM_LIMIT),
        cost_estimate=pl.CostEstimate(flops=10**11, bytes_accessed=1000, transcendentals=0),
        name="project",
    )(table, x, bias, cosines, sines, extq, extk, *weights)


def three_parts(value):
    high = value.astype(BF16).astype(F32)
    rest = value - high
    middle = rest.astype(BF16).astype(F32)
    return high, middle, rest - middle


def attend_kernel(plan_ref, q_ref, k_ref, v_ref, norm_ref, extq_ref, mixed_ref, lse_ref):
    step = pl.program_id(0)
    heads, count, _ = k_ref.shape
    blocks = count // BLOCK
    first, need = plan_ref[2 * step], plan_ref[2 * step + 1]
    safe = jnp.max(norm_ref[:, :128]) * jnp.max(norm_ref[:, 128:]) < SAFE * SAFE
    lane = lanes_of(BLOCK)
    start_lane, any_lane = lane < 0, lane < 0
    for h in range(heads):
        start_lane = start_lane | (lane == lse_lane(h))
        any_lane = any_lane | ((lane >= lse_lane(h)) & (lane < lse_lane(h) + 3))
    pad = extq_ref[:, HEAD_DIM + 4 : HEAD_DIM + 5].astype(F32) > 0.5

    def rows_of(c, plain):
        keys = pl.ds(pl.multiple_of(jnp.minimum(first, blocks - c) * BLOCK, BLOCK), c * BLOCK)
        scores = [dot_right(k_ref[h, keys, :], q_ref[h]) for h in range(heads)]
        outs = []
        packs = [jnp.zeros((24, BLOCK), F32)] * 2
        row = lax.broadcasted_iota(jnp.int32, (24, BLOCK), 0)
        for h in range(heads):
            s = scores[h]
            if not plain:
                peak = jnp.max(s, axis=0, keepdims=True)
                s = s - peak
            o = dot(v_ref[h, :, keys], jnp.exp2(s).astype(BF16))
            ones = delta_lane(h, heads)
            total = o[ones : ones + 1, :]
            outs.append((o[:HEAD_DIM] if h % 2 == 0 else o[HEAD_DIM:]) / total)
            lse = -jnp.log2(total)
            if not plain:
                lse = lse - peak
            for j, part in enumerate(three_parts(lse)):
                packs[h % 2] = jnp.where(row == 3 * h + j, part, packs[h % 2])
        mixed_ref[...] = jnp.concatenate(outs, axis=0).T.astype(BF16)
        gap = lambda n: jnp.zeros((n, BLOCK), F32)
        packed = jnp.concatenate([gap(8), packs[1], gap(40), packs[0], gap(32)], axis=0).T
        lse_ref[...] = jnp.where(pad & any_lane, jnp.where(start_lane, FAR, 0.0), packed).astype(BF16)

    @pl.when(need == 0)
    def _():
        mixed_ref[...] = jnp.zeros_like(mixed_ref)
        lse_ref[...] = jnp.where(start_lane, FAR, 0.0).astype(BF16)

    for c in range(1, blocks + 1):
        pl.when(safe & (need == c))(partial(rows_of, c, True))
    pl.when(jnp.logical_not(safe) & (need > 0))(partial(rows_of, blocks, False))


def attend(plan, q, k, v, norms, extq):
    heads, count, _ = q.shape
    whole = lambda a: pl.BlockSpec(a.shape, lambda i, p: (0,) * a.ndim)
    return pl.pallas_call(
        attend_kernel,
        out_shape=(jax.ShapeDtypeStruct((count, heads * HEAD_DIM), BF16), jax.ShapeDtypeStruct((count, 128), BF16)),
        grid_spec=pltpu.PrefetchScalarGridSpec(
            num_scalar_prefetch=1,
            grid=(count // BLOCK,),
            in_specs=[
                pl.BlockSpec((heads, BLOCK, 128), lambda i, p: (0, i, 0)), whole(k), whole(v), whole(norms),
                pl.BlockSpec((BLOCK, 128), lambda i, p: (i, 0)),
            ],
            out_specs=[pl.BlockSpec((BLOCK, heads * HEAD_DIM), lambda i, p: (i, 0)), pl.BlockSpec((BLOCK, 128), lambda i, p: (i, 0))],
        ),
        compiler_params=pltpu.CompilerParams(vmem_limit_bytes=36 * 2**20),
        cost_estimate=pl.CostEstimate(flops=10**11, bytes_accessed=1000, transcendentals=0),
        name="attend",
    )(plan, q, k, v, norms, extq)


def attend_back_kernel(plan_ref, q_ref, k_ref, v_ref, lse_ref, mixed_ref, grad_ref, cos_ref, sin_ref, cos_all, sin_all,
                       d_ref, dk_s, dv_s):
    step = pl.program_id(0)
    heads, count, _ = k_ref.shape
    width = heads * HEAD_DIM
    blocks = count // BLOCK
    first, need = plan_ref[2 * step], plan_ref[2 * step + 1]
    lane = lanes_of(BLOCK)
    first_half = lane < HEAD_DIM
    even_lane = lax.rem(lane, 2) == 0
    scale = HEAD_DIM**-0.5

    @pl.when(step == 0)
    def _():
        dk_s[...] = jnp.zeros_like(dk_s)
        dv_s[...] = jnp.zeros_like(dv_s)

    def rows_of(c):
        keys = pl.ds(pl.multiple_of(jnp.minimum(first, blocks - c) * BLOCK, BLOCK), c * BLOCK)
        grad = grad_ref[...].astype(F32)
        product = grad * mixed_ref[...].astype(F32)
        high = product.astype(BF16)
        low = (product - high.astype(F32)).astype(BF16)
        column = lax.broadcasted_iota(jnp.int32, (width, 128), 0) // HEAD_DIM
        slot = lax.broadcasted_iota(jnp.int32, (width, 128), 1)
        slot = slot - jnp.where(lax.rem(column, 2) == 0, delta_lane(0, heads), delta_lane(0, heads) - HEAD_DIM)
        picks = jnp.where((slot >= 3 * column) & (slot < 3 * column + 3), 1.0, 0.0).astype(BF16)
        delta = three_parts(-(dot(high, picks) + dot(low, picks)))
        inner = jnp.where(first_half, lane, lane - HEAD_DIM)
        part = lax.rem(inner + 1, 3)
        delta = jnp.where(part == 0, delta[0], jnp.where(part == 1, delta[1], delta[2]))
        extra = jnp.where(inner < 8 + 3 * heads, lse_ref[...].astype(F32), delta)
        dqs = []
        for p in range(width // 128):
            at = slice(p * 128, p * 128 + 128)
            pair = grad[:, at]
            pair_t = pair.T.astype(BF16)
            qs = [q_ref[2 * p].astype(F32), q_ref[2 * p + 1].astype(F32)]
            q_t = jnp.where(first_half, qs[0], qs[1]).T.astype(BF16)
            both = []
            for n in range(2):
                h = 2 * p + n
                own = first_half if n == 0 else jnp.logical_not(first_half)
                side = slice(n * HEAD_DIM, n * HEAD_DIM + HEAD_DIM)
                g = jnp.where(own, pair, extra).astype(BF16)
                q = jnp.where(own | (inner < 8), qs[n], extra).astype(BF16)
                k = k_ref[h, keys, :]
                probs = jnp.exp2(dot_right(q, k))
                shifted = dot(g, v_ref[h, :, keys])
                grads = (probs * shifted).astype(BF16)
                dv_s[h, :, keys] += dot(pair_t[side], probs.astype(BF16))
                dk_s[h, :, keys] += dot(q_t[side], grads)
                both.append(dot(grads, k))
            dq = jnp.where(first_half, both[0], both[1]) * scale
            d_ref[pl.ds(pl.multiple_of(step * BLOCK, BLOCK), BLOCK), at] = turned(dq, cos_ref[...], -sin_ref[...], even_lane).astype(BF16)

    @pl.when(need == 0)
    def _():
        d_ref[pl.ds(pl.multiple_of(step * BLOCK, BLOCK), BLOCK), :width] = jnp.zeros((BLOCK, width), BF16)

    for c in range(1, blocks + 1):
        pl.when(need == c)(partial(rows_of, c))

    @pl.when(step == blocks - 1)
    def _():
        for p in range(width // 128):
            for r in range(blocks):
                at = slice(r * BLOCK, r * BLOCK + BLOCK)
                dv = jnp.concatenate([dv_s[2 * p, :, at], dv_s[2 * p + 1, :, at]], axis=0).T
                dk = jnp.concatenate([dk_s[2 * p, :, at], dk_s[2 * p + 1, :, at]], axis=0).T * (1.0 / LOG2E)
                d_ref[at, 2 * width + p * 128 : 2 * width + p * 128 + 128] = dv.astype(BF16)
                d_ref[at, width + p * 128 : width + p * 128 + 128] = turned(dk, cos_all[at, :], -sin_all[at, :], even_lane).astype(BF16)


def attend_back(plan, q, k, v, lse, mixed, grad, tables):
    heads, count, _ = q.shape
    width = heads * HEAD_DIM
    cosines, sines = tables[:2]
    whole = lambda a: pl.BlockSpec(a.shape, lambda i, p: (0,) * a.ndim)
    row = lambda a: pl.BlockSpec((BLOCK, a.shape[1]), lambda i, p: (i, 0))
    shape = jax.ShapeDtypeStruct((count, 3 * width), BF16)
    return pl.pallas_call(
        attend_back_kernel,
        out_shape=shape,
        grid_spec=pltpu.PrefetchScalarGridSpec(
            num_scalar_prefetch=1,
            grid=(count // BLOCK,),
            in_specs=[
                pl.BlockSpec((heads, BLOCK, 128), lambda i, p: (0, i, 0)), whole(k), whole(v), row(lse), row(mixed), row(grad),
                row(cosines), row(sines), whole(cosines), whole(sines),
            ],
            out_specs=pl.BlockSpec((count, 3 * width), lambda i, p: (0, 0)),
            scratch_shapes=[pltpu.VMEM((heads, HEAD_DIM, count), F32)] * 2,
        ),
        compiler_params=pltpu.CompilerParams(vmem_limit_bytes=40 * 2**20),
        cost_estimate=pl.CostEstimate(flops=10**11, bytes_accessed=1000, transcendentals=0),
        name="attend_back",
    )(plan, q, k, v, lse, mixed, grad, cosines, sines, cosines, sines)


def described(lengths, count):
    total = lengths.shape[0]
    index = jnp.arange(total)
    ends = jnp.sum(jnp.where(index[:, None] >= index[None, :], lengths[None, :], 0), axis=1)
    starts = ends - lengths
    slots = jnp.arange(count, dtype=jnp.int32)
    segment = jnp.sum((slots[:, None] >= ends[None, :]).astype(jnp.int32), axis=1)
    owner = segment[:, None] == jnp.arange(total, dtype=jnp.int32)[None, :]
    begin = jnp.sum(jnp.where(owner, starts[None, :], 0), axis=1)
    position = (slots - begin).astype(F32)
    lane = jnp.arange(128, dtype=jnp.int32)
    inverse = jnp.power(10000.0, -2.0 * (lane % HEAD_DIM // 2).astype(F32) / HEAD_DIM)
    angle = position[:, None] * inverse[None, :]
    cosines, sines = jnp.cos(angle), jnp.sin(angle)
    code = (lane % HEAD_DIM)[None, :]
    extq = jnp.where(code == segment[:, None], 1.0, 0.0).astype(BF16)
    extk = jnp.where((code < total) & (code != segment[:, None]), FAR, 0.0).astype(BF16)
    filled = jnp.sum(lengths)
    opens = jnp.arange(count // BLOCK, dtype=jnp.int32) * BLOCK
    closes = jnp.minimum(opens + BLOCK, filled)
    low = jnp.max(jnp.where(ends[None, :] <= opens[:, None], ends[None, :], 0), axis=1)
    high = jnp.min(jnp.where(ends[None, :] >= closes[:, None], ends[None, :], filled), axis=1)
    first = low // BLOCK
    need = jnp.where(opens < filled, (high + BLOCK - 1) // BLOCK - first, 0)
    plan = jnp.stack([first, need], axis=1).reshape(-1)
    valid = (segment < total).astype(F32)
    return (cosines, sines, extq, extk), plan, valid


def normed_of(value):
    center = value - jnp.mean(value, axis=1, keepdims=True)
    scale = lax.rsqrt(jnp.mean(center * center, axis=1, keepdims=True) + EPSILON)
    return center * scale, scale


def norm_back(grad, gain, normed, scale):
    scaled = grad * gain
    return (scaled - jnp.mean(scaled, axis=1, keepdims=True) - normed * jnp.mean(scaled * normed, axis=1, keepdims=True)) * scale


def gelu_and_slope(value):
    bell = jnp.exp2(value * value * (-0.5 * LOG2E))
    t = 1.0 / (1.0 + (0.3275911 * 0.5**0.5) * jnp.abs(value))
    tail = t * (0.5 * 0.254829592 + t * (0.5 * -0.284496736 + t * (0.5 * 1.421413741 + t * (0.5 * -1.453152027 + t * (0.5 * 1.061405429)))))
    tail = tail * bell
    below = jnp.where(value < 0.0, tail, 1.0 - tail)
    return value * below, below + value * bell * (2.0 * math.pi) ** -0.5


CHUNK = 1024
MIDDLE = 512


def place_halves(place_ref, orders, sources, first, rows, target_ref, sem):
    copies = []
    for n, (order, refs) in enumerate(zip(orders, sources)):
        side = place_ref[0] if n == 0 else 1 - place_ref[0]
        blocks = 0
        for ref in refs:
            width = ref.shape[2]
            for i in range(ref.shape[0]):
                at = pl.ds(pl.multiple_of(order[blocks] * rows, math.gcd(rows, 256)), rows)
                columns = pl.ds(pl.multiple_of(side * width, 128), width)
                copies.append(pltpu.make_async_copy(ref.at[i, pl.ds(first, rows)], target_ref.at[at, columns], sem.at[len(copies)]))
                blocks += 1
    return copies


def middle_kernel(counts, place_ref, table_ref, other_ref, down_table_ref, other_down_ref, x_ref, mine_ref, theirs_ref, og_ref, valid_ref, vec_ref, bu_ref, *refs):
    weight_refs, refs = refs[: sum(counts)], refs[sum(counts) :]
    (
        out_ref, low_ref, act_ref, gtwo_ref, gup_ref, gone_ref, gm_mine_ref, gm_theirs_ref, mixed_ref, sums_ref, upsum_ref,
        wo, wu, wd, mixed_s, slope_s, gm_s, so, su, sd,
    ) = refs
    step = pl.program_id(0)
    sequences = 4
    core = place_ref[0]
    half = mine_ref.shape[1]
    width = 2 * half
    hidden = bu_ref.shape[1]
    lists = [weight_refs[sum(counts[:n]) : sum(counts[: n + 1])] for n in range(4)]
    orders, down_orders = (table_ref, other_ref), (down_table_ref, other_down_ref)
    blocks = table_ref.shape[0]
    down_rows, rows = hidden // blocks, width // blocks
    o_copies = place_halves(place_ref, down_orders, lists[2:], down_rows, rows, wo, so)
    u_copies = place_halves(place_ref, orders, lists[:2], 0, rows, wu, su)
    d_copies = place_halves(place_ref, down_orders, lists[2:], 0, down_rows, wd, sd)

    @pl.when(step == 0)
    def _():
        for c in o_copies + u_copies + d_copies:
            c.start()
        sums_ref[...] = jnp.zeros_like(sums_ref)
        upsum_ref[...] = jnp.zeros_like(upsum_ref)
        for c in o_copies:
            c.wait()

    vec = lambda i: vec_ref[i : i + 1, :]
    total = lambda v: jnp.sum(v, axis=0, keepdims=True)
    mine = pl.ds(pl.multiple_of(core * half, 128), half)
    theirs = pl.ds(pl.multiple_of((1 - core) * half, 128), half)
    mixed_s[:, mine] = mine_ref[...]
    mixed_s[:, theirs] = theirs_ref[...]
    mixed_ref[...] = mixed_s[...]
    groups = [slice(g * BLOCK, g * BLOCK + BLOCK) for g in range(x_ref.shape[0] // BLOCK)]
    chunks = [slice(c * CHUNK, c * CHUNK + CHUNK) for c in range(hidden // CHUNK)]
    firsts = [x_ref[g, :].astype(F32) + (dot(mixed_s[g, :], wo[...]) + vec(0)) for g in groups]
    ones = [normed_of(f) for f in firsts]
    normeds = [n * vec(1) + vec(2) for n, _ in ones]
    lows = [n.astype(BF16) for n in normeds]
    for g, low in zip(groups, lows):
        low_ref[g, :] = low

    @pl.when(step == 0)
    def _():
        for c in u_copies:
            c.wait()

    seconds = [n + vec(3) for n in normeds]
    aheads = [dot(low, wu[:, chunks[0]]) for low in lows]
    for c, at in enumerate(chunks):
        for n, g in enumerate(groups):
            upward = aheads[n] + bu_ref[:, at]
            if c + 1 < len(chunks):
                aheads[n] = dot(lows[n], wu[:, chunks[c + 1]])
            activated, slope = gelu_and_slope(upward)
            activated = activated.astype(BF16)
            act_ref[g, at] = activated
            slope_s[g, at] = slope.astype(BF16)
            if c == n == 0:

                @pl.when(step == 0)
                def _():
                    for copy in d_copies:
                        copy.wait()

            seconds[n] = seconds[n] + dot(activated, wd[at, :])
    sums = [0.0] * 6
    twos, grads = [], []
    for n, g in enumerate(groups):
        normal, scale = normed_of(seconds[n])
        valid = 1.0 - valid_ref[g, sequences : sequences + 1].astype(F32)
        out_ref[g, :] = (valid * (normal * vec(4) + vec(5))).astype(BF16)
        grad = og_ref[g, :].astype(F32) * valid
        grad_second = norm_back(grad, vec(4), normal, scale)
        grad_two = grad_second.astype(BF16)
        gtwo_ref[g, :] = grad_two
        sums[4] += total(grad * normal)
        sums[5] += total(grad)
        sums[3] += total(grad_two.astype(F32))
        twos.append(grad_two)
        grads.append(grad_second)
    aheads = [dot_right(two, wd[chunks[0], :]) for two in twos]
    for c, at in enumerate(chunks):
        for n, g in enumerate(groups):
            now = aheads[n]
            if c + 1 < len(chunks):
                aheads[n] = dot_right(twos[n], wd[chunks[c + 1], :])
            grad_up = (now * slope_s[g, at].astype(F32)).astype(BF16)
            gup_ref[g, at] = grad_up
            upsum_ref[:, at] += total(grad_up.astype(F32))
            grads[n] = grads[n] + dot_right(grad_up, wu[:, at])
    for n, g in enumerate(groups):
        normal, scale = ones[n]
        sums[1] += total(grads[n] * normal)
        sums[2] += total(grads[n])
        grad_one = norm_back(grads[n], vec(1), normal, scale).astype(BF16)
        gone_ref[g, :] = grad_one
        sums[0] += total(grad_one.astype(F32))
        gm_s[g, :] = dot_right(grad_one, wo[...]).astype(BF16)
    for i in range(6):
        sums_ref[i : i + 1, :] += sums[i]
    gm_mine_ref[...] = gm_s[:, mine]
    gm_theirs_ref[...] = gm_s[:, theirs]


def middle(place, table, other, down_table, other_down, x, mine, theirs, out_grad, valid, weights, vectors, up_bias):
    count, width = x.shape
    half = width // 2
    hidden = up_bias.shape[1]
    blocks = table.shape[0]
    row = lambda a: pl.BlockSpec((MIDDLE, a.shape[1]), lambda i, *_: (i, 0))
    rows_of = lambda n: pl.BlockSpec((MIDDLE, n), lambda i, *_: (i, 0))
    whole = lambda a: pl.BlockSpec(a.shape, lambda i, *_: (0, 0))
    anywhere = pl.BlockSpec(memory_space=pl.ANY)
    shape = lambda n: jax.ShapeDtypeStruct((count, n), BF16)
    sums, upsum = jax.ShapeDtypeStruct((8, width), F32), jax.ShapeDtypeStruct((1, hidden), F32)
    return pl.pallas_call(
        partial(middle_kernel, tuple(map(len, weights))),
        out_shape=(shape(width), shape(width), shape(hidden), shape(width), shape(hidden), shape(width), shape(half), shape(half), shape(width), sums, upsum),
        grid_spec=pltpu.PrefetchScalarGridSpec(
            num_scalar_prefetch=5,
            grid=(count // MIDDLE,),
            in_specs=[row(x), row(mine), row(theirs), row(out_grad), row(valid), whole(vectors), whole(up_bias)] + [anywhere] * sum(map(len, weights)),
            out_specs=[rows_of(width), rows_of(width), rows_of(hidden), rows_of(width), rows_of(hidden), rows_of(width), rows_of(half), rows_of(half), rows_of(width), whole(sums), whole(upsum)],
            scratch_shapes=[
                pltpu.VMEM((width, width), BF16), pltpu.VMEM((width, hidden), BF16), pltpu.VMEM((hidden, width), BF16),
                pltpu.VMEM((MIDDLE, width), BF16), pltpu.VMEM((MIDDLE, hidden), BF16), pltpu.VMEM((MIDDLE, width), BF16),
            ] + [pltpu.SemaphoreType.DMA((2 * blocks,))] * 3,
        ),
        compiler_params=pltpu.CompilerParams(vmem_limit_bytes=VMEM_LIMIT),
        cost_estimate=pl.CostEstimate(flops=10**11, bytes_accessed=1000, transcendentals=0),
        name="middle",
    )(place, table, other, down_table, other_down, x, mine, theirs, out_grad, valid, vectors, up_bias, *(w for group in weights for w in group))


def outer_kernel(split, extra, place_ref, table_ref, other_ref, left_ref, right_ref, *refs):
    slots_ref, (mine_ref, theirs_ref, total_s, sem, slot_sem) = (refs[0] if extra else None), refs[-5:]
    step = pl.program_id(0)
    steps = pl.num_programs(0)
    blocks, block_rows, width = mine_ref.shape
    width -= 128 * extra
    columns = 2 * width

    def slot_copies():
        return [
            pltpu.make_async_copy(slots_ref.at[order[i]], target.at[i, :, pl.ds(width, 128)], slot_sem.at[n * blocks + i])
            for n, (order, target) in enumerate(((table_ref, mine_ref), (other_ref, theirs_ref)))
            for i in range(blocks)
        ]

    if extra:

        @pl.when(step == 0)
        def _():
            for c in slot_copies():
                c.start()

    product = dot_rows(left_ref[...], right_ref[...]).astype(BF16)
    if split:
        total_s[:, pl.ds(pl.multiple_of(step * product.shape[1], 128), product.shape[1])] = product
    else:
        total_s[pl.ds(pl.multiple_of(step * product.shape[0], 256), product.shape[0]), :] = product

    def copies(first, count):
        made = []
        for n, (order, target) in enumerate(((other_ref, theirs_ref), (table_ref, mine_ref))):
            side = 1 - place_ref[0] if n == 0 else place_ref[0]
            for i in range(blocks):
                at = pl.ds(pl.multiple_of(order[i] * block_rows, math.gcd(block_rows, 256)), block_rows)
                source = total_s.at[at, pl.ds(pl.multiple_of(side * width + first, 128), count)]
                made.append(pltpu.make_async_copy(source, target.at[i, :, pl.ds(first, count)], sem.at[n * blocks + i]))
        return made

    @pl.when(step == steps - 1)
    def _():
        for c in copies(0, width):
            c.start()
        for c in copies(0, width):
            c.wait()
        if extra:
            for c in slot_copies():
                c.wait()


def outer(place, table, other, left, right, split, slots=()):
    count, rows = left.shape
    columns = right.shape[1]
    blocks = table.shape[0]
    extra = len(slots)
    shape = jax.ShapeDtypeStruct((blocks, rows // blocks, columns // 2 + 128 * extra), BF16)
    anywhere = pl.BlockSpec(memory_space=pl.ANY)
    if split:
        steps = max(1, columns // 768)
        specs = [pl.BlockSpec((count, rows), lambda i, *_: (0, 0)), pl.BlockSpec((count, columns // steps), lambda i, *_: (0, i))]
    else:
        steps = max(1, rows // 768)
        specs = [pl.BlockSpec((count, rows // steps), lambda i, *_: (0, i)), pl.BlockSpec((count, columns), lambda i, *_: (0, 0))]
    return pl.pallas_call(
        partial(outer_kernel, split, extra),
        out_shape=(shape, shape),
        grid_spec=pltpu.PrefetchScalarGridSpec(
            num_scalar_prefetch=3,
            grid=(steps,),
            in_specs=specs + [pl.BlockSpec(s.shape, lambda i, *_: (0, 0, 0)) for s in slots],
            out_specs=[anywhere, anywhere],
            scratch_shapes=[pltpu.VMEM((rows, columns), BF16), pltpu.SemaphoreType.DMA((2 * blocks,)), pltpu.SemaphoreType.DMA((2 * blocks,))],
        ),
        compiler_params=pltpu.CompilerParams(vmem_limit_bytes=28 * 2**20),
        cost_estimate=pl.CostEstimate(flops=10**11, bytes_accessed=1000, transcendentals=0),
        name="outer",
    )(place, table, other, left, right, *slots)


def qkv_grad_kernel(slotted, place_ref, table_ref, own_ref, other_ref, d_ref, dother_ref, out_ref, sums_ref, total_s, sums_s, slots_s, sem, slot_sem):
    step = pl.program_id(0)
    product = (dot_rows(own_ref[...], d_ref[...]) + dot_rows(other_ref[...], dother_ref[...])).astype(BF16)
    ones = jnp.ones((8, own_ref.shape[0]), BF16)
    sums_s[step] = dot(ones, d_ref[...]) + dot(ones, dother_ref[...])
    columns = product.shape[1]
    total_s[:, pl.ds(pl.multiple_of(step * columns, 128), columns)] = product

    @pl.when(step == pl.num_programs(0) - 1)
    def _():
        blocks, rows, _ = out_ref.shape
        copies = []
        for i in range(blocks):
            at = pl.ds(pl.multiple_of(table_ref[i] * rows, math.gcd(rows, 256)), rows)
            copies.append(pltpu.make_async_copy(total_s.at[at], out_ref.at[i, :, pl.ds(0, total_s.shape[1])], sem.at[i]))
        for c in copies:
            c.start()
        sums_ref[...] = sums_s[...]
        if slotted:
            slots_s[...] = jnp.zeros_like(slots_s)
            for n in range(blocks // 2):
                values = [sums_s[j, :1, n * rows : n * rows + rows] for j in range(3)]
                slots_s[place_ref[0] * (blocks // 2) + n, :3, :rows] = jnp.concatenate(values, axis=0).astype(BF16)
            slots = [
                pltpu.make_async_copy(slots_s.at[table_ref[i]], out_ref.at[i, :, pl.ds(total_s.shape[1], 128)], slot_sem.at[i])
                for i in range(blocks)
            ]
            for c in slots:
                c.start()
            copies = copies + slots
        for c in copies:
            c.wait()


def qkv_grad(place, table, own, other, grad_own, grad_other, slotted):
    count, rows = own.shape
    columns = grad_own.shape[1]
    half = columns // 3
    blocks = table.shape[0]
    whole = pl.BlockSpec((count, rows), lambda i, *_: (0, 0))
    tile = pl.BlockSpec((count, half), lambda i, *_: (0, i))
    return pl.pallas_call(
        partial(qkv_grad_kernel, slotted),
        out_shape=(
            jax.ShapeDtypeStruct((blocks, rows // blocks, columns + 128 * slotted), BF16),
            jax.ShapeDtypeStruct((3, 8, half), F32),
        ),
        grid_spec=pltpu.PrefetchScalarGridSpec(
            num_scalar_prefetch=2,
            grid=(3,),
            in_specs=[whole, whole, tile, tile],
            out_specs=[pl.BlockSpec(memory_space=pl.ANY), pl.BlockSpec((3, 8, half), lambda i, *_: (0, 0, 0))],
            scratch_shapes=[
                pltpu.VMEM((rows, columns), BF16), pltpu.VMEM((3, 8, half), F32),
                pltpu.VMEM((blocks, rows // blocks, 128) if slotted else (1, 16, 128), BF16),
                pltpu.SemaphoreType.DMA((blocks,)), pltpu.SemaphoreType.DMA((blocks,)),
            ],
        ),
        compiler_params=pltpu.CompilerParams(vmem_limit_bytes=28 * 2**20),
        cost_estimate=pl.CostEstimate(flops=10**11, bytes_accessed=1000, transcendentals=0),
        name="qkv_grad",
    )(place, table, own, other, grad_own, grad_other)


def pack_kernel(place_ref, *refs):
    *matrices, small_ref, out_ref = refs
    half = matrices[0].shape[1] // 2
    mine = pl.ds(pl.multiple_of(place_ref[0] * half, 128), half)
    for n, ref in enumerate(matrices):
        out_ref[0, :, n * half : n * half + half] = ref[:, mine]
    out_ref[0, :, len(matrices) * half :] = small_ref[...]


def pack(place, matrices, small):
    rows, width = matrices[0].shape
    whole = lambda a: pl.BlockSpec(a.shape, lambda i, *_: (0,) * len(a.shape))
    shape = jax.ShapeDtypeStruct((1, rows, len(matrices) * width // 2 + 128), BF16)
    return pl.pallas_call(
        pack_kernel,
        out_shape=shape,
        grid_spec=pltpu.PrefetchScalarGridSpec(
            num_scalar_prefetch=1,
            grid=(1,),
            in_specs=[whole(a) for a in (*matrices, small)],
            out_specs=whole(shape),
        ),
        name="pack",
    )(place, *matrices, small)


def finish_kernel(place_ref, own_ref, other_ref, *outs):
    half = outs[0].shape[1] // 2
    mine = pl.ds(pl.multiple_of(place_ref[0] * half, 128), half)
    theirs = pl.ds(pl.multiple_of((1 - place_ref[0]) * half, 128), half)
    for n, out in enumerate(outs[:3]):
        at = slice(n * half, n * half + half)
        out[:, mine] = own_ref[:, at].astype(F32)
        out[:, theirs] = other_ref[:, at].astype(F32)
    outs[3][...] = own_ref[:, 3 * half :].astype(F32) + other_ref[:, 3 * half :].astype(F32)


def finish(place, own, other):
    rows, columns = own.shape
    shape = jax.ShapeDtypeStruct((rows, (columns - 128) // 3 * 2), F32)
    whole = lambda s: pl.BlockSpec(s.shape, lambda i, *_: (0, 0))
    small = jax.ShapeDtypeStruct((rows, 128), F32)
    return pl.pallas_call(
        finish_kernel,
        out_shape=(shape, shape, shape, small),
        grid_spec=pltpu.PrefetchScalarGridSpec(
            num_scalar_prefetch=1,
            grid=(1,),
            in_specs=[whole(own), whole(other)],
            out_specs=[whole(shape)] * 3 + [whole(small)],
        ),
        name="finish",
    )(place, own, other)


def input_kernel(added, table_ref, grad_ref, *refs):
    added_refs, w_refs, (out_ref, w_s, sem) = refs[:added], refs[added:-3], refs[-3:]

    @pl.when(pl.program_id(0) == 0)
    def _():
        for c in load_rows(table_ref, w_refs, w_s, sem):
            c.wait()

    total = dot_right(grad_ref[...], w_s[...])
    for ref in added_refs:
        total = total + ref[...].astype(F32)
    out_ref[...] = total.astype(BF16)


def input_part(table, grad, weights, width, *added):
    count, columns = grad.shape
    blocks = table.shape[0]
    row = lambda n: pl.BlockSpec((BLOCK, n), lambda i, *_: (i, 0))
    return pl.pallas_call(
        partial(input_kernel, len(added)),
        out_shape=jax.ShapeDtypeStruct((count, width), BF16),
        grid_spec=pltpu.PrefetchScalarGridSpec(
            num_scalar_prefetch=1,
            grid=(count // BLOCK,),
            in_specs=[row(columns)] + [row(width)] * len(added) + [pl.BlockSpec(memory_space=pl.ANY)] * len(weights),
            out_specs=row(width),
            scratch_shapes=[pltpu.VMEM((width, columns), BF16), pltpu.SemaphoreType.DMA((blocks,))],
        ),
        compiler_params=pltpu.CompilerParams(vmem_limit_bytes=16 * 2**20),
        cost_estimate=pl.CostEstimate(flops=10**11, bytes_accessed=1000, transcendentals=0),
        name="input_part",
    )(table, grad, *added, *weights)


def copy_block(table_ref, source_ref, target_ref):
    target_ref[...] = source_ref[...]


def picked(blocks, table):
    block = (1, *blocks.shape[1:])
    return pl.pallas_call(
        copy_block,
        out_shape=jax.ShapeDtypeStruct(blocks.shape, blocks.dtype),
        grid_spec=pltpu.PrefetchScalarGridSpec(
            num_scalar_prefetch=1,
            grid=(blocks.shape[0],),
            in_specs=[pl.BlockSpec(block, lambda i, t: (t[i], 0, 0))],
            out_specs=pl.BlockSpec(block, lambda i, t: (i, 0, 0)),
        ),
        name="picked",
    )(table, blocks)


def sides(count):
    side = math.isqrt(count // 4)
    if count % 4 == 0 and 4 * side * side == count:
        return (4, side, side)
    return (count, 1, 1)


def hop(value, leg, step, shape):
    deep, tall, wide = shape
    count = deep * tall * wide
    pairs = []
    for core in range(2):
        for here in range(count):
            z, y, x = here // (tall * wide), here // wide % tall, here % wide
            if leg == 0:
                z = (z + step) % deep
            elif (leg == 1) == (core == 0):
                y = (y + step) % tall
            else:
                x = (x + step) % wide
            there = (z * tall + y) * wide + x
            pairs.append((core * count + there, core * count + here))
    return lax.ppermute(value, ("dp", "fsdp"), pairs)


def swapped(value):
    return lax.ppermute(value, "dp", [(0, 1), (1, 0)])


def received(blocks, leg, shape):
    return [hop(blocks, leg, s, shape) for s in range(1, shape[leg])]


def sent(total, leg, shape):
    pieces = total.reshape(shape[leg], -1, *total.shape[1:])
    return [pieces[0]] + [hop(pieces[s], leg, shape[leg] - s, shape) for s in range(1, shape[leg])]


def summed(values):
    return sum(v.astype(F32) for v in values).astype(BF16)


def staged(*values):
    return lax.optimization_barrier(values)


def join_kernel(*refs):
    *pieces, whole = refs
    first = 0
    for piece in pieces:
        whole[first : first + piece.shape[0]] = piece[...]
        first += piece.shape[0]


def join(pieces):
    spec = lambda s: pl.BlockSpec(s, lambda i: (0, 0, 0))
    shape = (sum(p.shape[0] for p in pieces), *pieces[0].shape[1:])
    return pl.pallas_call(
        join_kernel,
        out_shape=jax.ShapeDtypeStruct(shape, BF16),
        grid=(1,),
        in_specs=[spec(p.shape) for p in pieces],
        out_specs=spec(shape),
        compiler_params=pltpu.CompilerParams(vmem_limit_bytes=32 * 2**20),
        name="join",
    )(*pieces)


def order(core, shape, legs=(0, 1, 2)):
    deep, tall, wide = shape
    here = lax.axis_index("fsdp")
    z, y, x = here // (tall * wide), here // wide % tall, here % wide
    slot = jnp.arange(deep * tall * wide, dtype=jnp.int32)
    steps = {}
    for leg in legs:
        steps[leg] = slot % shape[leg]
        slot = slot // shape[leg]
    z = (z + steps[0]) % deep
    y = (y + jnp.where(core == 0, steps[1], steps[2])) % tall
    x = (x + jnp.where(core == 0, steps[2], steps[1])) % wide
    return (z * tall + y) * wide + x


def inverse(table):
    slots = jnp.arange(table.shape[0], dtype=jnp.int32)
    return jnp.sum(jnp.where(table[None, :] == slots[:, None], slots[None, :], 0), axis=1)


def half_of(array, side):
    width = array.shape[1] // 2
    return lax.dynamic_slice_in_dim(array, side * width, width, 1)


def joined(mine, theirs, core):
    first = jnp.where(core == 0, mine, theirs)
    second = jnp.where(core == 0, theirs, mine)
    return first, second


def reordered(small, table):
    slots = jnp.arange(table.shape[0], dtype=jnp.int32)
    chosen = (table[:, None] == slots[None, :]).astype(F32)
    flat = small.reshape(table.shape[0], -1)
    return jnp.dot(chosen, flat, precision=lax.Precision.HIGHEST).reshape(small.shape)


def shards(
    hidden_in,
    lengths,
    out_grad,
    query_matrix,
    query_offset,
    key_matrix,
    key_offset,
    value_matrix,
    value_offset,
    output_matrix,
    output_offset,
    first_gain,
    first_offset,
    up_matrix,
    up_offset,
    down_matrix,
    down_offset,
    second_gain,
    second_offset,
):
    count, width = hidden_in.shape
    half = width // 2
    rows = query_matrix.shape[0]
    parts = up_offset.shape[0] // rows
    core = lax.axis_index("dp")
    shape = sides(lax.axis_size("fsdp"))
    positions = math.prod(shape)
    table, other_table = order(core, shape), order(1 - core, shape)
    down_legs = (1, 0, 2)
    down_table, other_down_table = order(core, shape, down_legs), order(1 - core, shape, down_legs)
    direct = rows % 16 == 0
    place = jnp.reshape(core, (1,)).astype(jnp.int32)
    zero = jnp.zeros((1,), jnp.int32)
    own_order, their_order = (table, other_table) if direct else (zero, zero)
    own_down_order, their_down_order = (down_table, other_down_table) if direct else (zero, zero)
    down_rows = down_matrix.shape[0]

    def usable(pieces, places, cuts):
        if direct:
            return pieces
        blocks, parts, first = jnp.concatenate(pieces, axis=0), [], 0
        for cut in cuts:
            parts.append(picked(blocks[:, first : first + cut], inverse(places)).reshape(1, -1, blocks.shape[2]))
            first += cut
        return [jnp.concatenate(parts, axis=1)]

    def in_blocks(array, places):
        return array if direct else picked(array.reshape(positions, -1, array.shape[2]), places)

    vectors = (
        query_offset, key_offset, value_offset, output_offset, first_gain, first_offset,
        down_offset, second_gain, second_offset,
    )
    left = jnp.pad(jnp.stack(vectors), ((0, rows - len(vectors)), (0, 64 - rows)))
    right = jnp.pad(up_offset.reshape(parts, rows), ((0, rows - parts), (0, 64 - rows)))
    unit = pack(place, (query_matrix, key_matrix, value_matrix), jnp.concatenate([left, right], axis=1))
    attn_far = received(unit, 0, shape)
    other_lengths = swapped(lengths)
    down_unit = jnp.concatenate([half_of(down_matrix, core), half_of(output_matrix, core)], axis=0)[None]
    down_far = received(down_unit, 1, shape)
    other_in = swapped(hidden_in)
    tables, plan, _ = described(lengths[0], count)

    attn_far, up_matrix, other_lengths, down_far, other_in = staged(attn_far, up_matrix, other_lengths, down_far, other_in)
    attn_four = join([unit] + attn_far)
    attn_far = received(attn_four, 1, shape)
    down_two = join([down_unit] + down_far)
    down_far = received(down_two, 0, shape)
    other_tables, other_plan, _ = described(other_lengths[0], count)

    attn_far, attn_four, up_matrix = staged(attn_far, attn_four, up_matrix)
    attn_eight = join([attn_four] + attn_far)
    attn_far = received(attn_eight, 2, shape)
    up_unit = half_of(up_matrix, core)[None]

    attn_far, up_unit = staged(attn_far, up_unit)
    attn = [attn_eight] + attn_far
    small = jnp.concatenate([a[:, :, 3 * half :] for a in attn], axis=0).astype(F32)
    small = reordered(small, inverse(table))
    whole = small[:, : len(vectors), :rows].swapaxes(0, 1).reshape(len(vectors), width)
    up_bias = small[:, :parts, 64 : 64 + rows].reshape(1, -1)
    bias = lax.dynamic_slice_in_dim(whole[:3], core * half, half, 1).reshape(1, -1)
    vector_rows = jnp.pad(whole[3:], ((0, 2), (0, 0)))
    attn = usable(attn, table, (rows,))
    up_far = received(up_unit, 0, shape)
    other_q, other_k, other_v, other_norms = project(other_in, attn, own_order, bias, other_tables)

    down_far, up_far, other_q, hidden_in = staged(down_far, up_far, other_q, hidden_in)
    up_four = join([up_unit] + up_far)
    up_far = received(up_four, 1, shape)
    down_eight = join([down_two] + down_far)
    down_far = received(down_eight, 2, shape)
    other_mixed, other_lse = attend(other_plan, other_q, other_k, other_v, other_norms, other_tables[2])

    up_far, up_four, other_mixed, hidden_in = staged(up_far, up_four, other_mixed, hidden_in)
    up_eight = join([up_four] + up_far)
    up_far = received(up_eight, 2, shape)
    mixed_theirs = swapped(other_mixed)
    down_swapped = swapped(down_eight)
    q, k, v, norms = project(hidden_in, attn, own_order, bias, tables)

    down_far, down_swapped, mixed_theirs, q = staged(down_far, down_swapped, mixed_theirs, q)
    up_swapped = swapped(up_eight)
    down_swapped = [down_swapped] + [swapped(far) for far in down_far]
    mixed, lse = attend(plan, q, k, v, norms, tables[2])

    up_far, up_swapped, down_swapped, mixed, vector_rows, up_bias = staged(
        up_far, up_swapped, down_swapped, mixed, vector_rows, up_bias
    )
    up_swapped = [up_swapped] + [swapped(far) for far in up_far]
    up_weights = [usable([up_eight] + up_far, table, (rows,)), usable(up_swapped, other_table, (rows,))]
    down_weights = [
        usable([down_eight] + down_far, down_table, (down_rows, rows)),
        usable(down_swapped, other_down_table, (down_rows, rows)),
    ]
    (
        hidden_out, normed_low, activated, grad_two, grad_up, grad_one, grad_mine, grad_theirs, both_mixed, sums, up_sum,
    ) = middle(
        place, own_order, their_order, own_down_order, their_down_order, hidden_in, mixed, mixed_theirs, out_grad, tables[2],
        up_weights + down_weights, vector_rows, up_bias,
    )
    other_grad = swapped(grad_theirs)
    places = (place, own_order, their_order)
    slots_of = lambda vectors: vectors.reshape(-1, positions, rows).swapaxes(0, 1)
    left = jnp.pad(slots_of(sums[:6]), ((0, 0), (0, rows - 6), (0, 64 - rows)))
    right = jnp.pad(up_sum.reshape(positions, parts, rows), ((0, 0), (0, rows - parts), (0, 64 - rows)))
    slot_sums = jnp.concatenate([left, right], axis=2)

    def with_slots(pair, slots):
        if direct:
            return pair
        return [
            jnp.concatenate([in_blocks(p, t), reordered(slots, t).astype(BF16)], axis=2)
            for p, t in zip(pair, (table, other_table))
        ]

    output_pair = outer(*places, both_mixed, grad_one, 1, (slot_sums.astype(BF16),) if direct else ())
    output_pair = with_slots(output_pair, slot_sums)

    output_pair, grad_up = staged(output_pair, grad_up)
    output_arrived = swapped(output_pair[1])
    up_pair = outer(*places, normed_low, grad_up, 1)

    up_pair, output_arrived, activated = staged(up_pair, output_arrived, activated)
    up_arrived = swapped(in_blocks(up_pair[1], other_table))
    down_pair = outer(*places, activated, grad_two, 0)

    down_pair, up_arrived, other_grad = staged(down_pair, up_arrived, other_grad)
    up_total = [summed([in_blocks(up_pair[0], table), up_arrived]), summed([output_pair[0], output_arrived])]
    up_sent = sent(jnp.concatenate(up_total, axis=2), 2, shape)
    down_arrived = swapped(in_blocks(down_pair[1], other_table))
    other_d = attend_back(other_plan, other_q, other_k, other_v, other_lse, other_mixed, other_grad, other_tables)

    up_sent, down_arrived, other_d, grad_mine = staged(up_sent, down_arrived, other_d, grad_mine)
    down_sent = sent(summed([in_blocks(down_pair[0], table), down_arrived]), 2, shape)
    up_sent = sent(summed(up_sent), 1, shape)
    own_d = attend_back(plan, q, k, v, lse, mixed, grad_mine, tables)

    up_sent, down_sent, own_d = staged(up_sent, down_sent, own_d)
    up_sent = sent(summed(up_sent), 0, shape)
    down_sent = sent(summed(down_sent), 1, shape)
    matrices, qkv_sums = qkv_grad(place, own_order, hidden_in, other_in, own_d, other_d, direct)

    down_sent, matrices, other_d = staged(down_sent, matrices, other_d)
    if not direct:
        own_sums = jnp.zeros((3, width), F32)
        own_sums = lax.dynamic_update_slice_in_dim(own_sums, qkv_sums[:, 0], core * half, 1)
        own_sums = jnp.pad(slots_of(own_sums), ((0, 0), (0, rows - 3), (0, 128 - rows)))
        matrices = jnp.concatenate([in_blocks(matrices, table), reordered(own_sums, table).astype(BF16)], axis=2)
    matrices_sent = sent(matrices, 2, shape)
    down_sent = sent(summed(down_sent), 0, shape)
    sent_grad = input_part(own_order, other_d, attn, width)

    matrices_sent, up_sent, sent_grad = staged(matrices_sent, up_sent, sent_grad)
    matrices_sent = sent(summed(matrices_sent), 1, shape)
    up_done = summed(up_sent)[0]
    up_other = swapped(up_done)
    other_part = swapped(sent_grad)

    matrices_sent, down_sent, up_other, other_part, own_d = staged(matrices_sent, down_sent, up_other, other_part, own_d)
    matrices_sent = sent(summed(matrices_sent), 0, shape)
    down_done = summed(down_sent)[0]
    down_other = swapped(down_done)
    input_grad = input_part(own_order, own_d, attn, width, other_part, grad_one)

    matrices_sent, down_other, input_grad = staged(matrices_sent, down_other, input_grad)
    matrices_done = summed(matrices_sent)[0]

    up_first, up_second = joined(up_done, up_other, core)
    down_first, down_second = joined(down_done, down_other, core)
    query_grad, key_grad, value_grad, offsets = finish(place, matrices_done, swapped(matrices_done))
    wide = lambda a, b: jnp.concatenate([a, b], axis=1).astype(F32)
    hidden = up_matrix.shape[1] // 2
    others = up_first[:, hidden + half :].astype(F32)
    columns = slice(hidden, hidden + half)
    return (
        hidden_out,
        input_grad,
        query_grad,
        offsets[0, :rows],
        key_grad,
        offsets[1, :rows],
        value_grad,
        offsets[2, :rows],
        wide(up_first[:, columns], up_second[:, columns]),
        others[0, :rows],
        others[1, :rows],
        others[2, :rows],
        wide(up_first[:, :hidden], up_second[:, :hidden]),
        others[:parts, 64 : 64 + rows].reshape(-1),
        wide(down_first, down_second),
        others[3, :rows],
        others[4, :rows],
        others[5, :rows],
    )


def solution(mesh):
    placed = (
        P(("dp", "fsdp"), None),
        P(("dp", "fsdp"), None),
        P(("dp", "fsdp"), None),
        P("fsdp", None),
        P("fsdp"),
        P("fsdp", None),
        P("fsdp"),
        P("fsdp", None),
        P("fsdp"),
        P("fsdp", None),
        P("fsdp"),
        P("fsdp"),
        P("fsdp"),
        P("fsdp", None),
        P("fsdp"),
        P("fsdp", None),
        P("fsdp"),
        P("fsdp"),
        P("fsdp"),
    )
    return jax.shard_map(
        shards,
        mesh=mesh,
        in_specs=placed,
        out_specs=(
            P(("dp", "fsdp"), None),
            P(("dp", "fsdp"), None),
            P("fsdp", None),
            P("fsdp"),
            P("fsdp", None),
            P("fsdp"),
            P("fsdp", None),
            P("fsdp"),
            P("fsdp", None),
            P("fsdp"),
            P("fsdp"),
            P("fsdp"),
            P("fsdp", None),
            P("fsdp"),
            P("fsdp", None),
            P("fsdp"),
            P("fsdp"),
            P("fsdp"),
        ),
        check_vma=False,
    )
```
